32 devices in a mesh: gx: 16 (over z, y, x), gy: 2 (over core).
Axes of the slice: x: 2, y: 2, z: 4, core: 2. Of those that a mesh axis runs over, the one named last changes fastest.
Arguments:
- forcing: float32 [128, 64, 256], P('gx', 'gy'), may hold values from -20 to 20
- reaction: float32 [128, 64, 256], P('gx', 'gy'), may hold values from 0.1 to 1.9
- velocity: float32 [3, 128, 64, 256], P(None, 'gx', 'gy'), may hold values from -0.08 to 0.08
Outputs:
- basis_q: float32 [9, 128, 64, 256], P(None, 'gx', 'gy')
- factor_r: float32 [9, 9], replicated
The draws below stay inside these ranges and needn't reach their ends.
All inputs are finite; a program needn't handle non-finite values.
Results may differ from the reference program's by a relative error of at most 0.0018.
Values sent between devices are 32-bit elements; how exact they have to be, the bound alone decides.
No kernel may reach another device: no remote copies, remote signals or barrier semaphores. Data moves between devices by JAX's collectives and lax.ppermute only.
A program may use at most 128 MiB of HBM per device.

```python
import math
import jax
import jax.numpy as jnp
from jax import lax

STEPS = 8
BASIS = 9
NX = 128
NY = 64
NZ = 256


def draw_forcing(key, part):
    first_key, second_key = jax.random.split(jax.random.fold_in(key, 11))
    rough = jnp.clip(jax.random.normal(first_key, (NX, NY, NZ), jnp.float32), -2.5, 2.5)
    spread = jnp.exp(jax.random.uniform(second_key, (NX, NY, NZ), jnp.float32, 0.0, math.log(10.0)))
    return 0.8 * rough * spread


def shard_levels(own_key, extent, cuts, low, high):
    def one(position, shards_of):
        heights = jax.random.uniform(jax.random.fold_in(jax.random.fold_in(own_key, 6), position), (shards_of,), jnp.float32, low / len(cuts), high / len(cuts))
        return jnp.repeat(jnp.exp(heights), extent[position] // shards_of).reshape((-1,) + (1,) * (len(extent) - position - 1))

    factor_of = one(*cuts[0])
    for cut in cuts[1:]:
        factor_of = factor_of * one(*cut)
    return factor_of


def setup_inputs(seed: int = 0) -> dict:
    streams_of = jax.random.split(jax.random.key(seed), 4)
    return {
        "forcing": draw_forcing(jax.random.fold_in(streams_of[3], 71), 0),
        "reaction": jnp.clip(0.1 + 1.8 * jax.random.uniform(streams_of[1], (NX, NY, NZ), jnp.float32) ** shard_levels(streams_of[1], (NX, NY, NZ), ((0, 16), (1, 2)), -0.2, 0.2), 0.1, 1.9),
        "velocity": jnp.clip(jax.random.uniform(streams_of[2], (3, NX, NY, NZ), jnp.float32, -0.08, 0.08) * shard_levels(streams_of[2], (3, NX, NY, NZ), ((1, 16), (2, 2)), -0.4, 0.0), -0.08, 0.08),
    }


DIFFUSION = 0.03
CENTRE_SHIFT = 1.18
HALF_WIDTH = 0.95
EPSILON = 1e-06

def apply_scaled(field, reaction, velocity):
    east_cell = jnp.roll(field, -1, axis=0)
    west_cell = jnp.roll(field, 1, axis=0)
    north_cell = jnp.roll(field, -1, axis=1)
    south_cell = jnp.roll(field, 1, axis=1)
    upper_cell = jnp.roll(field, -1, axis=2)
    lower_cell = jnp.roll(field, 1, axis=2)
    neighbours = east_cell + west_cell + north_cell + south_cell + upper_cell + lower_cell
    advection = velocity[0] * (east_cell - west_cell) + velocity[1] * (north_cell - south_cell) + velocity[2] * (upper_cell - lower_cell)
    operated = reaction * field + DIFFUSION * (6.0 * field - neighbours) + 0.5 * advection
    return (operated - CENTRE_SHIFT * field) / HALF_WIDTH

def upper_inverse(factor):
    count = factor.shape[0]
    identity = jnp.eye(count, dtype=jnp.float32)
    inverse_rows = [None] * count
    for row_index in reversed(range(count)):
        accumulated = identity[row_index]
        for later_index in range(row_index + 1, count):
            accumulated = accumulated - factor[row_index, later_index] * inverse_rows[later_index]
        inverse_rows[row_index] = accumulated / factor[row_index, row_index]
    return jnp.stack(inverse_rows)

def reference(forcing, reaction, velocity):
    cell_count = float(NX * NY * NZ)
    mean_square = jnp.sum(forcing * forcing) / cell_count
    start = forcing / jnp.sqrt(mean_square + EPSILON)
    previous = start
    current = apply_scaled(start, reaction, velocity)
    vectors = [previous, current]
    for step_index in range(STEPS - 1):
        following = 2.0 * apply_scaled(current, reaction, velocity) - previous
        previous, current = (current, following)
        vectors.append(current)
    basis = jnp.stack(vectors)
    flattened = basis.reshape(BASIS, -1)
    gram_matrix = jnp.dot(flattened.astype(jnp.float32), flattened.T.astype(jnp.float32), precision=lax.Precision.HIGHEST, preferred_element_type=jnp.float32) / cell_count
    factor = jnp.linalg.cholesky(gram_matrix).T
    inverse = upper_inverse(factor)
    orthonormal = jnp.tensordot(inverse, basis, axes=((0,), (0,)), precision=lax.Precision.HIGHEST)
    return (orthonormal, factor)
```

```python
import jax
import jax.numpy as jnp
from jax import lax
from jax.experimental import pallas as pl
from jax.experimental.pallas import tpu as pltpu
from jax.sharding import PartitionSpec as P

BASIS = 9
HALO = 4

DIFFUSION = 0.03
CENTRE_SHIFT = 1.18
HALF_WIDTH = 0.95
EPSILON = 1e-06
LIFT = 1024.0
AXES = ("gx", "gy")
PAIRS = [(i, j) for i in range(BASIS) for j in range(i, BASIS)]
VMEM = pl.BlockSpec(memory_space=pltpu.VMEM)


def ring(axis, step):
    count = lax.axis_size(axis)
    return [(i, (i + step) % count) for i in range(count)]


def swap_x(to_low, to_high):
    return lax.ppermute(to_high, "gx", ring("gx", 1)), lax.ppermute(to_low, "gx", ring("gx", -1))


def swap_y(tile):
    if lax.axis_size("gy") == 2:
        return lax.ppermute(tile, "gy", ring("gy", 1))
    above = lax.ppermute(tile[:, :HALO], "gy", ring("gy", -1))
    below = lax.ppermute(tile[:, HALO:], "gy", ring("gy", 1))
    return jnp.concatenate([above, below], axis=1)


def edge_rows(block):
    rows = block.shape[-2]
    low, high = block[..., : 2 * HALO, :], block[..., rows - 2 * HALO :, :]
    lane = lax.broadcasted_iota(jnp.int32, low.shape, low.ndim - 2)
    return jnp.where(lane < HALO, low, high)


def doubled(centre, east, west, coef):
    rows, lanes = centre.shape
    north = pltpu.roll(centre, rows - 1, 0)
    south = pltpu.roll(centre, 1, 0)
    upper = pltpu.roll(centre, lanes - 1, 1)
    lower = pltpu.roll(centre, 1, 1)
    around = (east + west) + (north + south) + (upper + lower)
    slopes = coef[1] * (east - west) + coef[2] * (north - south) + coef[3] * (upper - lower)
    return coef[0] * centre + slopes - (2.0 * DIFFUSION / HALF_WIDTH) * around


def first_kernel(f, r, vel, low, high, own_rows, corner_rows, vectors, to_low, to_high, rows_out, coef, grid):
    bx, by, _ = f.shape
    h = HALO
    ext = bx + 2 * h
    grid[0, 0:h, 0:by] = low[0:h] * LIFT
    grid[0, h : h + bx, 0:by] = f[...] * LIFT
    grid[0, h + bx : ext, 0:by] = high[0:h] * LIFT
    grid[0, 0:h, by:] = corner_rows[0:h] * LIFT
    grid[0, h : h + bx, by:] = own_rows[0:bx] * LIFT
    half = low.shape[0]
    grid[0, h + bx : ext, by:] = corner_rows[half : half + h] * LIFT
    c = h - 1
    for k in range(4):
        scale = 2.0 / HALF_WIDTH if k == 0 else 1.0 / HALF_WIDTH
        shift = (6.0 * DIFFUSION - CENTRE_SHIFT) * scale if k == 0 else 0.0
        at = h + c * k
        coef[k, 0:c, 0:by] = low[at : at + c] * scale + shift
        coef[k, c : c + bx, 0:by] = (r[...] if k == 0 else vel[k - 1]) * scale + shift
        coef[k, c + bx :, 0:by] = high[at : at + c] * scale + shift
        coef[k, 0:c, by:] = corner_rows[at : at + c] * scale + shift
        coef[k, c : c + bx, by:] = own_rows[bx * (k + 1) : bx * (k + 2)] * scale + shift
        coef[k, c + bx :, by:] = corner_rows[half + at : half + at + c] * scale + shift
    for step in range(1, h + 1):

        def layer(x, carry, step=step):
            new = doubled(
                grid[step - 1, x], grid[step - 1, x + 1], grid[step - 1, x - 1], [coef[k, x - 1] for k in range(4)]
            )
            new = new * 0.5 if step == 1 else new - grid[step - 2, x]
            grid[step, x] = new
            return carry

        lax.fori_loop(step, ext - step, layer, 0)
    for step in range(h + 1):
        vectors[step] = grid[step, h : h + bx, 0:by]
    to_low[0:h] = grid[h, h : 2 * h, 0:by]
    to_low[h:] = grid[h - 1, h : 2 * h - 1, 0:by]
    to_high[0:h] = grid[h, bx : bx + h, 0:by]
    to_high[h:] = grid[h - 1, bx + 1 : bx + h, 0:by]
    rows_out[0:bx] = edge_rows(grid[h, h : h + bx, 0:by])
    rows_out[bx:] = edge_rows(grid[h - 1, h : h + bx, 0:by])


def second_kernel(vectors, coef, low, high, own_rows, corner_rows, later, gram, grid, sums):
    _, bx, by, nz = vectors.shape
    h = HALO
    ext = bx + 2 * h
    half = low.shape[0]
    last = h
    grid[1, 0:h, 0:by] = low[0:h]
    grid[1, h : h + bx, 0:by] = vectors[last]
    grid[1, h + bx : ext, 0:by] = high[0:h]
    grid[1, 0:h, by:] = corner_rows[0:h]
    grid[1, h : h + bx, by:] = own_rows[0:bx]
    grid[1, h + bx : ext, by:] = corner_rows[half : half + h]
    grid[0, 1:h, 0:by] = low[h:]
    grid[0, h : h + bx, 0:by] = vectors[last - 1]
    grid[0, h + bx : ext - 1, 0:by] = high[h:]
    grid[0, 1:h, by:] = corner_rows[h:half]
    grid[0, h : h + bx, by:] = own_rows[bx:]
    grid[0, h + bx : ext - 1, by:] = corner_rows[half + h :]
    for step in range(1, h + 1):

        def layer(x, carry, step=step):
            new = doubled(grid[step, x], grid[step, x + 1], grid[step, x - 1], [coef[k, x - 1] for k in range(4)])
            grid[step + 1, x] = new - grid[step - 1, x]
            return carry

        lax.fori_loop(step, ext - step, layer, 0)
    for step in range(h):
        later[step] = grid[step + 2, h : h + bx, 0:by]

    tiles = by // 8

    def products(at, totals):
        x, y = at // tiles, pl.multiple_of(at % tiles * 8, 8)
        for z in range(0, nz, 128):
            window = (pl.ds(y, 8), pl.ds(z, 128))
            cells = [vectors[(k, x) + window] for k in range(h + 1)]
            cells += [later[(k, x) + window] for k in range(h)]
            totals = tuple(t + cells[i] * cells[j] for t, (i, j) in zip(totals, PAIRS))
        return totals

    totals = lax.fori_loop(0, bx * tiles, products, tuple(jnp.zeros((8, 128), jnp.float32) for _ in PAIRS))
    sublane = lax.broadcasted_iota(jnp.int32, (8, 128), 0)
    sums[...] = jnp.zeros_like(sums)
    for base in range(0, len(PAIRS), 8):
        packed = jnp.zeros((8, 128), jnp.float32)
        for k, total in enumerate(totals[base : base + 8]):
            for distance in (4, 2, 1):
                total = total + pltpu.roll(total, distance, 0)
            packed = jnp.where(sublane == k, total, packed)
        sums[base : base + 8] = packed
    ones = jnp.ones(gram.shape, jnp.float32)
    gram[...] = lax.dot_general(
        ones, sums[...], (((1,), (1,)), ((), ())), precision=lax.Precision.HIGHEST, preferred_element_type=jnp.float32
    )


def last_kernel(cell_count, gram, vectors, later, out, factor, coef, result, sem):
    _, bx, by, nz = vectors.shape
    total = gram[0:8]
    for row in range(8, gram.shape[0], 8):
        total = total + gram[row : row + 8]
    for distance in (4, 2, 1):
        total = total + pltpu.roll(total, distance, 0)
    total = total * (1.0 / cell_count)
    entry = {}
    for k, (i, j) in enumerate(PAIRS):
        entry[i, j] = jnp.broadcast_to(total[:, k : k + 1], (8, 128))
    divisor = jnp.sqrt(entry[0, 0] * (1.0 / (LIFT * LIFT)) + EPSILON)
    scale = 1.0 / (divisor * LIFT)
    place = {pair: k for k, pair in enumerate(PAIRS)}
    for j in range(BASIS):
        length = jnp.sqrt(entry[j, j])
        inverse = 1.0 / length
        row = {k: entry[j, k] * inverse for k in range(j + 1, BASIS)}
        for i in range(j + 1, BASIS):
            for k in range(i, BASIS):
                entry[i, k] = entry[i, k] - row[i] * row[k]
        entry[j, j] = length
        coef[place[j, j]] = inverse
        for k in range(j + 1, BASIS):
            entry[j, k] = row[k]
            coef[place[j, k]] = row[k]
    sublane = lax.broadcasted_iota(jnp.int32, (8, 128), 0)
    lane = lax.broadcasted_iota(jnp.int32, (8, 128), 1)
    tops = []
    for base in range(0, BASIS, 8):
        packed = jnp.zeros((8, 128), jnp.float32)
        for (i, j), value in entry.items():
            if base <= i < base + 8:
                packed = jnp.where((sublane == i - base) & (lane == j), value, packed)
        tops.append(packed * scale)
    factor[...] = jnp.concatenate(tops, axis=0)[:BASIS, :BASIS]

    tiles = by // 8

    def solve(x, carry):
        for y in range(tiles):
            for z in range(0, nz, 128):
                window = (x, slice(8 * y, 8 * y + 8), slice(z, z + 128))
                columns = []
                for j in range(BASIS):
                    value = vectors[(j,) + window] if j <= HALO else later[(j - HALO - 1,) + window]
                    for i in range(j):
                        value = value - coef[place[i, j]] * columns[i]
                    value = value * coef[place[j, j]]
                    result[(j,) + window] = value
                    columns.append(value)
        pltpu.make_async_copy(result.at[:, x], out.at[:, x], sem.at[x]).start()
        return carry

    lax.fori_loop(0, bx, solve, 0)
    for x in range(bx):
        pltpu.make_async_copy(result.at[:, x], out.at[:, x], sem.at[x]).wait()


def shape(*dims):
    return jax.ShapeDtypeStruct(dims, jnp.float32)


def per_device(forcing, reaction, velocity):
    bx, by, nz = forcing.shape
    devices = lax.axis_size("gx") * lax.axis_size("gy")
    cell_count = float(bx * by * nz * devices)
    h, c, ext = HALO, HALO - 1, bx + 2 * HALO
    fields = [reaction, velocity[0], velocity[1], velocity[2]]
    params = pltpu.CompilerParams(vmem_limit_bytes=24 << 20)

    to_low = jnp.concatenate([forcing[:h]] + [v[:c] for v in fields])
    to_high = jnp.concatenate([forcing[bx - h :]] + [v[bx - c :] for v in fields])
    low, high = swap_x(to_low, to_high)
    own_rows = swap_y(edge_rows(jnp.concatenate([forcing] + fields)))
    corner_rows = swap_y(edge_rows(jnp.concatenate([low, high])))
    vectors, to_low, to_high, rows, coef = pl.pallas_call(
        first_kernel,
        out_shape=[
            shape(h + 1, bx, by, nz),
            shape(h + c, by, nz),
            shape(h + c, by, nz),
            shape(2 * bx, 2 * h, nz),
            shape(4, bx + 2 * c, by + 2 * h, nz),
        ],
        in_specs=[VMEM] * 7,
        out_specs=[VMEM] * 5,
        scratch_shapes=[pltpu.VMEM((h + 1, ext, by + 2 * h, nz), jnp.float32)],
        compiler_params=params,
        name="first",
    )(forcing, reaction, velocity, low, high, own_rows, corner_rows)

    low, high = swap_x(to_low, to_high)
    own_rows = swap_y(rows)
    corner_rows = swap_y(edge_rows(jnp.concatenate([low, high])))
    later, gram = pl.pallas_call(
        second_kernel,
        out_shape=[shape(h, bx, by, nz), shape(devices, 128)],
        in_specs=[VMEM] * 6,
        out_specs=[VMEM] * 2,
        scratch_shapes=[
            pltpu.VMEM((h + 2, ext, by + 2 * h, nz), jnp.float32),
            pltpu.VMEM((128, 128), jnp.float32),
        ],
        compiler_params=params,
        name="second",
    )(vectors, coef, low, high, own_rows, corner_rows)
    gram = lax.all_to_all(gram, AXES, 0, 0, tiled=True)

    def last(*refs):
        last_kernel(cell_count, *refs)

    return pl.pallas_call(
        last,
        out_shape=[shape(BASIS, bx, by, nz), shape(BASIS, BASIS)],
        in_specs=[VMEM] * 3,
        out_specs=[pl.BlockSpec(memory_space=pl.ANY), VMEM],
        scratch_shapes=[
            pltpu.VMEM((len(PAIRS), 8, 128), jnp.float32),
            pltpu.VMEM((BASIS, bx, by, nz), jnp.float32),
            pltpu.SemaphoreType.DMA((bx,)),
        ],
        compiler_params=params,
        name="last",
    )(gram, vectors, later)


def solution(mesh):
    in_specs = (P("gx", "gy", None), P("gx", "gy", None), P(None, "gx", "gy", None))
    out_specs = (P(None, "gx", "gy", None), P())
    return jax.shard_map(per_device, mesh=mesh, in_specs=in_specs, out_specs=out_specs, check_vma=False)
```

```python
import jax
import jax.numpy as jnp
from jax import lax
from jax.experimental import pallas as pl
from jax.experimental.pallas import tpu as pltpu
from jax.sharding import PartitionSpec as P

BASIS = 9
HALO = 4

DIFFUSION = 0.03
CENTRE_SHIFT = 1.18
HALF_WIDTH = 0.95
EPSILON = 1e-06
LIFT = 1024.0
AXES = ("gx", "gy")
PAIRS = [(i, j) for i in range(BASIS) for j in range(i, BASIS)]
VMEM = pl.BlockSpec(memory_space=pltpu.VMEM)


def ring(axis, step):
    count = lax.axis_size(axis)
    return [(i, (i + step) % count) for i in range(count)]


def swap_x(to_low, to_high):
    return lax.ppermute(to_high, "gx", ring("gx", 1)), lax.ppermute(to_low, "gx", ring("gx", -1))


def swap_y(tile):
    if lax.axis_size("gy") == 2:
        return lax.ppermute(tile, "gy", ring("gy", 1))
    above = lax.ppermute(tile[:, :HALO], "gy", ring("gy", -1))
    below = lax.ppermute(tile[:, HALO:], "gy", ring("gy", 1))
    return jnp.concatenate([above, below], axis=1)


def edge_rows(block):
    rows = block.shape[-2]
    low, high = block[..., : 2 * HALO, :], block[..., rows - 2 * HALO :, :]
    lane = lax.broadcasted_iota(jnp.int32, low.shape, low.ndim - 2)
    return jnp.where(lane < HALO, low, high)


def doubled(centre, east, west, coef):
    rows, lanes = centre.shape
    north = pltpu.roll(centre, rows - 1, 0)
    south = pltpu.roll(centre, 1, 0)
    upper = pltpu.roll(centre, lanes - 1, 1)
    lower = pltpu.roll(centre, 1, 1)
    around = (east + west) + (north + south) + (upper + lower)
    slopes = coef[1] * (east - west) + coef[2] * (north - south) + coef[3] * (upper - lower)
    return coef[0] * centre + slopes - (2.0 * DIFFUSION / HALF_WIDTH) * around


def first_kernel(f, r, vel, low, high, own_rows, corner_rows, vectors, to_low, to_high, rows_out, coef, grid):
    bx, by, _ = f.shape
    h = HALO
    ext = bx + 2 * h
    grid[0, 0:h, 0:by] = low[0:h] * LIFT
    grid[0, h : h + bx, 0:by] = f[...] * LIFT
    grid[0, h + bx : ext, 0:by] = high[0:h] * LIFT
    grid[0, 0:h, by:] = corner_rows[0:h] * LIFT
    grid[0, h : h + bx, by:] = own_rows[0:bx] * LIFT
    half = low.shape[0]
    grid[0, h + bx : ext, by:] = corner_rows[half : half + h] * LIFT
    c = h - 1
    for k in range(4):
        scale = 2.0 / HALF_WIDTH if k == 0 else 1.0 / HALF_WIDTH
        shift = (6.0 * DIFFUSION - CENTRE_SHIFT) * scale if k == 0 else 0.0
        at = h + c * k
        coef[k, 0:c, 0:by] = low[at : at + c] * scale + shift
        coef[k, c : c + bx, 0:by] = (r[...] if k == 0 else vel[k - 1]) * scale + shift
        coef[k, c + bx :, 0:by] = high[at : at + c] * scale + shift
        coef[k, 0:c, by:] = corner_rows[at : at + c] * scale + shift
        coef[k, c : c + bx, by:] = own_rows[bx * (k + 1) : bx * (k + 2)] * scale + shift
        coef[k, c + bx :, by:] = corner_rows[half + at : half + at + c] * scale + shift
    for step in range(1, h + 1):

        def layer(x, carry, step=step):
            new = doubled(
                grid[step - 1, x], grid[step - 1, x + 1], grid[step - 1, x - 1], [coef[k, x - 1] for k in range(4)]
            )
            new = new * 0.5 if step == 1 else new - grid[step - 2, x]
            grid[step, x] = new
            return carry

        lax.fori_loop(step, ext - step, layer, 0, unroll=True)
    for step in range(h + 1):
        vectors[step] = grid[step, h : h + bx, 0:by]
    to_low[0:h] = grid[h, h : 2 * h, 0:by]
    to_low[h:] = grid[h - 1, h : 2 * h - 1, 0:by]
    to_high[0:h] = grid[h, bx : bx + h, 0:by]
    to_high[h:] = grid[h - 1, bx + 1 : bx + h, 0:by]
    rows_out[0:bx] = edge_rows(grid[h, h : h + bx, 0:by])
    rows_out[bx:] = edge_rows(grid[h - 1, h : h + bx, 0:by])


def second_kernel(vectors, coef, low, high, own_rows, corner_rows, later, gram, grid, sums):
    _, bx, by, nz = vectors.shape
    h = HALO
    ext = bx + 2 * h
    half = low.shape[0]
    last = h
    grid[1, 0:h, 0:by] = low[0:h]
    grid[1, h : h + bx, 0:by] = vectors[last]
    grid[1, h + bx : ext, 0:by] = high[0:h]
    grid[1, 0:h, by:] = corner_rows[0:h]
    grid[1, h : h + bx, by:] = own_rows[0:bx]
    grid[1, h + bx : ext, by:] = corner_rows[half : half + h]
    grid[0, 1:h, 0:by] = low[h:]
    grid[0, h : h + bx, 0:by] = vectors[last - 1]
    grid[0, h + bx : ext - 1, 0:by] = high[h:]
    grid[0, 1:h, by:] = corner_rows[h:half]
    grid[0, h : h + bx, by:] = own_rows[bx:]
    grid[0, h + bx : ext - 1, by:] = corner_rows[half + h :]
    for step in range(1, h + 1):

        def layer(x, carry, step=step):
            new = doubled(grid[step, x], grid[step, x + 1], grid[step, x - 1], [coef[k, x - 1] for k in range(4)])
            grid[step + 1, x] = new - grid[step - 1, x]
            return carry

        lax.fori_loop(step, ext - step, layer, 0, unroll=True)
    for step in range(h):
        later[step] = grid[step + 2, h : h + bx, 0:by]

    tiles = by // 8

    def products(at, totals):
        x, y = at // tiles, pl.multiple_of(at % tiles * 8, 8)
        for z in range(0, nz, 128):
            window = (pl.ds(y, 8), pl.ds(z, 128))
            cells = [vectors[(k, x) + window] for k in range(h + 1)]
            cells += [later[(k, x) + window] for k in range(h)]
            totals = tuple(t + cells[i] * cells[j] for t, (i, j) in zip(totals, PAIRS))
        return totals

    totals = lax.fori_loop(0, bx * tiles, products, tuple(jnp.zeros((8, 128), jnp.float32) for _ in PAIRS))
    sublane = lax.broadcasted_iota(jnp.int32, (8, 128), 0)
    sums[...] = jnp.zeros_like(sums)
    for base in range(0, len(PAIRS), 8):
        packed = jnp.zeros((8, 128), jnp.float32)
        for k, total in enumerate(totals[base : base + 8]):
            for distance in (4, 2, 1):
                total = total + pltpu.roll(total, distance, 0)
            packed = jnp.where(sublane == k, total, packed)
        sums[base : base + 8] = packed
    ones = jnp.ones(gram.shape, jnp.float32)
    gram[...] = lax.dot_general(
        ones, sums[...], (((1,), (1,)), ((), ())), precision=lax.Precision.HIGHEST, preferred_element_type=jnp.float32
    )


def last_kernel(cell_count, gram, vectors, later, out, factor, coef, result, sem):
    _, bx, by, nz = vectors.shape
    total = gram[0:8]
    for row in range(8, gram.shape[0], 8):
        total = total + gram[row : row + 8]
    for distance in (4, 2, 1):
        total = total + pltpu.roll(total, distance, 0)
    total = total * (1.0 / cell_count)
    entry = {}
    for k, (i, j) in enumerate(PAIRS):
        entry[i, j] = jnp.broadcast_to(total[:, k : k + 1], (8, 128))
    divisor = jnp.sqrt(entry[0, 0] * (1.0 / (LIFT * LIFT)) + EPSILON)
    scale = 1.0 / (divisor * LIFT)
    place = {pair: k for k, pair in enumerate(PAIRS)}
    for j in range(BASIS):
        length = jnp.sqrt(entry[j, j])
        inverse = 1.0 / length
        row = {k: entry[j, k] * inverse for k in range(j + 1, BASIS)}
        for i in range(j + 1, BASIS):
            for k in range(i, BASIS):
                entry[i, k] = entry[i, k] - row[i] * row[k]
        entry[j, j] = length
        coef[place[j, j]] = inverse
        for k in range(j + 1, BASIS):
            entry[j, k] = row[k]
            coef[place[j, k]] = row[k]
    sublane = lax.broadcasted_iota(jnp.int32, (8, 128), 0)
    lane = lax.broadcasted_iota(jnp.int32, (8, 128), 1)
    tops = []
    for base in range(0, BASIS, 8):
        packed = jnp.zeros((8, 128), jnp.float32)
        for (i, j), value in entry.items():
            if base <= i < base + 8:
                packed = jnp.where((sublane == i - base) & (lane == j), value, packed)
        tops.append(packed * scale)
    factor[...] = jnp.concatenate(tops, axis=0)[:BASIS, :BASIS]

    tiles = by // 8

    def solve(x, carry):
        for y in range(tiles):
            for z in range(0, nz, 128):
                window = (x, slice(8 * y, 8 * y + 8), slice(z, z + 128))
                columns = []
                for j in range(BASIS):
                    value = vectors[(j,) + window] if j <= HALO else later[(j - HALO - 1,) + window]
                    for i in range(j):
                        value = value - coef[place[i, j]] * columns[i]
                    value = value * coef[place[j, j]]
                    result[(j,) + window] = value
                    columns.append(value)
        pltpu.make_async_copy(result.at[:, x], out.at[:, x], sem.at[x]).start()
        return carry

    lax.fori_loop(0, bx, solve, 0)
    for x in range(bx):
        pltpu.make_async_copy(result.at[:, x], out.at[:, x], sem.at[x]).wait()


def shape(*dims):
    return jax.ShapeDtypeStruct(dims, jnp.float32)


def per_device(forcing, reaction, velocity):
    bx, by, nz = forcing.shape
    devices = lax.axis_size("gx") * lax.axis_size("gy")
    cell_count = float(bx * by * nz * devices)
    h, c, ext = HALO, HALO - 1, bx + 2 * HALO
    fields = [reaction, velocity[0], velocity[1], velocity[2]]
    params = pltpu.CompilerParams(vmem_limit_bytes=24 << 20)

    to_low = jnp.concatenate([forcing[:h]] + [v[:c] for v in fields])
    to_high = jnp.concatenate([forcing[bx - h :]] + [v[bx - c :] for v in fields])
    low, high = swap_x(to_low, to_high)
    own_rows = swap_y(edge_rows(jnp.concatenate([forcing] + fields)))
    corner_rows = swap_y(edge_rows(jnp.concatenate([low, high])))
    vectors, to_low, to_high, rows, coef = pl.pallas_call(
        first_kernel,
        out_shape=[
            shape(h + 1, bx, by, nz),
            shape(h + c, by, nz),
            shape(h + c, by, nz),
            shape(2 * bx, 2 * h, nz),
            shape(4, bx + 2 * c, by + 2 * h, nz),
        ],
        in_specs=[VMEM] * 7,
        out_specs=[VMEM] * 5,
        scratch_shapes=[pltpu.VMEM((h + 1, ext, by + 2 * h, nz), jnp.float32)],
        compiler_params=params,
        name="first",
    )(forcing, reaction, velocity, low, high, own_rows, corner_rows)

    low, high = swap_x(to_low, to_high)
    own_rows = swap_y(rows)
    corner_rows = swap_y(edge_rows(jnp.concatenate([low, high])))
    later, gram = pl.pallas_call(
        second_kernel,
        out_shape=[shape(h, bx, by, nz), shape(devices, 128)],
        in_specs=[VMEM] * 6,
        out_specs=[VMEM] * 2,
        scratch_shapes=[
            pltpu.VMEM((h + 2, ext, by + 2 * h, nz), jnp.float32),
            pltpu.VMEM((128, 128), jnp.float32),
        ],
        compiler_params=params,
        name="second",
    )(vectors, coef, low, high, own_rows, corner_rows)
    gram = lax.all_to_all(gram, AXES, 0, 0, tiled=True)

    def last(*refs):
        last_kernel(cell_count, *refs)

    return pl.pallas_call(
        last,
        out_shape=[shape(BASIS, bx, by, nz), shape(BASIS, BASIS)],
        in_specs=[VMEM] * 3,
        out_specs=[pl.BlockSpec(memory_space=pl.ANY), VMEM],
        scratch_shapes=[
            pltpu.VMEM((len(PAIRS), 8, 128), jnp.float32),
            pltpu.VMEM((BASIS, bx, by, nz), jnp.float32),
            pltpu.SemaphoreType.DMA((bx,)),
        ],
        compiler_params=params,
        name="last",
    )(gram, vectors, later)


def solution(mesh):
    in_specs = (P("gx", "gy", None), P("gx", "gy", None), P(None, "gx", "gy", None))
    out_specs = (P(None, "gx", "gy", None), P())
    return jax.shard_map(per_device, mesh=mesh, in_specs=in_specs, out_specs=out_specs, check_vma=False)
```

```python
import jax
import jax.numpy as jnp
from jax import lax
from jax.experimental import pallas as pl
from jax.experimental.pallas import tpu as pltpu
from jax.sharding import PartitionSpec as P

BASIS = 9
STEPS = 4
MARGIN = 8
EDGE = 4

DIFFUSION = 0.03
CENTRE_SHIFT = 1.18
HALF_WIDTH = 0.95
EPSILON = 1e-06
LIFT = 1024.0
SCALES = (2.0 / HALF_WIDTH, 1.0 / HALF_WIDTH, 1.0 / HALF_WIDTH, 1.0 / HALF_WIDTH)
SHIFTS = (2.0 * (6.0 * DIFFUSION - CENTRE_SHIFT) / HALF_WIDTH, 0.0, 0.0, 0.0)
AXES = ("gx", "gy")
VMEM = pl.BlockSpec(memory_space=pltpu.VMEM)
HBM = pl.BlockSpec(memory_space=pltpu.MemorySpace.HBM)


COMPUTED = ((1, 1), (2, 1), (2, 2), (3, 1))
GIVEN = ((0, 1), (0, 2), (1, 2))
TIP = (2, 2)
DEPTHS = (2, 1, 2, 1, 1)
OFFSETS = (0, 2, 3, 5, 6)


def pairs_of(low, high):
    return [(i, j) for j in range(low, high) for i in range(j + 1)]


GROUPS = (pairs_of(0, STEPS + 1), pairs_of(STEPS + 1, BASIS))
STARTS = (0, -(-len(GROUPS[0]) // 8) * 8)
GRAM_ROWS = STARTS[1] - (-len(GROUPS[1]) // 8) * 8
PLACE = {pair: start + k for start, group in zip(STARTS, GROUPS) for k, pair in enumerate(group)}


def ring(axis, step):
    count = lax.axis_size(axis)
    return [(i, (i + step) % count) for i in range(count)]


def swap_x(to_low, to_high):
    return lax.ppermute(to_high, "gx", ring("gx", 1)), lax.ppermute(to_low, "gx", ring("gx", -1))


def swap_y(block):
    rows = block.shape[1]
    return swap_rows(block[:, :MARGIN], block[:, rows - MARGIN :])


def swap_rows(low, high):
    if lax.axis_size("gy") == 2:
        return lax.ppermute(jnp.concatenate([low, high], axis=1), "gy", ring("gy", 1))
    above = lax.ppermute(low, "gy", ring("gy", -1))
    below = lax.ppermute(high, "gy", ring("gy", 1))
    return jnp.concatenate([above, below], axis=1)


def doubled(centre, east, west, coef):
    rows, lanes = centre.shape
    kept = east.shape[0]
    north = pltpu.roll(centre, rows - 1, 0)[:kept]
    south = pltpu.roll(centre, 1, 0)[:kept]
    centre = centre[:kept]
    upper = pltpu.roll(centre, lanes - 1, 1)
    lower = pltpu.roll(centre, 1, 1)
    around = (east + west) + (north + south) + (upper + lower)
    slopes = coef[1] * (east - west) + coef[2] * (north - south) + coef[3] * (upper - lower)
    return coef[0] * centre + slopes - (2.0 * DIFFUSION / HALF_WIDTH) * around


def scaled(k, value):
    return value * SCALES[k] + SHIFTS[k]


def products(pairs, bx, by, nz, cell):
    needed = sorted({i for pair in pairs for i in pair})
    tiles = by // 8

    def add(at, totals):
        x, y = at // tiles, pl.multiple_of(at % tiles * 8, 8)
        for z in range(0, nz, 128):
            cells = {i: cell(i, x, pl.ds(y, 8), pl.ds(z, 128)) for i in needed}
            totals = tuple(t + cells[i] * cells[j] for t, (i, j) in zip(totals, pairs))
        return totals

    totals = lax.fori_loop(0, bx * tiles, add, tuple(jnp.zeros((8, 128), jnp.float32) for _ in pairs), unroll=2)
    sublane = lax.broadcasted_iota(jnp.int32, (8, 128), 0)
    rows = []
    for base in range(0, len(pairs), 8):
        packed = jnp.zeros((8, 128), jnp.float32)
        for k, total in enumerate(totals[base : base + 8]):
            for distance in (4, 2, 1):
                total = total + pltpu.roll(total, distance, 0)
            packed = jnp.where(sublane == k, total, packed)
        rows.append(packed)
    return rows


def reader(start, one, two=None):
    def cell(i, x, y, z):
        if i == 0:
            return start[x, y, z]
        if i <= STEPS:
            return one[i - 1, x, y, z]
        return two[i - 1 - STEPS, x, y, z]

    return cell


def second_interior_kernel(by, start, one, coef, given, vectors, gram):
    del given
    bx, _, nz = start.shape
    places = own_places(bx, STEPS, vectors)
    cells = Cells(bx, coef, None, lambda j, x: places[j, x])
    for x in (1, 2, bx - 3, bx - 2):
        cells.known[STEPS + 1, x] = lambda x=x: vectors[0, x]
    for x in range(bx):
        cells.known[STEPS, x] = lambda x=x: one[STEPS - 1, x]
        cells.known[STEPS - 1, x] = lambda x=x: one[STEPS - 2, x]
    cells.interior(STEPS)
    for k, row in enumerate(products(GROUPS[0], bx, by, nz, reader(start, one))):
        gram[8 * k : 8 * k + 8] = row


def copy_all(copies, sem):
    copies = [pltpu.make_async_copy(a, b, sem.at[k]) for k, (a, b) in enumerate(copies)]
    for copy in copies:
        copy.start()
    for copy in copies:
        copy.wait()


def fields_of(f, r, vel):
    return f, r, vel.at[0], vel.at[1], vel.at[2]


REACH = ((0, 3),) + ((1, 3),) * 4
SWAPPED = tuple(sum(2 * (high - low) for low, high in REACH[:k]) for k in range(6))


def edge_rows(block):
    rows = block.shape[-2]
    low, high = block[..., : 2 * EDGE, :], block[..., rows - 2 * EDGE :, :]
    row = lax.broadcasted_iota(jnp.int32, low.shape, low.ndim - 2)
    return jnp.where(row < EDGE, low, high)


def pack_kernel(f, r, vel, fields, to_low, to_high, rows, sem):
    bx = f.shape[0]
    copy_all([(field, fields.at[k]) for k, field in enumerate(fields_of(f, r, vel))], sem)
    for k in range(5):
        depth, at = DEPTHS[k], OFFSETS[k]
        to_low[at : at + depth] = fields[k, 0:depth]
        to_high[at : at + depth] = fields[k, bx - depth : bx]
        (low, high), at = REACH[k], SWAPPED[k]
        rows[at : at + high - low] = edge_rows(fields[k, low:high])
        rows[at + high - low : at + 2 * (high - low)] = edge_rows(fields[k, bx - high : bx - low])


def inner_kernel(fields, rows, to_low, to_high, scratch):
    _, bx, by, _ = fields.shape

    def layer(k, x):
        (low, high), at = REACH[k], SWAPPED[k]
        at += x - low if x < high else high - low + x - (bx - high)
        return jnp.concatenate([fields[k, x], rows[at]], axis=0)

    class Coefficients:
        shape = (4, bx)

        def __getitem__(self, at):
            return scaled(at[0], layer(at[0] + 1, at[1]))

    cells = Cells(bx, Coefficients(), None, lambda j, x: (scratch, {1: 0, 2: 1, bx - 3: 2, bx - 2: 3}[x]))
    for x in (0, 1, 2, 3, bx - 4, bx - 3, bx - 2, bx - 1):
        if 3 <= x < bx - 3:
            cells.known[0, x] = lambda x=x: jnp.concatenate([fields[0, x], jnp.zeros_like(rows[0])], axis=0) * LIFT
        else:
            cells.known[0, x] = lambda x=x: layer(0, x) * LIFT
    to_low[0] = cells.get(1, 1)[:by]
    to_high[0] = cells.get(1, bx - 2)[:by]
    to_low[1] = cells.tip(0, 1, True)[:by]
    to_high[1] = cells.tip(0, bx - 2, False)[:by]


class Cells:
    def __init__(self, bx, coef, edge, place):
        self.bx, self.coef, self.edge, self.place = bx, coef, edge, place
        self.known, self.computed = {}, {}

    def coefficients(self, x):
        if 0 <= x < self.bx:
            return [self.coef[k, x] for k in range(4)]
        return [self.edge[k, 0 if x < 0 else 1] for k in range(4)]

    def get(self, j, x):
        if (j, x) not in self.known:
            if (j, x) in self.computed:
                new = self.computed[j, x]()
            else:
                new = doubled(self.get(j - 1, x), self.get(j - 1, x + 1), self.get(j - 1, x - 1), self.coefficients(x))
                new = new * 0.5 if j == 1 else new - self.get(j - 2, x)
            ref, at = self.place(j, x)
            ref[at] = new
            self.known[j, x] = lambda: ref[at]
        return self.known[j, x]()

    def tip(self, base, x, below):
        j = base + TIP[0]
        centre, beyond = self.get(j - 1, x), self.get(j - 1, x + 1 if below else x - 1)
        nothing = jnp.zeros_like(centre)
        pair = (beyond, nothing) if below else (nothing, beyond)
        return doubled(centre, *pair, self.coefficients(x)) - self.get(j - 2, x)

    def interior(self, base):
        for j in range(1, STEPS):
            for x in range(j, self.bx - j):
                self.get(base + j, x)

    def finish(self, base):
        for j in range(1, STEPS + 1):
            reach = max([m for i, m in COMPUTED if i == j], default=0)
            for x in range(-reach, self.bx + reach):
                self.get(base + j, x)


def halo_layer(bx, m, low_side):
    return -m if low_side else bx - 1 + m


def own_places(bx, base, ref):
    return {(base + j, x): (ref, (j - 1, x)) for j in range(1, STEPS + 1) for x in range(bx)}


def mark_interior(cells, bx, base, ref):
    for j in range(1, STEPS):
        for x in range(j, bx - j):
            cells.known[base + j, x] = lambda j=j, x=x: ref[j - 1, x]


def halo_places(bx, base, scratch, sides=None):
    places, slot = {}, 0
    for j, m in COMPUTED:
        for low_side in (True, False):
            at = (base + j, halo_layer(bx, m, low_side))
            if sides is not None and (j, m) == (STEPS - 1, 1):
                places[at] = (sides, 0 if low_side else 1)
            else:
                places[at] = (scratch, slot)
                slot += 1
    return places


def prepare_kernel(fields, rows, start, coef, vectors):
    _, bx, by, _ = fields.shape
    start[:, 0:by] = fields[0] * LIFT
    start[:, by:] = rows[0:bx] * LIFT
    for k in range(4):
        coef[k, :, 0:by] = scaled(k, fields[k + 1])
        coef[k, :, by:] = scaled(k, rows[bx * (k + 1) : bx * (k + 2)])
    places = own_places(bx, 0, vectors)
    cells = Cells(bx, coef, None, lambda j, x: places[j, x])
    for x in range(bx):
        cells.known[0, x] = lambda x=x: start[x]
    cells.interior(0)


def first_kernel(
    start, coef, low, high, low_later, high_later, corner, given, vectors, to_low, to_high, following, sides, edge, weight, scratch
):
    del given
    bx, by = start.shape[0], low.shape[1]
    size, later = low.shape[0], low_later.shape[0]
    places = own_places(bx, 0, vectors) | own_places(bx, STEPS, following) | halo_places(bx, 0, scratch, sides)
    for side, slab, base in ((0, low, 0), (1, high, size)):
        for k in range(4):
            depth, at = DEPTHS[k + 1], OFFSETS[k + 1]
            at += depth - 1 if side == 0 else 0
            edge[k, side, 0:by] = scaled(k, slab[at])
            edge[k, side, by:] = scaled(k, corner[base + at])
        at = OFFSETS[2] + (0 if side == 0 else 1)
        sign = SCALES[1] if side == 0 else -SCALES[1]
        weight[side, 0:by] = slab[at] * sign - 2.0 * DIFFUSION / HALF_WIDTH
        weight[side, by:] = corner[base + at] * sign - 2.0 * DIFFUSION / HALF_WIDTH
    cells = Cells(bx, coef, edge, lambda j, x: places[j, x])
    mark_interior(cells, bx, 0, vectors)
    for x in range(bx):
        cells.known[0, x] = lambda x=x: start[x]
    for side, slab, after, base, after_base in (
        (0, low, low_later, 0, 2 * size),
        (1, high, high_later, size, 2 * size + later),
    ):

        def wide(ref, at, offset):
            return jnp.concatenate([ref[at], corner[offset + at]], axis=0)

        def starting(m, side=side, slab=slab, base=base):
            return wide(slab, DEPTHS[0] - m if side == 0 else m - 1, base) * LIFT

        near, far = halo_layer(bx, 1, side == 0), halo_layer(bx, 2, side == 0)
        cells.known[0, near] = lambda f=starting: f(1)
        cells.known[0, far] = lambda f=starting: f(2)
        cells.known[1, far] = lambda a=after, o=after_base: wide(a, 0, o)
        cells.computed[2, far] = lambda a=after, o=after_base, side=side, near=near: (
            wide(a, 1, o) + weight[side] * cells.get(1, near)
        )
    cells.finish(0)
    for out, below, one, two in ((to_low, True, 0, 1), (to_high, False, bx - 1, bx - 2)):
        leaving = [
            cells.get(STEPS, one),
            cells.get(STEPS, two),
            cells.get(STEPS + 1, two),
            cells.tip(STEPS, two, below),
        ]
        for at, layer in enumerate(leaving):
            above, under = layer[by : by + MARGIN], layer[by + MARGIN :]
            row = lax.broadcasted_iota(jnp.int32, above.shape, 0)
            out[at, 0:by] = layer[:by]
            out[at, by:] = jnp.where(row < EDGE, above, under)


def second_kernel(start, one, given, sides, coef, edge, weight, low, high, early_gram, two, gram, scratch):
    del given
    bx, _, nz = start.shape
    by = low.shape[1] - 2 * EDGE
    places = own_places(bx, STEPS, two) | halo_places(bx, STEPS, scratch)
    cells = Cells(bx, coef, edge, lambda j, x: places[j, x])
    mark_interior(cells, bx, STEPS, two)
    for x in range(bx):
        cells.known[STEPS, x] = lambda x=x: one[STEPS - 1, x]
        cells.known[STEPS - 1, x] = lambda x=x: one[STEPS - 2, x]
    for side, slab in ((0, low), (1, high)):
        near, far = halo_layer(bx, 1, side == 0), halo_layer(bx, 2, side == 0)

        def wide(at, slab=slab):
            return jnp.concatenate([slab[at], slab[at, by:]], axis=0)

        cells.known[STEPS - 1, near] = lambda side=side: sides[side]
        cells.known[STEPS, near] = lambda f=wide: f(0)
        cells.known[STEPS, far] = lambda f=wide: f(1)
        cells.known[STEPS + 1, far] = lambda f=wide: f(2)
        cells.computed[STEPS + 2, far] = lambda f=wide, side=side, near=near: (
            f(3) + weight[side] * cells.get(STEPS + 1, near)
        )
    cells.finish(STEPS)
    rows = products(GROUPS[1], bx, by, nz, reader(start, one, two))
    sums = jnp.concatenate([early_gram[...]] + rows, axis=0)
    on = lax.broadcasted_iota(jnp.int32, sums.shape, 0) == lax.broadcasted_iota(jnp.int32, sums.shape, 1)
    line = jnp.sum(jnp.where(on, jnp.sum(sums, axis=1, keepdims=True), 0.0), axis=0, keepdims=True)
    gram[...] = jnp.broadcast_to(line, gram.shape)


def last_kernel(cell_count, gram, start, one, two, out, factor, coef, result, sem):
    _, bx, by, nz = result.shape
    total = gram[0:8]
    for row in range(8, gram.shape[0], 8):
        total = total + gram[row : row + 8]
    for distance in (4, 2, 1):
        total = total + pltpu.roll(total, distance, 0)
    total = total * (1.0 / cell_count)
    entry = {pair: jnp.broadcast_to(total[:, k : k + 1], (8, 128)) for pair, k in PLACE.items()}
    divisor = jnp.sqrt(entry[0, 0] * (1.0 / (LIFT * LIFT)) + EPSILON)
    scale = 1.0 / (divisor * LIFT)
    for j in range(BASIS):
        length = jnp.sqrt(entry[j, j])
        inverse = 1.0 / length
        row = {k: entry[j, k] * inverse for k in range(j + 1, BASIS)}
        for i in range(j + 1, BASIS):
            for k in range(i, BASIS):
                entry[i, k] = entry[i, k] - row[i] * row[k]
        entry[j, j] = length
        coef[PLACE[j, j]] = inverse
        for k in range(j + 1, BASIS):
            entry[j, k] = row[k]
            coef[PLACE[j, k]] = row[k]
    cell = reader(start, one, two)
    tiles = by // 8

    def solve(x, carry):
        for y in range(0, tiles, 2):
            windows = [
                (x, slice(8 * t, 8 * t + 8), slice(z, z + 128))
                for t in range(y, min(y + 2, tiles))
                for z in range(0, nz, 128)
            ]
            columns = []
            for j in range(BASIS):
                values = [cell(j, *window) for window in windows]
                for i in range(j):
                    factor_ = coef[PLACE[i, j]]
                    values = [v - factor_ * c for v, c in zip(values, columns[i])]
                factor_ = coef[PLACE[j, j]]
                values = [v * factor_ for v in values]
                for window, value in zip(windows, values):
                    result[(j,) + window] = value
                columns.append(values)
        pltpu.make_async_copy(result.at[:, x], out.at[:, x], sem.at[x]).start()
        return carry

    lax.fori_loop(0, bx, solve, 0)
    sublane = lax.broadcasted_iota(jnp.int32, (8, 128), 0)
    lane = lax.broadcasted_iota(jnp.int32, (8, 128), 1)
    tops = []
    for base in range(0, BASIS, 8):
        packed = jnp.zeros((8, 128), jnp.float32)
        for (i, j), value in entry.items():
            if base <= i < base + 8:
                packed = jnp.where((sublane == i - base) & (lane == j), value, packed)
        tops.append(packed * scale)
    factor[...] = jnp.concatenate(tops, axis=0)[:BASIS, :BASIS]
    for x in range(bx):
        pltpu.make_async_copy(result.at[:, x], out.at[:, x], sem.at[x]).wait()


def shape(*dims):
    return jax.ShapeDtypeStruct(dims, jnp.float32)


def call(kernel, outs, *args, name, scratch=(), us=0.02, in_specs=None, out_specs=None, aliases=None):
    return pl.pallas_call(
        kernel,
        out_shape=outs,
        in_specs=in_specs or [VMEM] * len(args),
        out_specs=out_specs or [VMEM] * len(outs),
        scratch_shapes=scratch,
        input_output_aliases=aliases or {},
        compiler_params=pltpu.CompilerParams(vmem_limit_bytes=24 << 20),
        cost_estimate=pl.CostEstimate(flops=0, transcendentals=0, bytes_accessed=int(us * 3e6)),
        name=name,
    )(*args)


def per_device(forcing, reaction, velocity):
    bx, by, nz = forcing.shape
    devices = lax.axis_size("gx") * lax.axis_size("gy")
    cell_count = float(bx * by * nz * devices)
    wide = by + 2 * MARGIN
    inputs = tuple(pltpu.with_memory_space_constraint(v, pltpu.MemorySpace.HBM) for v in (forcing, reaction, velocity))
    vectors = shape(STEPS, bx, wide, nz)
    fields, to_low, to_high, rows = call(
        pack_kernel,
        [shape(5, bx, by, nz)] + [shape(sum(DEPTHS), by, nz)] * 2 + [shape(SWAPPED[5], 2 * EDGE, nz)],
        *inputs,
        name="pack",
        in_specs=[HBM] * 3,
        scratch=[pltpu.SemaphoreType.DMA((5,))],
    )
    low, high = swap_x(to_low, to_high)
    rows = swap_rows(rows[:, :EDGE], rows[:, EDGE:])
    to_low, to_high = call(
        inner_kernel,
        [shape(2, by, nz)] * 2,
        fields,
        rows,
        name="inner",
        scratch=[pltpu.VMEM((4, by + 2 * EDGE, nz), jnp.float32)],
    )
    low_later, high_later = swap_x(to_low, to_high)
    rows = swap_y(fields.reshape(5 * bx, by, nz))
    start, coef, one = call(
        prepare_kernel, [shape(bx, wide, nz), shape(4, bx, wide, nz), vectors], fields, rows, name="prepare"
    )
    corner = swap_y(jnp.concatenate([low, high, low_later, high_later]))
    one, to_low, to_high, two, sides, edge, weight = call(
        first_kernel,
        [
            vectors,
            shape(4, by + 2 * EDGE, nz),
            shape(4, by + 2 * EDGE, nz),
            vectors,
            shape(2, wide, nz),
            shape(4, 2, wide, nz),
            shape(2, wide, nz),
        ],
        start,
        coef,
        low,
        high,
        low_later,
        high_later,
        corner,
        one,
        name="first",
        scratch=[pltpu.VMEM((2 * len(COMPUTED), wide, nz), jnp.float32)],
        aliases={7: 0},
    )
    low, high = swap_x(to_low, to_high)
    two, early_gram = call(
        lambda *refs: second_interior_kernel(by, *refs),
        [vectors, shape(STARTS[1], 128)],
        start,
        one,
        coef,
        two,
        name="second_interior",
        aliases={3: 0},
    )
    two, gram = call(
        second_kernel,
        [vectors, shape(devices, 128)],
        start,
        one,
        two,
        sides,
        coef,
        edge,
        weight,
        low,
        high,
        early_gram,
        name="second",
        scratch=[pltpu.VMEM((2 * len(COMPUTED), wide, nz), jnp.float32)],
        aliases={2: 0},
    )
    gram = lax.all_to_all(gram, AXES, 0, 0, tiled=True)
    return call(
        lambda *refs: last_kernel(cell_count, *refs),
        [shape(BASIS, bx, by, nz), shape(BASIS, BASIS)],
        gram,
        start,
        one,
        two,
        name="last",
        out_specs=[pl.BlockSpec(memory_space=pl.ANY), VMEM],
        scratch=[
            pltpu.VMEM((GRAM_ROWS, 8, 128), jnp.float32),
            pltpu.VMEM((BASIS, bx, by, nz), jnp.float32),
            pltpu.SemaphoreType.DMA((bx,)),
        ],
    )


def solution(mesh):
    in_specs = (P("gx", "gy", None), P("gx", "gy", None), P(None, "gx", "gy", None))
    out_specs = (P(None, "gx", "gy", None), P())
    return jax.shard_map(per_device, mesh=mesh, in_specs=in_specs, out_specs=out_specs, check_vma=False)
```

```python
import jax
import jax.numpy as jnp
from jax import lax
from jax.experimental import pallas as pl
from jax.experimental.pallas import tpu as pltpu
from jax.sharding import PartitionSpec as P

BASIS = 9
STEPS = 4
MARGIN = 8
EDGE = 4

DIFFUSION = 0.03
CENTRE_SHIFT = 1.18
HALF_WIDTH = 0.95
EPSILON = 1e-06
LIFT = 1024.0
SCALES = (2.0 / HALF_WIDTH, 1.0 / HALF_WIDTH, 1.0 / HALF_WIDTH, 1.0 / HALF_WIDTH)
SHIFTS = (2.0 * (6.0 * DIFFUSION - CENTRE_SHIFT) / HALF_WIDTH, 0.0, 0.0, 0.0)
AXES = ("gx", "gy")
VMEM = pl.BlockSpec(memory_space=pltpu.VMEM)
HBM = pl.BlockSpec(memory_space=pltpu.MemorySpace.HBM)


COMPUTED = ((1, 1), (2, 1), (2, 2), (3, 1))
GIVEN = ((0, 1), (0, 2), (1, 2))
TIP = (2, 2)
DEPTHS = (2, 1, 2, 1, 1)
OFFSETS = (0, 2, 3, 5, 6)


def pairs_of(low, high):
    return [(i, j) for j in range(low, high) for i in range(j + 1)]


GROUPS = (pairs_of(0, STEPS + 1), pairs_of(STEPS + 1, BASIS))
STARTS = (0, -(-len(GROUPS[0]) // 8) * 8)
GRAM_ROWS = STARTS[1] - (-len(GROUPS[1]) // 8) * 8
PLACE = {pair: start + k for start, group in zip(STARTS, GROUPS) for k, pair in enumerate(group)}


def ring(axis, step):
    count = lax.axis_size(axis)
    return [(i, (i + step) % count) for i in range(count)]


def swap_x(to_low, to_high):
    return lax.ppermute(to_high, "gx", ring("gx", 1)), lax.ppermute(to_low, "gx", ring("gx", -1))


def swap_y(block):
    rows = block.shape[1]
    return swap_rows(block[:, :MARGIN], block[:, rows - MARGIN :])


def swap_rows(low, high):
    if lax.axis_size("gy") == 2:
        return lax.ppermute(jnp.concatenate([low, high], axis=1), "gy", ring("gy", 1))
    above = lax.ppermute(low, "gy", ring("gy", -1))
    below = lax.ppermute(high, "gy", ring("gy", 1))
    return jnp.concatenate([above, below], axis=1)


def doubled(centre, east, west, coef):
    rows, lanes = centre.shape
    kept = east.shape[0]
    north = pltpu.roll(centre, rows - 1, 0)[:kept]
    south = pltpu.roll(centre, 1, 0)[:kept]
    centre = centre[:kept]
    upper = pltpu.roll(centre, lanes - 1, 1)
    lower = pltpu.roll(centre, 1, 1)
    around = (east + west) + (north + south) + (upper + lower)
    slopes = coef[1] * (east - west) + coef[2] * (north - south) + coef[3] * (upper - lower)
    return coef[0] * centre + slopes - (2.0 * DIFFUSION / HALF_WIDTH) * around


def scaled(k, value):
    return value * SCALES[k] + SHIFTS[k]


def products(pairs, bx, by, nz, cell):
    needed = sorted({i for pair in pairs for i in pair})
    tiles = by // 8

    def add(at, totals):
        x, y = at // tiles, pl.multiple_of(at % tiles * 8, 8)
        for z in range(0, nz, 128):
            cells = {i: cell(i, x, pl.ds(y, 8), pl.ds(z, 128)) for i in needed}
            totals = tuple(t + cells[i] * cells[j] for t, (i, j) in zip(totals, pairs))
        return totals

    totals = lax.fori_loop(0, bx * tiles, add, tuple(jnp.zeros((8, 128), jnp.float32) for _ in pairs), unroll=2)
    sublane = lax.broadcasted_iota(jnp.int32, (8, 128), 0)
    rows = []
    for base in range(0, len(pairs), 8):
        packed = jnp.zeros((8, 128), jnp.float32)
        for k, total in enumerate(totals[base : base + 8]):
            for distance in (4, 2, 1):
                total = total + pltpu.roll(total, distance, 0)
            packed = jnp.where(sublane == k, total, packed)
        rows.append(packed)
    return rows


def reader(start, one, two=None):
    def cell(i, x, y, z):
        if i == 0:
            return start[x, y, z]
        if i <= STEPS:
            return one[i - 1, x, y, z]
        return two[i - 1 - STEPS, x, y, z]

    return cell


def second_interior_kernel(by, start, one, coef, given, vectors, gram):
    del given
    bx, _, nz = start.shape
    places = own_places(bx, STEPS, vectors)
    cells = Cells(bx, coef, None, lambda j, x: places[j, x])
    for x in (1, 2, bx - 3, bx - 2):
        cells.known[STEPS + 1, x] = lambda x=x: vectors[0, x]
    for x in range(bx):
        cells.known[STEPS, x] = lambda x=x: one[STEPS - 1, x]
        cells.known[STEPS - 1, x] = lambda x=x: one[STEPS - 2, x]
    cells.interior(STEPS)
    for k, row in enumerate(products(GROUPS[0], bx, by, nz, reader(start, one))):
        gram[8 * k : 8 * k + 8] = row


def fields_of(f, r, vel):
    return f, r, vel.at[0], vel.at[1], vel.at[2]


REACH = ((0, 3),) + ((1, 3),) * 4
SWAPPED = tuple(sum(2 * (high - low) for low, high in REACH[:k]) for k in range(6))


def edge_rows(block):
    rows = block.shape[-2]
    low, high = block[..., : 2 * EDGE, :], block[..., rows - 2 * EDGE :, :]
    row = lax.broadcasted_iota(jnp.int32, low.shape, low.ndim - 2)
    return jnp.where(row < EDGE, low, high)


def pack_kernel(f, r, vel, fields, to_low, to_high, rows, sem):
    bx = f.shape[0]
    copies = [pltpu.make_async_copy(field, fields.at[k], sem.at[k]) for k, field in enumerate(fields_of(f, r, vel))]
    for copy in copies:
        copy.start()
    for k in range(5):
        copies[k].wait()
        depth, at = DEPTHS[k], OFFSETS[k]
        to_low[at : at + depth] = fields[k, 0:depth]
        to_high[at : at + depth] = fields[k, bx - depth : bx]
        (low, high), at = REACH[k], SWAPPED[k]
        rows[at : at + high - low] = edge_rows(fields[k, low:high])
        rows[at + high - low : at + 2 * (high - low)] = edge_rows(fields[k, bx - high : bx - low])


def inner_kernel(fields, rows, to_low, to_high, scratch):
    _, bx, by, _ = fields.shape

    def layer(k, x):
        (low, high), at = REACH[k], SWAPPED[k]
        at += x - low if x < high else high - low + x - (bx - high)
        return jnp.concatenate([fields[k, x], rows[at]], axis=0)

    class Coefficients:
        shape = (4, bx)

        def __getitem__(self, at):
            return scaled(at[0], layer(at[0] + 1, at[1]))

    cells = Cells(bx, Coefficients(), None, lambda j, x: (scratch, {1: 0, 2: 1, bx - 3: 2, bx - 2: 3}[x]))
    for x in (0, 1, 2, 3, bx - 4, bx - 3, bx - 2, bx - 1):
        if 3 <= x < bx - 3:
            cells.known[0, x] = lambda x=x: jnp.concatenate([fields[0, x], jnp.zeros_like(rows[0])], axis=0) * LIFT
        else:
            cells.known[0, x] = lambda x=x: layer(0, x) * LIFT
    to_low[0] = cells.get(1, 1)[:by]
    to_high[0] = cells.get(1, bx - 2)[:by]
    to_low[1] = cells.tip(0, 1, True)[:by]
    to_high[1] = cells.tip(0, bx - 2, False)[:by]


class Cells:
    def __init__(self, bx, coef, edge, place):
        self.bx, self.coef, self.edge, self.place = bx, coef, edge, place
        self.known, self.computed = {}, {}

    def coefficients(self, x):
        if 0 <= x < self.bx:
            return [self.coef[k, x] for k in range(4)]
        return [self.edge[k, 0 if x < 0 else 1] for k in range(4)]

    def get(self, j, x):
        if (j, x) not in self.known:
            if (j, x) in self.computed:
                new = self.computed[j, x]()
            else:
                new = doubled(self.get(j - 1, x), self.get(j - 1, x + 1), self.get(j - 1, x - 1), self.coefficients(x))
                new = new * 0.5 if j == 1 else new - self.get(j - 2, x)
            ref, at = self.place(j, x)
            ref[at] = new
            self.known[j, x] = lambda: ref[at]
        return self.known[j, x]()

    def tip(self, base, x, below):
        j = base + TIP[0]
        centre, beyond = self.get(j - 1, x), self.get(j - 1, x + 1 if below else x - 1)
        nothing = jnp.zeros_like(centre)
        pair = (beyond, nothing) if below else (nothing, beyond)
        return doubled(centre, *pair, self.coefficients(x)) - self.get(j - 2, x)

    def interior(self, base):
        for j in range(1, STEPS):
            for x in range(j, self.bx - j):
                self.get(base + j, x)

    def finish(self, base):
        for j in range(1, STEPS + 1):
            reach = max([m for i, m in COMPUTED if i == j], default=0)
            for x in range(-reach, self.bx + reach):
                self.get(base + j, x)


def halo_layer(bx, m, low_side):
    return -m if low_side else bx - 1 + m


def own_places(bx, base, ref):
    return {(base + j, x): (ref, (j - 1, x)) for j in range(1, STEPS + 1) for x in range(bx)}


def mark_interior(cells, bx, base, ref):
    for j in range(1, STEPS):
        for x in range(j, bx - j):
            cells.known[base + j, x] = lambda j=j, x=x: ref[j - 1, x]


def halo_places(bx, base, scratch, sides=None):
    places, slot = {}, 0
    for j, m in COMPUTED:
        for low_side in (True, False):
            at = (base + j, halo_layer(bx, m, low_side))
            if sides is not None and (j, m) == (STEPS - 1, 1):
                places[at] = (sides, 0 if low_side else 1)
            else:
                places[at] = (scratch, slot)
                slot += 1
    return places


def prepare_kernel(fields, rows, start, coef, vectors):
    _, bx, by, _ = fields.shape
    start[:, 0:by] = fields[0] * LIFT
    start[:, by:] = rows[0:bx] * LIFT
    for k in range(4):
        coef[k, :, 0:by] = scaled(k, fields[k + 1])
        coef[k, :, by:] = scaled(k, rows[bx * (k + 1) : bx * (k + 2)])
    places = own_places(bx, 0, vectors)
    cells = Cells(bx, coef, None, lambda j, x: places[j, x])
    for x in range(bx):
        cells.known[0, x] = lambda x=x: start[x]
    cells.interior(0)


def wide_layer(slab, corner, at, base):
    return jnp.concatenate([slab[at], corner[base + at]], axis=0)


def know_start(cells, start, low, high, corner):
    bx, size = start.shape[0], low.shape[0]
    for x in range(bx):
        cells.known[0, x] = lambda x=x: start[x]
    for side, slab, base in ((0, low, 0), (1, high, size)):
        for m in (1, 2):
            at = DEPTHS[0] - m if side == 0 else m - 1
            cells.known[0, halo_layer(bx, m, side == 0)] = lambda slab=slab, base=base, at=at: (
                wide_layer(slab, corner, at, base) * LIFT
            )


def early_range(j, bx):
    return range(j - 2, bx - (j - 2))


def first_kernel(start, coef, low, high, corner, given, vectors, beside, edge, weight):
    del given
    bx, by = start.shape[0], low.shape[1]
    size = low.shape[0]
    places = own_places(bx, 0, vectors)
    places[1, -1], places[1, bx] = (beside, 0), (beside, 1)
    for side, slab, base in ((0, low, 0), (1, high, size)):
        for k in range(4):
            depth, at = DEPTHS[k + 1], OFFSETS[k + 1]
            at += depth - 1 if side == 0 else 0
            edge[k, side, 0:by] = scaled(k, slab[at])
            edge[k, side, by:] = scaled(k, corner[base + at])
        at = OFFSETS[2] + (0 if side == 0 else 1)
        sign = SCALES[1] if side == 0 else -SCALES[1]
        weight[side, 0:by] = slab[at] * sign - 2.0 * DIFFUSION / HALF_WIDTH
        weight[side, by:] = corner[base + at] * sign - 2.0 * DIFFUSION / HALF_WIDTH
    cells = Cells(bx, coef, edge, lambda j, x: places[j, x])
    mark_interior(cells, bx, 0, vectors)
    know_start(cells, start, low, high, corner)
    for j in range(1, STEPS + 1):
        for x in early_range(j, bx):
            cells.get(j, x)


def rest_kernel(
    start, coef, low, high, corner, beside, edge, weight, low_later, high_later, later_corner, given, vectors, to_low, to_high, following, sides, scratch
):
    del given
    bx, by = start.shape[0], low.shape[1]
    later = low_later.shape[0]
    places = own_places(bx, 0, vectors) | own_places(bx, STEPS, following) | halo_places(bx, 0, scratch, sides)
    cells = Cells(bx, coef, edge, lambda j, x: places[j, x])
    know_start(cells, start, low, high, corner)
    for j in range(1, STEPS + 1):
        for x in early_range(j, bx):
            cells.known[j, x] = lambda j=j, x=x: vectors[j - 1, x]
    cells.known[1, -1], cells.known[1, bx] = (lambda: beside[0]), (lambda: beside[1])
    for side, slab, base in ((0, low_later, 0), (1, high_later, later)):
        near, far = halo_layer(bx, 1, side == 0), halo_layer(bx, 2, side == 0)
        cells.known[1, far] = lambda slab=slab, base=base: wide_layer(slab, later_corner, 0, base)
        cells.computed[2, far] = lambda slab=slab, base=base, side=side, near=near: (
            wide_layer(slab, later_corner, 1, base) + weight[side] * cells.get(1, near)
        )
    cells.finish(0)
    for out, below, one, two in ((to_low, True, 0, 1), (to_high, False, bx - 1, bx - 2)):
        leaving = [
            cells.get(STEPS, one),
            cells.get(STEPS, two),
            cells.get(STEPS + 1, two),
            cells.tip(STEPS, two, below),
        ]
        for at, layer in enumerate(leaving):
            above, under = layer[by : by + MARGIN], layer[by + MARGIN :]
            row = lax.broadcasted_iota(jnp.int32, above.shape, 0)
            out[at, 0:by] = layer[:by]
            out[at, by:] = jnp.where(row < EDGE, above, under)


def second_kernel(start, one, given, sides, coef, edge, weight, low, high, early_gram, two, gram, scratch):
    del given
    bx, _, nz = start.shape
    by = low.shape[1] - 2 * EDGE
    places = own_places(bx, STEPS, two) | halo_places(bx, STEPS, scratch)
    cells = Cells(bx, coef, edge, lambda j, x: places[j, x])
    mark_interior(cells, bx, STEPS, two)
    for x in range(bx):
        cells.known[STEPS, x] = lambda x=x: one[STEPS - 1, x]
        cells.known[STEPS - 1, x] = lambda x=x: one[STEPS - 2, x]
    for side, slab in ((0, low), (1, high)):
        near, far = halo_layer(bx, 1, side == 0), halo_layer(bx, 2, side == 0)

        def wide(at, slab=slab):
            return jnp.concatenate([slab[at], slab[at, by:]], axis=0)

        cells.known[STEPS - 1, near] = lambda side=side: sides[side]
        cells.known[STEPS, near] = lambda f=wide: f(0)
        cells.known[STEPS, far] = lambda f=wide: f(1)
        cells.known[STEPS + 1, far] = lambda f=wide: f(2)
        cells.computed[STEPS + 2, far] = lambda f=wide, side=side, near=near: (
            f(3) + weight[side] * cells.get(STEPS + 1, near)
        )
    cells.finish(STEPS)
    rows = products(GROUPS[1], bx, by, nz, reader(start, one, two))
    sums = jnp.concatenate([early_gram[...]] + rows, axis=0)
    on = lax.broadcasted_iota(jnp.int32, sums.shape, 0) == lax.broadcasted_iota(jnp.int32, sums.shape, 1)
    line = jnp.sum(jnp.where(on, jnp.sum(sums, axis=1, keepdims=True), 0.0), axis=0, keepdims=True)
    gram[...] = jnp.broadcast_to(line, gram.shape)


def last_kernel(cell_count, gram, start, one, two, out, factor, result, sem):
    _, bx, by, nz = result.shape
    total = gram[0:8]
    for row in range(8, gram.shape[0], 8):
        total = total + gram[row : row + 8]
    for distance in (4, 2, 1):
        total = total + pltpu.roll(total, distance, 0)
    total = total * (1.0 / cell_count)
    cell = reader(start, one, two)
    entry, inverse, copies = {}, [], []
    for j in range(BASIS):
        for i in range(j + 1):
            k = PLACE[i, j]
            value = jnp.broadcast_to(total[:, k : k + 1], (8, 128))
            if (i, j) == (0, 0):
                mean_square = value * (1.0 / (LIFT * LIFT))
            for above in range(i):
                value = value - entry[above, i] * entry[above, j]
            if i == j:
                inverse.append(lax.rsqrt(value))
            entry[i, j] = value * inverse[i]
        for x in range(bx):
            for y in range(0, by, 8):
                for z in range(0, nz, 128):
                    window = (x, slice(y, y + 8), slice(z, z + 128))
                    value = cell(j, *window)
                    for i in range(j):
                        value = value - entry[i, j] * result[(i,) + window]
                    result[(j,) + window] = value * inverse[j]
        copies.append(pltpu.make_async_copy(result.at[j], out.at[j], sem.at[j]))
        copies[j].start()
    scale = lax.rsqrt(mean_square + EPSILON) * (1.0 / LIFT)
    sublane = lax.broadcasted_iota(jnp.int32, (8, 128), 0)
    lane = lax.broadcasted_iota(jnp.int32, (8, 128), 1)
    tops = []
    for base in range(0, BASIS, 8):
        packed = jnp.zeros((8, 128), jnp.float32)
        for (i, j), value in entry.items():
            if base <= i < base + 8:
                packed = jnp.where((sublane == i - base) & (lane == j), value, packed)
        tops.append(packed * scale)
    factor[...] = jnp.concatenate(tops, axis=0)[:BASIS, :BASIS]
    for copy in copies:
        copy.wait()


def shape(*dims):
    return jax.ShapeDtypeStruct(dims, jnp.float32)


def call(kernel, outs, *args, name, scratch=(), us=0.02, in_specs=None, out_specs=None, aliases=None):
    return pl.pallas_call(
        kernel,
        out_shape=outs,
        in_specs=in_specs or [VMEM] * len(args),
        out_specs=out_specs or [VMEM] * len(outs),
        scratch_shapes=scratch,
        input_output_aliases=aliases or {},
        compiler_params=pltpu.CompilerParams(vmem_limit_bytes=24 << 20),
        cost_estimate=pl.CostEstimate(flops=0, transcendentals=0, bytes_accessed=int(us * 3e6)),
        name=name,
    )(*args)


def per_device(forcing, reaction, velocity):
    bx, by, nz = forcing.shape
    devices = lax.axis_size("gx") * lax.axis_size("gy")
    cell_count = float(bx * by * nz * devices)
    wide = by + 2 * MARGIN
    inputs = tuple(pltpu.with_memory_space_constraint(v, pltpu.MemorySpace.HBM) for v in (forcing, reaction, velocity))
    vectors = shape(STEPS, bx, wide, nz)
    fields, to_low, to_high, rows = call(
        pack_kernel,
        [shape(5, bx, by, nz)] + [shape(sum(DEPTHS), by, nz)] * 2 + [shape(SWAPPED[5], 2 * EDGE, nz)],
        *inputs,
        name="pack",
        in_specs=[HBM] * 3,
        scratch=[pltpu.SemaphoreType.DMA((5,))],
    )
    low, high = swap_x(to_low, to_high)
    rows = swap_rows(rows[:, :EDGE], rows[:, EDGE:])
    to_low, to_high = call(
        inner_kernel,
        [shape(2, by, nz)] * 2,
        fields,
        rows,
        name="inner",
        scratch=[pltpu.VMEM((4, by + 2 * EDGE, nz), jnp.float32)],
    )
    low_later, high_later = swap_x(to_low, to_high)
    rows = swap_y(fields.reshape(5 * bx, by, nz))
    start, coef, one = call(
        prepare_kernel, [shape(bx, wide, nz), shape(4, bx, wide, nz), vectors], fields, rows, name="prepare"
    )
    corner = swap_y(jnp.concatenate([low, high]))
    one, beside, edge, weight = call(
        first_kernel,
        [vectors, shape(2, wide, nz), shape(4, 2, wide, nz), shape(2, wide, nz)],
        start,
        coef,
        low,
        high,
        corner,
        one,
        name="first",
        aliases={5: 0},
    )
    one, to_low, to_high, two, sides = call(
        rest_kernel,
        [vectors, shape(4, by + 2 * EDGE, nz), shape(4, by + 2 * EDGE, nz), vectors, shape(2, wide, nz)],
        start,
        coef,
        low,
        high,
        corner,
        beside,
        edge,
        weight,
        low_later,
        high_later,
        swap_y(jnp.concatenate([low_later, high_later])),
        one,
        name="rest",
        scratch=[pltpu.VMEM((2 * len(COMPUTED), wide, nz), jnp.float32)],
        aliases={11: 0},
    )
    low, high = swap_x(to_low, to_high)
    two, early_gram = call(
        lambda *refs: second_interior_kernel(by, *refs),
        [vectors, shape(STARTS[1], 128)],
        start,
        one,
        coef,
        two,
        name="second_interior",
        aliases={3: 0},
    )
    two, gram = call(
        second_kernel,
        [vectors, shape(devices, 128)],
        start,
        one,
        two,
        sides,
        coef,
        edge,
        weight,
        low,
        high,
        early_gram,
        name="second",
        scratch=[pltpu.VMEM((2 * len(COMPUTED), wide, nz), jnp.float32)],
        aliases={2: 0},
    )
    gram = lax.all_to_all(gram, AXES, 0, 0, tiled=True)
    return call(
        lambda *refs: last_kernel(cell_count, *refs),
        [shape(BASIS, bx, by, nz), shape(BASIS, BASIS)],
        gram,
        start,
        one,
        two,
        name="last",
        out_specs=[pl.BlockSpec(memory_space=pl.ANY), VMEM],
        scratch=[
            pltpu.VMEM((BASIS, bx, by, nz), jnp.float32),
            pltpu.SemaphoreType.DMA((BASIS,)),
        ],
    )


def solution(mesh):
    in_specs = (P("gx", "gy", None), P("gx", "gy", None), P(None, "gx", "gy", None))
    out_specs = (P(None, "gx", "gy", None), P())
    return jax.shard_map(per_device, mesh=mesh, in_specs=in_specs, out_specs=out_specs, check_vma=False)
```

```python
import jax
import jax.numpy as jnp
from jax import lax
from jax.experimental import pallas as pl
from jax.experimental.pallas import tpu as pltpu
from jax.sharding import PartitionSpec as P

BASIS = 9
STEPS = 4
MARGIN = 8
EDGE = 4

DIFFUSION = 0.03
CENTRE_SHIFT = 1.18
HALF_WIDTH = 0.95
EPSILON = 1e-06
LIFT = 1024.0
SCALES = (2.0 / HALF_WIDTH, 1.0 / HALF_WIDTH, 1.0 / HALF_WIDTH, 1.0 / HALF_WIDTH)
SHIFTS = (2.0 * (6.0 * DIFFUSION - CENTRE_SHIFT) / HALF_WIDTH, 0.0, 0.0, 0.0)
AXES = ("gx", "gy")
VMEM = pl.BlockSpec(memory_space=pltpu.VMEM)
HBM = pl.BlockSpec(memory_space=pltpu.MemorySpace.HBM)


COMPUTED = ((1, 1), (2, 1), (2, 2), (3, 1))
GIVEN = ((0, 1), (0, 2), (1, 2))
TIP = (2, 2)
DEPTHS = (2, 1, 2, 1, 1)
OFFSETS = (0, 2, 3, 5, 6)


def pairs_of(low, high):
    return [(i, j) for j in range(low, high) for i in range(j + 1)]


GROUPS = (pairs_of(0, STEPS + 1), pairs_of(STEPS + 1, BASIS))
STARTS = (0, -(-len(GROUPS[0]) // 8) * 8)
GRAM_ROWS = STARTS[1] - (-len(GROUPS[1]) // 8) * 8
PLACE = {pair: start + k for start, group in zip(STARTS, GROUPS) for k, pair in enumerate(group)}


def ring(axis, step):
    count = lax.axis_size(axis)
    return [(i, (i + step) % count) for i in range(count)]


def swap_x(to_low, to_high):
    return lax.ppermute(to_high, "gx", ring("gx", 1)), lax.ppermute(to_low, "gx", ring("gx", -1))


def swap_y(block):
    rows = block.shape[1]
    return swap_rows(block[:, :MARGIN], block[:, rows - MARGIN :])


def swap_rows(low, high):
    if lax.axis_size("gy") == 2:
        return lax.ppermute(jnp.concatenate([low, high], axis=1), "gy", ring("gy", 1))
    above = lax.ppermute(low, "gy", ring("gy", -1))
    below = lax.ppermute(high, "gy", ring("gy", 1))
    return jnp.concatenate([above, below], axis=1)


def doubled(centre, east, west, coef):
    rows, lanes = centre.shape
    kept = east.shape[0]
    north = pltpu.roll(centre, rows - 1, 0)[:kept]
    south = pltpu.roll(centre, 1, 0)[:kept]
    centre = centre[:kept]
    upper = pltpu.roll(centre, lanes - 1, 1)
    lower = pltpu.roll(centre, 1, 1)
    around = (east + west) + (north + south) + (upper + lower)
    slopes = coef[1] * (east - west) + coef[2] * (north - south) + coef[3] * (upper - lower)
    return coef[0] * centre + slopes - (2.0 * DIFFUSION / HALF_WIDTH) * around


def scaled(k, value):
    return value * SCALES[k] + SHIFTS[k]


def products(pairs, first, last, by, nz, cell, totals=None):
    needed = sorted({i for pair in pairs for i in pair})
    tiles = by // 8

    def add(at, totals):
        x, y = first + at // tiles, pl.multiple_of(at % tiles * 8, 8)
        for z in range(0, nz, 128):
            cells = {i: cell(i, x, pl.ds(y, 8), pl.ds(z, 128)) for i in needed}
            totals = tuple(t + cells[i] * cells[j] for t, (i, j) in zip(totals, pairs))
        return totals

    if totals is None:
        totals = tuple(jnp.zeros((8, 128), jnp.float32) for _ in pairs)
    return lax.fori_loop(0, (last - first) * tiles, add, totals, unroll=2)


def summed_rows(totals):
    sublane = lax.broadcasted_iota(jnp.int32, (8, 128), 0)
    rows = []
    for base in range(0, len(totals), 8):
        packed = jnp.zeros((8, 128), jnp.float32)
        for k, total in enumerate(totals[base : base + 8]):
            for distance in (4, 2, 1):
                total = total + pltpu.roll(total, distance, 0)
            packed = jnp.where(sublane == k, total, packed)
        rows.append(packed)
    return rows


def reader(start, one, two=None):
    def cell(i, x, y, z):
        if i == 0:
            return start[x, y, z]
        if i <= STEPS:
            return one[i - 1, x, y, z]
        return two[i - 1 - STEPS, x, y, z]

    return cell


def second_interior_kernel(by, start, one, coef, given, vectors, gram):
    del given
    bx, _, nz = start.shape
    places = own_places(bx, STEPS, vectors)
    cells = Cells(bx, coef, None, lambda j, x: places[j, x])
    for x in (1, 2, bx - 3, bx - 2):
        cells.known[STEPS + 1, x] = lambda x=x: vectors[0, x]
    for x in range(bx):
        cells.known[STEPS, x] = lambda x=x: one[STEPS - 1, x]
        cells.known[STEPS - 1, x] = lambda x=x: one[STEPS - 2, x]
    cells.interior(STEPS)
    for k, row in enumerate(summed_rows(products(GROUPS[0], 0, bx, by, nz, reader(start, one)))):
        gram[8 * k : 8 * k + 8] = row


def fields_of(f, r, vel):
    return f, r, vel.at[0], vel.at[1], vel.at[2]


REACH = ((0, 3),) + ((1, 3),) * 4
SWAPPED = tuple(sum(2 * (high - low) for low, high in REACH[:k]) for k in range(6))


def edge_rows(block):
    rows = block.shape[-2]
    low, high = block[..., : 2 * EDGE, :], block[..., rows - 2 * EDGE :, :]
    row = lax.broadcasted_iota(jnp.int32, low.shape, low.ndim - 2)
    return jnp.where(row < EDGE, low, high)


def pack_kernel(f, r, vel, fields, to_low, to_high, rows, sem):
    bx = f.shape[0]
    copies = [pltpu.make_async_copy(field, fields.at[k], sem.at[k]) for k, field in enumerate(fields_of(f, r, vel))]
    for copy in copies:
        copy.start()
    for k in range(5):
        copies[k].wait()
        depth, at = DEPTHS[k], OFFSETS[k]
        to_low[at : at + depth] = fields[k, 0:depth]
        to_high[at : at + depth] = fields[k, bx - depth : bx]
        (low, high), at = REACH[k], SWAPPED[k]
        rows[at : at + high - low] = edge_rows(fields[k, low:high])
        rows[at + high - low : at + 2 * (high - low)] = edge_rows(fields[k, bx - high : bx - low])


def inner_kernel(fields, rows, to_low, to_high, scratch):
    _, bx, by, _ = fields.shape

    def layer(k, x):
        (low, high), at = REACH[k], SWAPPED[k]
        at += x - low if x < high else high - low + x - (bx - high)
        return jnp.concatenate([fields[k, x], rows[at]], axis=0)

    class Coefficients:
        shape = (4, bx)

        def __getitem__(self, at):
            return scaled(at[0], layer(at[0] + 1, at[1]))

    cells = Cells(bx, Coefficients(), None, lambda j, x: (scratch, ({1: 0, 2: 1, bx - 3: 2, bx - 2: 3}[x],)))
    for x in (0, 1, 2, 3, bx - 4, bx - 3, bx - 2, bx - 1):
        if 3 <= x < bx - 3:
            cells.known[0, x] = lambda x=x: jnp.concatenate([fields[0, x], jnp.zeros_like(rows[0])], axis=0) * LIFT
        else:
            cells.known[0, x] = lambda x=x: layer(0, x) * LIFT
    to_low[0] = cells.get(1, 1)[:by]
    to_high[0] = cells.get(1, bx - 2)[:by]
    to_low[1] = cells.tip(0, 1, True)[:by]
    to_high[1] = cells.tip(0, bx - 2, False)[:by]


class Cells:
    def __init__(self, bx, coef, edge, place):
        self.bx, self.coef, self.edge, self.place = bx, coef, edge, place
        self.known, self.computed = {}, {}

    def coefficients(self, x):
        if 0 <= x < self.bx:
            return [self.coef[k, x] for k in range(4)]
        return [self.edge[k, 0 if x < 0 else 1] for k in range(4)]

    def get(self, j, x):
        if (j, x) not in self.known:
            ref, at = self.place(j, x)
            rows = ref.shape[-2] - (2 * MARGIN if j == BASIS - 1 else 0)
            if (j, x) in self.computed:
                new = self.computed[j, x]()
            else:
                east, west = self.get(j - 1, x + 1)[:rows], self.get(j - 1, x - 1)[:rows]
                new = doubled(self.get(j - 1, x), east, west, [c[:rows] for c in self.coefficients(x)])
                new = new * 0.5 if j == 1 else new - self.get(j - 2, x)[:rows]
            at = at + (slice(0, rows),)
            ref[at] = new
            self.known[j, x] = lambda: ref[at]
        return self.known[j, x]()

    def tip(self, base, x, below):
        j = base + TIP[0]
        centre, beyond = self.get(j - 1, x), self.get(j - 1, x + 1 if below else x - 1)
        nothing = jnp.zeros_like(centre)
        pair = (beyond, nothing) if below else (nothing, beyond)
        return doubled(centre, *pair, self.coefficients(x)) - self.get(j - 2, x)

    def interior(self, base):
        for j in range(1, STEPS):
            for x in range(j, self.bx - j):
                self.get(base + j, x)

    def finish(self, base):
        for j in range(1, STEPS + 1):
            reach = max([m for i, m in COMPUTED if i == j], default=0)
            for x in range(-reach, self.bx + reach):
                self.get(base + j, x)


def halo_layer(bx, m, low_side):
    return -m if low_side else bx - 1 + m


def own_places(bx, base, ref):
    return {(base + j, x): (ref, (j - 1, x)) for j in range(1, STEPS + 1) for x in range(bx)}


def mark_interior(cells, bx, base, ref):
    for j in range(1, STEPS):
        for x in range(j, bx - j):
            cells.known[base + j, x] = lambda j=j, x=x: ref[j - 1, x]


def halo_places(bx, base, scratch, sides=None):
    places, slot = {}, 0
    for j, m in COMPUTED:
        for low_side in (True, False):
            at = (base + j, halo_layer(bx, m, low_side))
            if sides is not None and (j, m) == (STEPS - 1, 1):
                places[at] = (sides, (0 if low_side else 1,))
            else:
                places[at] = (scratch, (slot,))
                slot += 1
    return places


def prepare_kernel(fields, rows, start, coef, vectors):
    _, bx, by, _ = fields.shape
    start[:, 0:by] = fields[0] * LIFT
    start[:, by:] = rows[0:bx] * LIFT
    for k in range(4):
        coef[k, :, 0:by] = scaled(k, fields[k + 1])
        coef[k, :, by:] = scaled(k, rows[bx * (k + 1) : bx * (k + 2)])
    places = own_places(bx, 0, vectors)
    cells = Cells(bx, coef, None, lambda j, x: places[j, x])
    for x in range(bx):
        cells.known[0, x] = lambda x=x: start[x]
    cells.interior(0)


def wide_layer(slab, corner, at, base):
    return jnp.concatenate([slab[at], corner[base + at]], axis=0)


def know_start(cells, start, low, high, corner):
    bx, size = start.shape[0], low.shape[0]
    for x in range(bx):
        cells.known[0, x] = lambda x=x: start[x]
    for side, slab, base in ((0, low, 0), (1, high, size)):
        for m in (1, 2):
            at = DEPTHS[0] - m if side == 0 else m - 1
            cells.known[0, halo_layer(bx, m, side == 0)] = lambda slab=slab, base=base, at=at: (
                wide_layer(slab, corner, at, base) * LIFT
            )


def early_range(j, bx):
    return range(j - 2, bx - (j - 2))


def first_kernel(start, coef, low, high, corner, given, vectors, beside, edge, weight):
    del given
    bx, by = start.shape[0], low.shape[1]
    size = low.shape[0]
    places = own_places(bx, 0, vectors)
    places[1, -1], places[1, bx] = (beside, (0,)), (beside, (1,))
    for side, slab, base in ((0, low, 0), (1, high, size)):
        for k in range(4):
            depth, at = DEPTHS[k + 1], OFFSETS[k + 1]
            at += depth - 1 if side == 0 else 0
            edge[k, side, 0:by] = scaled(k, slab[at])
            edge[k, side, by:] = scaled(k, corner[base + at])
        at = OFFSETS[2] + (0 if side == 0 else 1)
        sign = SCALES[1] if side == 0 else -SCALES[1]
        weight[side, 0:by] = slab[at] * sign - 2.0 * DIFFUSION / HALF_WIDTH
        weight[side, by:] = corner[base + at] * sign - 2.0 * DIFFUSION / HALF_WIDTH
    cells = Cells(bx, coef, edge, lambda j, x: places[j, x])
    mark_interior(cells, bx, 0, vectors)
    know_start(cells, start, low, high, corner)
    for j in range(1, STEPS + 1):
        for x in early_range(j, bx):
            cells.get(j, x)


def rest_kernel(
    start, coef, low, high, corner, beside, edge, weight, low_later, high_later, later_corner, given, vectors, to_low, to_high, following, sides, scratch
):
    del given
    bx, by = start.shape[0], low.shape[1]
    later = low_later.shape[0]
    places = own_places(bx, 0, vectors) | own_places(bx, STEPS, following) | halo_places(bx, 0, scratch, sides)
    cells = Cells(bx, coef, edge, lambda j, x: places[j, x])
    know_start(cells, start, low, high, corner)
    for j in range(1, STEPS + 1):
        for x in early_range(j, bx):
            cells.known[j, x] = lambda j=j, x=x: vectors[j - 1, x]
    cells.known[1, -1], cells.known[1, bx] = (lambda: beside[0]), (lambda: beside[1])
    for side, slab, base in ((0, low_later, 0), (1, high_later, later)):
        near, far = halo_layer(bx, 1, side == 0), halo_layer(bx, 2, side == 0)
        cells.known[1, far] = lambda slab=slab, base=base: wide_layer(slab, later_corner, 0, base)
        cells.computed[2, far] = lambda slab=slab, base=base, side=side, near=near: (
            wide_layer(slab, later_corner, 1, base) + weight[side] * cells.get(1, near)
        )
    cells.finish(0)
    for out, below, one, two in ((to_low, True, 0, 1), (to_high, False, bx - 1, bx - 2)):
        leaving = [
            cells.get(STEPS, one),
            cells.get(STEPS, two),
            cells.get(STEPS + 1, two),
            cells.tip(STEPS, two, below),
        ]
        for at, layer in enumerate(leaving):
            above, under = layer[by : by + MARGIN], layer[by + MARGIN :]
            row = lax.broadcasted_iota(jnp.int32, above.shape, 0)
            out[at, 0:by] = layer[:by]
            out[at, by:] = jnp.where(row < EDGE, above, under)


def second_cells(one, sides, coef, edge, weight, slab, side, two, scratch):
    bx = coef.shape[1]
    by = slab.shape[1] - 2 * EDGE
    places = own_places(bx, STEPS, two) | halo_places(bx, STEPS, scratch)
    cells = Cells(bx, coef, edge, lambda j, x: places[j, x])
    mark_interior(cells, bx, STEPS, two)
    for x in range(bx):
        cells.known[STEPS, x] = lambda x=x: one[STEPS - 1, x]
        cells.known[STEPS - 1, x] = lambda x=x: one[STEPS - 2, x]
    near, far = halo_layer(bx, 1, side == 0), halo_layer(bx, 2, side == 0)

    def wide(at):
        return jnp.concatenate([slab[at], slab[at, by:]], axis=0)

    cells.known[STEPS - 1, near] = lambda: sides[side]
    cells.known[STEPS, near] = lambda: wide(0)
    cells.known[STEPS, far] = lambda: wide(1)
    cells.known[STEPS + 1, far] = lambda: wide(2)
    cells.computed[STEPS + 2, far] = lambda: wide(3) + weight[side] * cells.get(STEPS + 1, near)
    return cells


def low_kernel(start, one, given, sides, coef, edge, weight, low, two, partial, scratch):
    del given
    bx, _, nz = start.shape
    by = low.shape[1] - 2 * EDGE
    cells = second_cells(one, sides, coef, edge, weight, low, 0, two, scratch)
    for j in range(1, STEPS + 1):
        reach = max([m for i, m in COMPUTED if i == j], default=0)
        for x in range(-reach, bx - j):
            cells.get(STEPS + j, x)
    totals = products(GROUPS[1], 0, bx - STEPS, by, nz, reader(start, one, two))
    for k, total in enumerate(totals):
        partial[k] = total


def high_kernel(start, one, given, sides, coef, edge, weight, high, early_gram, partial, two, gram, scratch):
    del given
    bx, _, nz = start.shape
    by = high.shape[1] - 2 * EDGE
    cells = second_cells(one, sides, coef, edge, weight, high, 1, two, scratch)
    for j in range(1, STEPS + 1):
        for x in range(bx - j):
            cells.known[STEPS + j, x] = lambda j=j, x=x: two[j - 1, x]
    for j in range(1, STEPS + 1):
        reach = max([m for i, m in COMPUTED if i == j], default=0)
        for x in range(bx - j, bx + reach):
            cells.get(STEPS + j, x)
    before = tuple(partial[k] for k in range(len(GROUPS[1])))
    rows = summed_rows(products(GROUPS[1], bx - STEPS, bx, by, nz, reader(start, one, two), before))
    sums = jnp.concatenate([early_gram[...]] + rows, axis=0)
    on = lax.broadcasted_iota(jnp.int32, sums.shape, 0) == lax.broadcasted_iota(jnp.int32, sums.shape, 1)
    line = jnp.sum(jnp.where(on, jnp.sum(sums, axis=1, keepdims=True), 0.0), axis=0, keepdims=True)
    gram[...] = jnp.broadcast_to(line, gram.shape)


def last_kernel(cell_count, gram, start, one, two, out, factor, result, sem):
    _, bx, by, nz = result.shape
    total = gram[0:8]
    for row in range(8, gram.shape[0], 8):
        total = total + gram[row : row + 8]
    for distance in (4, 2, 1):
        total = total + pltpu.roll(total, distance, 0)
    total = total * (1.0 / cell_count)
    cell = reader(start, one, two)
    entry, inverse, copies = {}, [], []
    for j in range(BASIS):
        for i in range(j + 1):
            k = PLACE[i, j]
            value = jnp.broadcast_to(total[:, k : k + 1], (8, 128))
            if (i, j) == (0, 0):
                mean_square = value * (1.0 / (LIFT * LIFT))
            for above in range(i):
                value = value - entry[above, i] * entry[above, j]
            if i == j:
                inverse.append(lax.rsqrt(value))
            entry[i, j] = value * inverse[i]
        for x in range(bx):
            for y in range(0, by, 8):
                for z in range(0, nz, 128):
                    window = (x, slice(y, y + 8), slice(z, z + 128))
                    value = cell(j, *window)
                    for i in range(j):
                        value = value - entry[i, j] * result[(i,) + window]
                    result[(j,) + window] = value * inverse[j]
        copies.append(pltpu.make_async_copy(result.at[j], out.at[j], sem.at[j]))
        copies[j].start()
    scale = lax.rsqrt(mean_square + EPSILON) * (1.0 / LIFT)
    sublane = lax.broadcasted_iota(jnp.int32, (8, 128), 0)
    lane = lax.broadcasted_iota(jnp.int32, (8, 128), 1)
    tops = []
    for base in range(0, BASIS, 8):
        packed = jnp.zeros((8, 128), jnp.float32)
        for (i, j), value in entry.items():
            if base <= i < base + 8:
                packed = jnp.where((sublane == i - base) & (lane == j), value, packed)
        tops.append(packed * scale)
    factor[...] = jnp.concatenate(tops, axis=0)[:BASIS, :BASIS]
    for copy in copies:
        copy.wait()


def shape(*dims):
    return jax.ShapeDtypeStruct(dims, jnp.float32)


def call(kernel, outs, *args, name, scratch=(), us=0.02, in_specs=None, out_specs=None, aliases=None):
    return pl.pallas_call(
        kernel,
        out_shape=outs,
        in_specs=in_specs or [VMEM] * len(args),
        out_specs=out_specs or [VMEM] * len(outs),
        scratch_shapes=scratch,
        input_output_aliases=aliases or {},
        compiler_params=pltpu.CompilerParams(vmem_limit_bytes=24 << 20),
        cost_estimate=pl.CostEstimate(flops=0, transcendentals=0, bytes_accessed=int(us * 3e6)),
        name=name,
    )(*args)


def per_device(forcing, reaction, velocity):
    bx, by, nz = forcing.shape
    devices = lax.axis_size("gx") * lax.axis_size("gy")
    cell_count = float(bx * by * nz * devices)
    wide = by + 2 * MARGIN
    inputs = tuple(pltpu.with_memory_space_constraint(v, pltpu.MemorySpace.HBM) for v in (forcing, reaction, velocity))
    vectors = shape(STEPS, bx, wide, nz)
    fields, to_low, to_high, rows = call(
        pack_kernel,
        [shape(5, bx, by, nz)] + [shape(sum(DEPTHS), by, nz)] * 2 + [shape(SWAPPED[5], 2 * EDGE, nz)],
        *inputs,
        name="pack",
        in_specs=[HBM] * 3,
        scratch=[pltpu.SemaphoreType.DMA((5,))],
    )
    low, high = swap_x(to_low, to_high)
    rows = swap_rows(rows[:, :EDGE], rows[:, EDGE:])
    to_low, to_high = call(
        inner_kernel,
        [shape(2, by, nz)] * 2,
        fields,
        rows,
        name="inner",
        scratch=[pltpu.VMEM((4, by + 2 * EDGE, nz), jnp.float32)],
    )
    low_later, high_later = swap_x(to_low, to_high)
    rows = swap_y(fields.reshape(5 * bx, by, nz))
    start, coef, one = call(
        prepare_kernel, [shape(bx, wide, nz), shape(4, bx, wide, nz), vectors], fields, rows, name="prepare"
    )
    corner = swap_y(jnp.concatenate([low, high]))
    one, beside, edge, weight = call(
        first_kernel,
        [vectors, shape(2, wide, nz), shape(4, 2, wide, nz), shape(2, wide, nz)],
        start,
        coef,
        low,
        high,
        corner,
        one,
        name="first",
        aliases={5: 0},
    )
    one, to_low, to_high, two, sides = call(
        rest_kernel,
        [vectors, shape(4, by + 2 * EDGE, nz), shape(4, by + 2 * EDGE, nz), vectors, shape(2, wide, nz)],
        start,
        coef,
        low,
        high,
        corner,
        beside,
        edge,
        weight,
        low_later,
        high_later,
        swap_y(jnp.concatenate([low_later, high_later])),
        one,
        name="rest",
        scratch=[pltpu.VMEM((2 * len(COMPUTED), wide, nz), jnp.float32)],
        aliases={11: 0},
    )
    low, high = swap_x(to_low, to_high)
    two, early_gram = call(
        lambda *refs: second_interior_kernel(by, *refs),
        [vectors, shape(STARTS[1], 128)],
        start,
        one,
        coef,
        two,
        name="second_interior",
        aliases={3: 0},
    )
    halo = [pltpu.VMEM((2 * len(COMPUTED), wide, nz), jnp.float32)]
    two, partial = call(
        low_kernel,
        [vectors, shape(len(GROUPS[1]), 8, 128)],
        start,
        one,
        two,
        sides,
        coef,
        edge,
        weight,
        low,
        name="low",
        scratch=halo,
        aliases={2: 0},
    )
    two, gram = call(
        high_kernel,
        [vectors, shape(devices, 128)],
        start,
        one,
        two,
        sides,
        coef,
        edge,
        weight,
        high,
        early_gram,
        partial,
        name="high",
        scratch=halo,
        aliases={2: 0},
    )
    gram = lax.all_to_all(gram, AXES, 0, 0, tiled=True)
    return call(
        lambda *refs: last_kernel(cell_count, *refs),
        [shape(BASIS, bx, by, nz), shape(BASIS, BASIS)],
        gram,
        start,
        one,
        two,
        name="last",
        out_specs=[pl.BlockSpec(memory_space=pl.ANY), VMEM],
        scratch=[
            pltpu.VMEM((BASIS, bx, by, nz), jnp.float32),
            pltpu.SemaphoreType.DMA((BASIS,)),
        ],
    )


def solution(mesh):
    in_specs = (P("gx", "gy", None), P("gx", "gy", None), P(None, "gx", "gy", None))
    out_specs = (P(None, "gx", "gy", None), P())
    return jax.shard_map(per_device, mesh=mesh, in_specs=in_specs, out_specs=out_specs, check_vma=False)
```

```python
import jax
import jax.numpy as jnp
from jax import lax
from jax.experimental import pallas as pl
from jax.experimental.pallas import tpu as pltpu
from jax.sharding import PartitionSpec as P

BASIS = 9
STEPS = 4
MARGIN = 8
EDGE = 4

DIFFUSION = 0.03
CENTRE_SHIFT = 1.18
HALF_WIDTH = 0.95
EPSILON = 1e-06
LIFT = 1024.0
SCALES = (2.0 / HALF_WIDTH, 1.0 / HALF_WIDTH, 1.0 / HALF_WIDTH, 1.0 / HALF_WIDTH)
SHIFTS = (2.0 * (6.0 * DIFFUSION - CENTRE_SHIFT) / HALF_WIDTH, 0.0, 0.0, 0.0)
AXES = ("gx", "gy")
VMEM = pl.BlockSpec(memory_space=pltpu.VMEM)
HBM = pl.BlockSpec(memory_space=pltpu.MemorySpace.HBM)


COMPUTED = ((1, 1), (2, 1), (2, 2), (3, 1))
GIVEN = ((0, 1), (0, 2), (1, 2))
TIP = (2, 2)
DEPTHS = (2, 1, 2, 1, 1)
OFFSETS = (0, 2, 3, 5, 6)


def pairs_of(low, high):
    return [(i, j) for j in range(low, high) for i in range(j + 1)]


GROUPS = (pairs_of(0, STEPS + 1), pairs_of(STEPS + 1, BASIS))
STARTS = (0, -(-len(GROUPS[0]) // 8) * 8)
GRAM_ROWS = STARTS[1] - (-len(GROUPS[1]) // 8) * 8
PLACE = {pair: start + k for start, group in zip(STARTS, GROUPS) for k, pair in enumerate(group)}


def ring(axis, step):
    count = lax.axis_size(axis)
    return [(i, (i + step) % count) for i in range(count)]


def swap_x(to_low, to_high):
    return lax.ppermute(to_high, "gx", ring("gx", 1)), lax.ppermute(to_low, "gx", ring("gx", -1))


def swap_y(block):
    rows = block.shape[1]
    return swap_rows(block[:, :MARGIN], block[:, rows - MARGIN :])


def swap_rows(low, high):
    if lax.axis_size("gy") == 2:
        return lax.ppermute(jnp.concatenate([low, high], axis=1), "gy", ring("gy", 1))
    above = lax.ppermute(low, "gy", ring("gy", -1))
    below = lax.ppermute(high, "gy", ring("gy", 1))
    return jnp.concatenate([above, below], axis=1)


def doubled(centre, east, west, coef):
    rows, lanes = centre.shape
    kept = east.shape[0]
    north = pltpu.roll(centre, rows - 1, 0)[:kept]
    south = pltpu.roll(centre, 1, 0)[:kept]
    centre = centre[:kept]
    upper = pltpu.roll(centre, lanes - 1, 1)
    lower = pltpu.roll(centre, 1, 1)
    around = (east + west) + (north + south) + (upper + lower)
    slopes = coef[1] * (east - west) + coef[2] * (north - south) + coef[3] * (upper - lower)
    return coef[0] * centre + slopes - (2.0 * DIFFUSION / HALF_WIDTH) * around


def scaled(k, value):
    return value * SCALES[k] + SHIFTS[k]


def products(pairs, first, last, by, nz, cell, totals=None):
    needed = sorted({i for pair in pairs for i in pair})
    tiles = by // 8

    def add(at, totals):
        x, y = first + at // tiles, pl.multiple_of(at % tiles * 8, 8)
        for z in range(0, nz, 128):
            cells = {i: cell(i, x, pl.ds(y, 8), pl.ds(z, 128)) for i in needed}
            totals = tuple(t + cells[i] * cells[j] for t, (i, j) in zip(totals, pairs))
        return totals

    if totals is None:
        totals = tuple(jnp.zeros((8, 128), jnp.float32) for _ in pairs)
    return lax.fori_loop(0, (last - first) * tiles, add, totals, unroll=2)


def summed_rows(totals):
    sublane = lax.broadcasted_iota(jnp.int32, (8, 128), 0)
    rows = []
    for base in range(0, len(totals), 8):
        packed = jnp.zeros((8, 128), jnp.float32)
        for k, total in enumerate(totals[base : base + 8]):
            for distance in (4, 2, 1):
                total = total + pltpu.roll(total, distance, 0)
            packed = jnp.where(sublane == k, total, packed)
        rows.append(packed)
    return rows


def reader(start, one, two=None):
    def cell(i, x, y, z):
        if i == 0:
            return start[x, y, z]
        if i <= STEPS:
            return one[i - 1, x, y, z]
        return two[i - 1 - STEPS, x, y, z]

    return cell


def second_interior_kernel(by, start, one, coef, given, vectors, gram):
    del given
    bx, _, nz = start.shape
    places = own_places(bx, STEPS, vectors)
    cells = Cells(bx, coef, None, lambda j, x: places[j, x])
    for x in (1, 2, bx - 3, bx - 2):
        cells.known[STEPS + 1, x] = lambda x=x: vectors[0, x]
    for x in range(bx):
        cells.known[STEPS, x] = lambda x=x: one[STEPS - 1, x]
        cells.known[STEPS - 1, x] = lambda x=x: one[STEPS - 2, x]
    cells.interior(STEPS)
    for k, row in enumerate(summed_rows(products(GROUPS[0], 0, bx, by, nz, reader(start, one)))):
        gram[8 * k : 8 * k + 8] = row


def fields_of(f, r, vel):
    return f, r, vel.at[0], vel.at[1], vel.at[2]


REACH = ((0, 3),) + ((1, 3),) * 4
SWAPPED = tuple(sum(2 * (high - low) for low, high in REACH[:k]) for k in range(6))


def edge_rows(block):
    rows = block.shape[-2]
    low, high = block[..., : 2 * EDGE, :], block[..., rows - 2 * EDGE :, :]
    row = lax.broadcasted_iota(jnp.int32, low.shape, low.ndim - 2)
    return jnp.where(row < EDGE, low, high)


def pack_kernel(f, r, vel, fields, to_low, to_high, rows, sem):
    bx = f.shape[0]
    copies = [pltpu.make_async_copy(field, fields.at[k], sem.at[k]) for k, field in enumerate(fields_of(f, r, vel))]
    for copy in copies:
        copy.start()
    for k in range(5):
        copies[k].wait()
        depth, at = DEPTHS[k], OFFSETS[k]
        to_low[at : at + depth] = fields[k, 0:depth]
        to_high[at : at + depth] = fields[k, bx - depth : bx]
        (low, high), at = REACH[k], SWAPPED[k]
        rows[at : at + high - low] = edge_rows(fields[k, low:high])
        rows[at + high - low : at + 2 * (high - low)] = edge_rows(fields[k, bx - high : bx - low])


def inner_kernel(fields, rows, to_low, to_high, scratch):
    _, bx, by, _ = fields.shape

    def layer(k, x):
        (low, high), at = REACH[k], SWAPPED[k]
        at += x - low if x < high else high - low + x - (bx - high)
        return jnp.concatenate([fields[k, x], rows[at]], axis=0)

    class Coefficients:
        shape = (4, bx)

        def __getitem__(self, at):
            return scaled(at[0], layer(at[0] + 1, at[1]))

    cells = Cells(bx, Coefficients(), None, lambda j, x: (scratch, ({1: 0, 2: 1, bx - 3: 2, bx - 2: 3}[x],)))
    for x in (0, 1, 2, 3, bx - 4, bx - 3, bx - 2, bx - 1):
        if 3 <= x < bx - 3:
            cells.known[0, x] = lambda x=x: jnp.concatenate([fields[0, x], jnp.zeros_like(rows[0])], axis=0) * LIFT
        else:
            cells.known[0, x] = lambda x=x: layer(0, x) * LIFT
    to_low[0] = cells.get(1, 1)[:by]
    to_high[0] = cells.get(1, bx - 2)[:by]
    to_low[1] = cells.tip(0, 1, True)[:by]
    to_high[1] = cells.tip(0, bx - 2, False)[:by]


class Cells:
    def __init__(self, bx, coef, edge, place):
        self.bx, self.coef, self.edge, self.place = bx, coef, edge, place
        self.known, self.computed = {}, {}

    def coefficients(self, x):
        if 0 <= x < self.bx:
            return [self.coef[k, x] for k in range(4)]
        return [self.edge[k, 0 if x < 0 else 1] for k in range(4)]

    def get(self, j, x):
        if (j, x) not in self.known:
            ref, at = self.place(j, x)
            rows = ref.shape[-2] - (2 * MARGIN if j == BASIS - 1 else 0)
            if (j, x) in self.computed:
                new = self.computed[j, x]()
            else:
                east, west = self.get(j - 1, x + 1)[:rows], self.get(j - 1, x - 1)[:rows]
                new = doubled(self.get(j - 1, x), east, west, [c[:rows] for c in self.coefficients(x)])
                new = new * 0.5 if j == 1 else new - self.get(j - 2, x)[:rows]
            at = at + (slice(0, rows),)
            ref[at] = new
            self.known[j, x] = lambda: ref[at]
        return self.known[j, x]()

    def tip(self, base, x, below):
        j = base + TIP[0]
        centre, beyond = self.get(j - 1, x), self.get(j - 1, x + 1 if below else x - 1)
        nothing = jnp.zeros_like(centre)
        pair = (beyond, nothing) if below else (nothing, beyond)
        return doubled(centre, *pair, self.coefficients(x)) - self.get(j - 2, x)

    def interior(self, base):
        for j in range(1, STEPS):
            for x in range(j, self.bx - j):
                self.get(base + j, x)

    def finish(self, base):
        for j in range(1, STEPS + 1):
            reach = max([m for i, m in COMPUTED if i == j], default=0)
            for x in range(-reach, self.bx + reach):
                self.get(base + j, x)


def halo_layer(bx, m, low_side):
    return -m if low_side else bx - 1 + m


def own_places(bx, base, ref):
    return {(base + j, x): (ref, (j - 1, x)) for j in range(1, STEPS + 1) for x in range(bx)}


def mark_interior(cells, bx, base, ref):
    for j in range(1, STEPS):
        for x in range(j, bx - j):
            cells.known[base + j, x] = lambda j=j, x=x: ref[j - 1, x]


def halo_places(bx, base, scratch, sides=None):
    places, slot = {}, 0
    for j, m in COMPUTED:
        for low_side in (True, False):
            at = (base + j, halo_layer(bx, m, low_side))
            if sides is not None and (j, m) == (STEPS - 1, 1):
                places[at] = (sides, (0 if low_side else 1,))
            else:
                places[at] = (scratch, (slot,))
                slot += 1
    return places


def prepare_kernel(fields, rows, start, coef, vectors):
    _, bx, by, _ = fields.shape
    start[:, 0:by] = fields[0] * LIFT
    start[:, by:] = rows[0:bx] * LIFT
    for k in range(4):
        coef[k, :, 0:by] = scaled(k, fields[k + 1])
        coef[k, :, by:] = scaled(k, rows[bx * (k + 1) : bx * (k + 2)])
    places = own_places(bx, 0, vectors)
    cells = Cells(bx, coef, None, lambda j, x: places[j, x])
    for x in range(bx):
        cells.known[0, x] = lambda x=x: start[x]
    cells.interior(0)


def wide_layer(slab, corner, at, base):
    return jnp.concatenate([slab[at], corner[base + at]], axis=0)


def know_start(cells, start, low, high, corner):
    bx, size = start.shape[0], low.shape[0]
    for x in range(bx):
        cells.known[0, x] = lambda x=x: start[x]
    for side, slab, base in ((0, low, 0), (1, high, size)):
        for m in (1, 2):
            at = DEPTHS[0] - m if side == 0 else m - 1
            cells.known[0, halo_layer(bx, m, side == 0)] = lambda slab=slab, base=base, at=at: (
                wide_layer(slab, corner, at, base) * LIFT
            )


def early_range(j, bx):
    return range(j - 2, bx - (j - 2))


def first_kernel(start, coef, low, high, corner, given, vectors, beside, edge, weight):
    del given
    bx, by = start.shape[0], low.shape[1]
    size = low.shape[0]
    places = own_places(bx, 0, vectors)
    places[1, -1], places[1, bx] = (beside, (0,)), (beside, (1,))
    for side, slab, base in ((0, low, 0), (1, high, size)):
        for k in range(4):
            depth, at = DEPTHS[k + 1], OFFSETS[k + 1]
            at += depth - 1 if side == 0 else 0
            edge[k, side, 0:by] = scaled(k, slab[at])
            edge[k, side, by:] = scaled(k, corner[base + at])
        at = OFFSETS[2] + (0 if side == 0 else 1)
        sign = SCALES[1] if side == 0 else -SCALES[1]
        weight[side, 0:by] = slab[at] * sign - 2.0 * DIFFUSION / HALF_WIDTH
        weight[side, by:] = corner[base + at] * sign - 2.0 * DIFFUSION / HALF_WIDTH
    cells = Cells(bx, coef, edge, lambda j, x: places[j, x])
    mark_interior(cells, bx, 0, vectors)
    know_start(cells, start, low, high, corner)
    for j in range(1, STEPS + 1):
        for x in early_range(j, bx):
            cells.get(j, x)


def rest_kernel(
    start, coef, low, high, corner, beside, edge, weight, low_later, high_later, later_corner, given, vectors, to_low, to_high, following, sides, scratch
):
    del given
    bx, by = start.shape[0], low.shape[1]
    later = low_later.shape[0]
    places = own_places(bx, 0, vectors) | own_places(bx, STEPS, following) | halo_places(bx, 0, scratch, sides)
    cells = Cells(bx, coef, edge, lambda j, x: places[j, x])
    know_start(cells, start, low, high, corner)
    for j in range(1, STEPS + 1):
        for x in early_range(j, bx):
            cells.known[j, x] = lambda j=j, x=x: vectors[j - 1, x]
    cells.known[1, -1], cells.known[1, bx] = (lambda: beside[0]), (lambda: beside[1])
    for side, slab, base in ((0, low_later, 0), (1, high_later, later)):
        near, far = halo_layer(bx, 1, side == 0), halo_layer(bx, 2, side == 0)
        cells.known[1, far] = lambda slab=slab, base=base: wide_layer(slab, later_corner, 0, base)
        cells.computed[2, far] = lambda slab=slab, base=base, side=side, near=near: (
            wide_layer(slab, later_corner, 1, base) + weight[side] * cells.get(1, near)
        )
    cells.finish(0)
    for out, below, one, two in ((to_low, True, 0, 1), (to_high, False, bx - 1, bx - 2)):
        leaving = [
            cells.get(STEPS, one),
            cells.get(STEPS, two),
            cells.get(STEPS + 1, two),
            cells.tip(STEPS, two, below),
        ]
        for at, layer in enumerate(leaving):
            out[at * by : (at + 1) * by] = layer[:by]
        tiles = [(layer[by : by + MARGIN], layer[by + MARGIN :]) for layer in leaving[:3]]
        row = lax.broadcasted_iota(jnp.int32, tiles[0][0].shape, 0)
        out[4 * by : 4 * by + 8] = jnp.where(row < EDGE, *tiles[0])
        middle = jnp.where(row < EDGE, pltpu.roll(tiles[2][0], 2, 0), pltpu.roll(tiles[2][1], 6, 0))
        outer = jnp.where(row < EDGE, *tiles[1])
        out[4 * by + 8 :] = jnp.where((row == 2) | (row == 5), middle, outer)


def second_cells(one, sides, coef, edge, weight, slab, side, two, scratch):
    bx = coef.shape[1]
    by = slab.shape[0] // 4 - EDGE
    places = own_places(bx, STEPS, two) | halo_places(bx, STEPS, scratch)
    cells = Cells(bx, coef, edge, lambda j, x: places[j, x])
    mark_interior(cells, bx, STEPS, two)
    for x in range(bx):
        cells.known[STEPS, x] = lambda x=x: one[STEPS - 1, x]
        cells.known[STEPS - 1, x] = lambda x=x: one[STEPS - 2, x]
    near, far = halo_layer(bx, 1, side == 0), halo_layer(bx, 2, side == 0)

    def wide(at):
        first, second = slab[4 * by : 4 * by + 8], slab[4 * by + 8 :]
        above, below = ((first, first), (second, second), (pltpu.roll(second, 6, 0), pltpu.roll(second, 2, 0)))[min(at, 2)]
        return jnp.concatenate([slab[at * by : (at + 1) * by], above, below], axis=0)

    cells.known[STEPS - 1, near] = lambda: sides[side]
    cells.known[STEPS, near] = lambda: wide(0)
    cells.known[STEPS, far] = lambda: wide(1)
    cells.known[STEPS + 1, far] = lambda: wide(2)
    cells.computed[STEPS + 2, far] = lambda: wide(3) + weight[side] * cells.get(STEPS + 1, near)
    return cells


def reach_of(j):
    return max([m for i, m in COMPUTED if i == j], default=0)


def sooner_kernel(start, one, given, sides, coef, edge, weight, high, two, partial, scratch):
    del given
    bx, _, nz = start.shape
    by = high.shape[0] // 4 - EDGE
    cells = second_cells(one, sides, coef, edge, weight, high, 1, two, scratch)
    for j in range(1, STEPS + 1):
        for x in range(j, bx + reach_of(j)):
            cells.get(STEPS + j, x)
    totals = products(GROUPS[1], STEPS, bx, by, nz, reader(start, one, two))
    for k, total in enumerate(totals):
        partial[k] = total


def later_kernel(start, one, given, sides, coef, edge, weight, low, early_gram, partial, two, gram, scratch):
    del given
    bx, _, nz = start.shape
    by = low.shape[0] // 4 - EDGE
    cells = second_cells(one, sides, coef, edge, weight, low, 0, two, scratch)
    for j in range(1, STEPS + 1):
        for x in range(j, bx):
            cells.known[STEPS + j, x] = lambda j=j, x=x: two[j - 1, x]
    for j in range(1, STEPS + 1):
        for x in range(-reach_of(j), j):
            cells.get(STEPS + j, x)
    before = tuple(partial[k] for k in range(len(GROUPS[1])))
    rows = summed_rows(products(GROUPS[1], 0, STEPS, by, nz, reader(start, one, two), before))
    sums = jnp.concatenate([early_gram[...]] + rows, axis=0)
    on = lax.broadcasted_iota(jnp.int32, sums.shape, 0) == lax.broadcasted_iota(jnp.int32, sums.shape, 1)
    line = jnp.sum(jnp.where(on, jnp.sum(sums, axis=1, keepdims=True), 0.0), axis=0, keepdims=True)
    gram[...] = jnp.broadcast_to(line, gram.shape)


def last_kernel(cell_count, gram, start, one, two, out, factor, result, sem):
    _, bx, by, nz = result.shape
    total = gram[0:8]
    for row in range(8, gram.shape[0], 8):
        total = total + gram[row : row + 8]
    for distance in (4, 2, 1):
        total = total + pltpu.roll(total, distance, 0)
    total = total * (1.0 / cell_count)
    cell = reader(start, one, two)
    entry, inverse, copies = {}, [], []
    for j in range(BASIS):
        for i in range(j + 1):
            k = PLACE[i, j]
            value = jnp.broadcast_to(total[:, k : k + 1], (8, 128))
            if (i, j) == (0, 0):
                mean_square = value * (1.0 / (LIFT * LIFT))
            for above in range(i):
                value = value - entry[above, i] * entry[above, j]
            if i == j:
                inverse.append(lax.rsqrt(value))
            entry[i, j] = value * inverse[i]
        for x in range(bx):
            for y in range(0, by, 8):
                for z in range(0, nz, 128):
                    window = (x, slice(y, y + 8), slice(z, z + 128))
                    value = cell(j, *window)
                    for i in range(j):
                        value = value - entry[i, j] * result[(i,) + window]
                    result[(j,) + window] = value * inverse[j]
        copies.append(pltpu.make_async_copy(result.at[j], out.at[j], sem.at[j]))
        copies[j].start()
    scale = lax.rsqrt(mean_square + EPSILON) * (1.0 / LIFT)
    sublane = lax.broadcasted_iota(jnp.int32, (8, 128), 0)
    lane = lax.broadcasted_iota(jnp.int32, (8, 128), 1)
    tops = []
    for base in range(0, BASIS, 8):
        packed = jnp.zeros((8, 128), jnp.float32)
        for (i, j), value in entry.items():
            if base <= i < base + 8:
                packed = jnp.where((sublane == i - base) & (lane == j), value, packed)
        tops.append(packed * scale)
    factor[...] = jnp.concatenate(tops, axis=0)[:BASIS, :BASIS]
    for copy in copies:
        copy.wait()


def shape(*dims):
    return jax.ShapeDtypeStruct(dims, jnp.float32)


def call(kernel, outs, *args, name, scratch=(), us=0.02, in_specs=None, out_specs=None, aliases=None):
    return pl.pallas_call(
        kernel,
        out_shape=outs,
        in_specs=in_specs or [VMEM] * len(args),
        out_specs=out_specs or [VMEM] * len(outs),
        scratch_shapes=scratch,
        input_output_aliases=aliases or {},
        compiler_params=pltpu.CompilerParams(vmem_limit_bytes=24 << 20),
        cost_estimate=pl.CostEstimate(flops=0, transcendentals=0, bytes_accessed=int(us * 3e6)),
        name=name,
    )(*args)


def per_device(forcing, reaction, velocity):
    bx, by, nz = forcing.shape
    devices = lax.axis_size("gx") * lax.axis_size("gy")
    cell_count = float(bx * by * nz * devices)
    wide = by + 2 * MARGIN
    inputs = tuple(pltpu.with_memory_space_constraint(v, pltpu.MemorySpace.HBM) for v in (forcing, reaction, velocity))
    vectors = shape(STEPS, bx, wide, nz)
    fields, to_low, to_high, rows = call(
        pack_kernel,
        [shape(5, bx, by, nz)] + [shape(sum(DEPTHS), by, nz)] * 2 + [shape(SWAPPED[5], 2 * EDGE, nz)],
        *inputs,
        name="pack",
        in_specs=[HBM] * 3,
        scratch=[pltpu.SemaphoreType.DMA((5,))],
    )
    low, high = swap_x(to_low, to_high)
    rows = swap_rows(rows[:, :EDGE], rows[:, EDGE:])
    to_low, to_high = call(
        inner_kernel,
        [shape(2, by, nz)] * 2,
        fields,
        rows,
        name="inner",
        scratch=[pltpu.VMEM((4, by + 2 * EDGE, nz), jnp.float32)],
    )
    low_later, high_later = swap_x(to_low, to_high)
    rows = swap_y(fields.reshape(5 * bx, by, nz))
    start, coef, one = call(
        prepare_kernel, [shape(bx, wide, nz), shape(4, bx, wide, nz), vectors], fields, rows, name="prepare"
    )
    corner = swap_y(jnp.concatenate([low, high]))
    one, beside, edge, weight = call(
        first_kernel,
        [vectors, shape(2, wide, nz), shape(4, 2, wide, nz), shape(2, wide, nz)],
        start,
        coef,
        low,
        high,
        corner,
        one,
        name="first",
        aliases={5: 0},
    )
    one, to_low, to_high, two, sides = call(
        rest_kernel,
        [vectors, shape(4 * by + 16, nz), shape(4 * by + 16, nz), vectors, shape(2, wide, nz)],
        start,
        coef,
        low,
        high,
        corner,
        beside,
        edge,
        weight,
        low_later,
        high_later,
        swap_y(jnp.concatenate([low_later, high_later])),
        one,
        name="rest",
        scratch=[pltpu.VMEM((2 * len(COMPUTED), wide, nz), jnp.float32)],
        aliases={11: 0},
    )
    low, high = swap_x(to_low, to_high)
    two, early_gram = call(
        lambda *refs: second_interior_kernel(by, *refs),
        [vectors, shape(STARTS[1], 128)],
        start,
        one,
        coef,
        two,
        name="second_interior",
        aliases={3: 0},
    )
    halo = [pltpu.VMEM((2 * len(COMPUTED), wide, nz), jnp.float32)]
    two, partial = call(
        sooner_kernel,
        [vectors, shape(len(GROUPS[1]), 8, 128)],
        start,
        one,
        two,
        sides,
        coef,
        edge,
        weight,
        high,
        name="sooner",
        scratch=halo,
        aliases={2: 0},
    )
    two, gram = call(
        later_kernel,
        [vectors, shape(devices, 128)],
        start,
        one,
        two,
        sides,
        coef,
        edge,
        weight,
        low,
        early_gram,
        partial,
        name="later",
        scratch=halo,
        aliases={2: 0},
    )
    gram = lax.all_to_all(gram, AXES, 0, 0, tiled=True)
    return call(
        lambda *refs: last_kernel(cell_count, *refs),
        [shape(BASIS, bx, by, nz), shape(BASIS, BASIS)],
        gram,
        start,
        one,
        two,
        name="last",
        out_specs=[pl.BlockSpec(memory_space=pl.ANY), VMEM],
        scratch=[
            pltpu.VMEM((BASIS, bx, by, nz), jnp.float32),
            pltpu.SemaphoreType.DMA((BASIS,)),
        ],
    )


def solution(mesh):
    in_specs = (P("gx", "gy", None), P("gx", "gy", None), P(None, "gx", "gy", None))
    out_specs = (P(None, "gx", "gy", None), P())
    return jax.shard_map(per_device, mesh=mesh, in_specs=in_specs, out_specs=out_specs, check_vma=False)
```

```python
import jax
import jax.numpy as jnp
from jax import lax
from jax.experimental import pallas as pl
from jax.experimental.pallas import tpu as pltpu
from jax.sharding import PartitionSpec as P

BASIS = 9
STEPS = 4
MARGIN = 8
EDGE = 4

DIFFUSION = 0.03
CENTRE_SHIFT = 1.18
HALF_WIDTH = 0.95
EPSILON = 1e-06
LIFT = 1024.0
SCALES = (2.0 / HALF_WIDTH, 1.0 / HALF_WIDTH, 1.0 / HALF_WIDTH, 1.0 / HALF_WIDTH)
SHIFTS = (2.0 * (6.0 * DIFFUSION - CENTRE_SHIFT) / HALF_WIDTH, 0.0, 0.0, 0.0)
AXES = ("gx", "gy")
VMEM = pl.BlockSpec(memory_space=pltpu.VMEM)
HBM = pl.BlockSpec(memory_space=pltpu.MemorySpace.HBM)


COMPUTED = ((1, 1), (2, 1), (2, 2), (3, 1))
GIVEN = ((0, 1), (0, 2), (1, 2))
TIP = (2, 2)
DEPTHS = (2, 1, 2, 1, 1)
OFFSETS = (0, 2, 3, 5, 6)


def pairs_of(low, high):
    return [(i, j) for j in range(low, high) for i in range(j + 1)]


GROUPS = (pairs_of(0, STEPS + 1), pairs_of(STEPS + 1, BASIS))
STARTS = (0, -(-len(GROUPS[0]) // 8) * 8)
GRAM_ROWS = STARTS[1] - (-len(GROUPS[1]) // 8) * 8
PLACE = {pair: start + k for start, group in zip(STARTS, GROUPS) for k, pair in enumerate(group)}


def ring(axis, step):
    count = lax.axis_size(axis)
    return [(i, (i + step) % count) for i in range(count)]


def swap_x(to_low, to_high):
    return lax.ppermute(to_high, "gx", ring("gx", 1)), lax.ppermute(to_low, "gx", ring("gx", -1))


def swap_y(block):
    rows = block.shape[1]
    return swap_rows(block[:, :MARGIN], block[:, rows - MARGIN :])


def swap_rows(low, high):
    if lax.axis_size("gy") == 2:
        return lax.ppermute(jnp.concatenate([low, high], axis=1), "gy", ring("gy", 1))
    above = lax.ppermute(low, "gy", ring("gy", -1))
    below = lax.ppermute(high, "gy", ring("gy", 1))
    return jnp.concatenate([above, below], axis=1)


def doubled(centre, east, west, coef):
    rows, lanes = centre.shape
    kept = east.shape[0]
    north = pltpu.roll(centre, rows - 1, 0)[:kept]
    south = pltpu.roll(centre, 1, 0)[:kept]
    centre = centre[:kept]
    upper = pltpu.roll(centre, lanes - 1, 1)
    lower = pltpu.roll(centre, 1, 1)
    around = (east + west) + (north + south) + (upper + lower)
    slopes = coef[1] * (east - west) + coef[2] * (north - south) + coef[3] * (upper - lower)
    return coef[0] * centre + slopes - (2.0 * DIFFUSION / HALF_WIDTH) * around


def scaled(k, value):
    return value * SCALES[k] + SHIFTS[k]


def products(pairs, first, last, by, nz, cell, totals=None):
    needed = sorted({i for pair in pairs for i in pair})
    tiles = by // 8

    def add(at, totals):
        x, y = first + at // tiles, pl.multiple_of(at % tiles * 8, 8)
        for z in range(0, nz, 128):
            cells = {i: cell(i, x, pl.ds(y, 8), pl.ds(z, 128)) for i in needed}
            totals = tuple(t + cells[i] * cells[j] for t, (i, j) in zip(totals, pairs))
        return totals

    if totals is None:
        totals = tuple(jnp.zeros((8, 128), jnp.float32) for _ in pairs)
    return lax.fori_loop(0, (last - first) * tiles, add, totals, unroll=True)


def summed_rows(totals):
    sublane = lax.broadcasted_iota(jnp.int32, (8, 128), 0)
    rows = []
    for base in range(0, len(totals), 8):
        packed = jnp.zeros((8, 128), jnp.float32)
        for k, total in enumerate(totals[base : base + 8]):
            for distance in (4, 2, 1):
                total = total + pltpu.roll(total, distance, 0)
            packed = jnp.where(sublane == k, total, packed)
        rows.append(packed)
    return rows


def reader(start, one, two=None):
    def cell(i, x, y, z):
        if i == 0:
            return start[x, y, z]
        if i <= STEPS:
            return one[i - 1, x, y, z]
        return two[i - 1 - STEPS, x, y, z]

    return cell


def second_interior_kernel(by, start, one, coef, given, vectors, gram):
    del given
    bx, _, nz = start.shape
    places = own_places(bx, STEPS, vectors)
    cells = Cells(bx, coef, None, lambda j, x: places[j, x])
    for x in (1, 2, bx - 3, bx - 2):
        cells.known[STEPS + 1, x] = lambda x=x: vectors[0, x]
    for x in range(bx):
        cells.known[STEPS, x] = lambda x=x: one[STEPS - 1, x]
        cells.known[STEPS - 1, x] = lambda x=x: one[STEPS - 2, x]
    cells.interior(STEPS)
    for k, row in enumerate(summed_rows(products(GROUPS[0], 0, bx, by, nz, reader(start, one)))):
        gram[8 * k : 8 * k + 8] = row


def fields_of(f, r, vel):
    return f, r, vel.at[0], vel.at[1], vel.at[2]


REACH = ((0, 3),) + ((1, 3),) * 4
SWAPPED = tuple(sum(2 * (high - low) for low, high in REACH[:k]) for k in range(6))


def edge_rows(block):
    rows = block.shape[-2]
    low, high = block[..., : 2 * EDGE, :], block[..., rows - 2 * EDGE :, :]
    row = lax.broadcasted_iota(jnp.int32, low.shape, low.ndim - 2)
    return jnp.where(row < EDGE, low, high)


def pack_kernel(f, r, vel, fields, to_low, to_high, rows, sem):
    bx = f.shape[0]
    copies = [pltpu.make_async_copy(field, fields.at[k], sem.at[k]) for k, field in enumerate(fields_of(f, r, vel))]
    for copy in copies:
        copy.start()
    for k in range(5):
        copies[k].wait()
        depth, at = DEPTHS[k], OFFSETS[k]
        to_low[at : at + depth] = fields[k, 0:depth]
        to_high[at : at + depth] = fields[k, bx - depth : bx]
        (low, high), at = REACH[k], SWAPPED[k]
        rows[at : at + high - low] = edge_rows(fields[k, low:high])
        rows[at + high - low : at + 2 * (high - low)] = edge_rows(fields[k, bx - high : bx - low])


def inner_kernel(fields, rows, to_low, to_high, scratch):
    _, bx, by, _ = fields.shape

    def layer(k, x):
        (low, high), at = REACH[k], SWAPPED[k]
        at += x - low if x < high else high - low + x - (bx - high)
        return jnp.concatenate([fields[k, x], rows[at]], axis=0)

    class Coefficients:
        shape = (4, bx)

        def __getitem__(self, at):
            return scaled(at[0], layer(at[0] + 1, at[1]))

    cells = Cells(bx, Coefficients(), None, lambda j, x: (scratch, ({1: 0, 2: 1, bx - 3: 2, bx - 2: 3}[x],)))
    for x in (0, 1, 2, 3, bx - 4, bx - 3, bx - 2, bx - 1):
        if 3 <= x < bx - 3:
            cells.known[0, x] = lambda x=x: jnp.concatenate([fields[0, x], jnp.zeros_like(rows[0])], axis=0) * LIFT
        else:
            cells.known[0, x] = lambda x=x: layer(0, x) * LIFT
    to_low[0] = cells.get(1, 1)[:by]
    to_high[0] = cells.get(1, bx - 2)[:by]
    to_low[1] = cells.tip(0, 1, True)[:by]
    to_high[1] = cells.tip(0, bx - 2, False)[:by]


class Cells:
    def __init__(self, bx, coef, edge, place):
        self.bx, self.coef, self.edge, self.place = bx, coef, edge, place
        self.known, self.computed = {}, {}

    def coefficients(self, x):
        if 0 <= x < self.bx:
            return [self.coef[k, x] for k in range(4)]
        return [self.edge[k, 0 if x < 0 else 1] for k in range(4)]

    def get(self, j, x):
        if (j, x) not in self.known:
            ref, at = self.place(j, x)
            rows = ref.shape[-2] - (2 * MARGIN if j == BASIS - 1 else 0)
            if (j, x) in self.computed:
                new = self.computed[j, x]()
            else:
                east, west = self.get(j - 1, x + 1)[:rows], self.get(j - 1, x - 1)[:rows]
                new = doubled(self.get(j - 1, x), east, west, [c[:rows] for c in self.coefficients(x)])
                new = new * 0.5 if j == 1 else new - self.get(j - 2, x)[:rows]
            at = at + (slice(0, rows),)
            ref[at] = new
            self.known[j, x] = lambda: ref[at]
        return self.known[j, x]()

    def tip(self, base, x, below):
        j = base + TIP[0]
        centre, beyond = self.get(j - 1, x), self.get(j - 1, x + 1 if below else x - 1)
        nothing = jnp.zeros_like(centre)
        pair = (beyond, nothing) if below else (nothing, beyond)
        return doubled(centre, *pair, self.coefficients(x)) - self.get(j - 2, x)

    def interior(self, base):
        for j in range(1, STEPS):
            for x in range(j, self.bx - j):
                self.get(base + j, x)

    def finish(self, base):
        for j in range(1, STEPS + 1):
            reach = max([m for i, m in COMPUTED if i == j], default=0)
            for x in range(-reach, self.bx + reach):
                self.get(base + j, x)


def halo_layer(bx, m, low_side):
    return -m if low_side else bx - 1 + m


def own_places(bx, base, ref):
    return {(base + j, x): (ref, (j - 1, x)) for j in range(1, STEPS + 1) for x in range(bx)}


def mark_interior(cells, bx, base, ref):
    for j in range(1, STEPS):
        for x in range(j, bx - j):
            cells.known[base + j, x] = lambda j=j, x=x: ref[j - 1, x]


def halo_places(bx, base, scratch, sides=None):
    places, slot = {}, 0
    for j, m in COMPUTED:
        for low_side in (True, False):
            at = (base + j, halo_layer(bx, m, low_side))
            if sides is not None and (j, m) == (STEPS - 1, 1):
                places[at] = (sides, (0 if low_side else 1,))
            else:
                places[at] = (scratch, (slot,))
                slot += 1
    return places


def prepare_kernel(fields, rows, start, coef, vectors):
    _, bx, by, _ = fields.shape
    start[:, 0:by] = fields[0] * LIFT
    start[:, by:] = rows[0:bx] * LIFT
    for k in range(4):
        coef[k, :, 0:by] = scaled(k, fields[k + 1])
        coef[k, :, by:] = scaled(k, rows[bx * (k + 1) : bx * (k + 2)])
    places = own_places(bx, 0, vectors)
    cells = Cells(bx, coef, None, lambda j, x: places[j, x])
    for x in range(bx):
        cells.known[0, x] = lambda x=x: start[x]
    cells.interior(0)


def wide_layer(slab, corner, at, base):
    return jnp.concatenate([slab[at], corner[base + at]], axis=0)


def know_start(cells, start, low, high, corner):
    bx, size = start.shape[0], low.shape[0]
    for x in range(bx):
        cells.known[0, x] = lambda x=x: start[x]
    for side, slab, base in ((0, low, 0), (1, high, size)):
        for m in (1, 2):
            at = DEPTHS[0] - m if side == 0 else m - 1
            cells.known[0, halo_layer(bx, m, side == 0)] = lambda slab=slab, base=base, at=at: (
                wide_layer(slab, corner, at, base) * LIFT
            )


def early_range(j, bx):
    return range(j - 2, bx - (j - 2))


def first_kernel(start, coef, low, high, corner, given, vectors, beside, edge, weight):
    del given
    bx, by = start.shape[0], low.shape[1]
    size = low.shape[0]
    places = own_places(bx, 0, vectors)
    places[1, -1], places[1, bx] = (beside, (0,)), (beside, (1,))
    for side, slab, base in ((0, low, 0), (1, high, size)):
        for k in range(4):
            depth, at = DEPTHS[k + 1], OFFSETS[k + 1]
            at += depth - 1 if side == 0 else 0
            edge[k, side, 0:by] = scaled(k, slab[at])
            edge[k, side, by:] = scaled(k, corner[base + at])
        at = OFFSETS[2] + (0 if side == 0 else 1)
        sign = SCALES[1] if side == 0 else -SCALES[1]
        weight[side, 0:by] = slab[at] * sign - 2.0 * DIFFUSION / HALF_WIDTH
        weight[side, by:] = corner[base + at] * sign - 2.0 * DIFFUSION / HALF_WIDTH
    cells = Cells(bx, coef, edge, lambda j, x: places[j, x])
    mark_interior(cells, bx, 0, vectors)
    know_start(cells, start, low, high, corner)
    for j in range(1, STEPS + 1):
        for x in early_range(j, bx):
            cells.get(j, x)


def rest_kernel(
    start, coef, low, high, corner, beside, edge, weight, low_later, high_later, later_corner, given, vectors, to_low, to_high, following, sides, scratch
):
    del given
    bx, by = start.shape[0], low.shape[1]
    later = low_later.shape[0]
    places = own_places(bx, 0, vectors) | own_places(bx, STEPS, following) | halo_places(bx, 0, scratch, sides)
    cells = Cells(bx, coef, edge, lambda j, x: places[j, x])
    know_start(cells, start, low, high, corner)
    for j in range(1, STEPS + 1):
        for x in early_range(j, bx):
            cells.known[j, x] = lambda j=j, x=x: vectors[j - 1, x]
    cells.known[1, -1], cells.known[1, bx] = (lambda: beside[0]), (lambda: beside[1])
    for side, slab, base in ((0, low_later, 0), (1, high_later, later)):
        near, far = halo_layer(bx, 1, side == 0), halo_layer(bx, 2, side == 0)
        cells.known[1, far] = lambda slab=slab, base=base: wide_layer(slab, later_corner, 0, base)
        cells.computed[2, far] = lambda slab=slab, base=base, side=side, near=near: (
            wide_layer(slab, later_corner, 1, base) + weight[side] * cells.get(1, near)
        )
    cells.finish(0)
    for out, below, one, two in ((to_low, True, 0, 1), (to_high, False, bx - 1, bx - 2)):
        leaving = [
            cells.get(STEPS, one),
            cells.get(STEPS, two),
            cells.get(STEPS + 1, two),
            cells.tip(STEPS, two, below),
        ]
        for at, layer in enumerate(leaving):
            out[at * by : (at + 1) * by] = layer[:by]
        tiles = [(layer[by : by + MARGIN], layer[by + MARGIN :]) for layer in leaving[:3]]
        row = lax.broadcasted_iota(jnp.int32, tiles[0][0].shape, 0)
        out[4 * by : 4 * by + 8] = jnp.where(row < EDGE, *tiles[0])
        middle = jnp.where(row < EDGE, pltpu.roll(tiles[2][0], 2, 0), pltpu.roll(tiles[2][1], 6, 0))
        outer = jnp.where(row < EDGE, *tiles[1])
        out[4 * by + 8 :] = jnp.where((row == 2) | (row == 5), middle, outer)


def second_cells(one, sides, coef, edge, weight, slab, side, two, scratch):
    bx = coef.shape[1]
    by = slab.shape[0] // 4 - EDGE
    places = own_places(bx, STEPS, two) | halo_places(bx, STEPS, scratch)
    cells = Cells(bx, coef, edge, lambda j, x: places[j, x])
    mark_interior(cells, bx, STEPS, two)
    for x in range(bx):
        cells.known[STEPS, x] = lambda x=x: one[STEPS - 1, x]
        cells.known[STEPS - 1, x] = lambda x=x: one[STEPS - 2, x]
    near, far = halo_layer(bx, 1, side == 0), halo_layer(bx, 2, side == 0)

    def wide(at):
        first, second = slab[4 * by : 4 * by + 8], slab[4 * by + 8 :]
        above, below = ((first, first), (second, second), (pltpu.roll(second, 6, 0), pltpu.roll(second, 2, 0)))[min(at, 2)]
        return jnp.concatenate([slab[at * by : (at + 1) * by], above, below], axis=0)

    cells.known[STEPS - 1, near] = lambda: sides[side]
    cells.known[STEPS, near] = lambda: wide(0)
    cells.known[STEPS, far] = lambda: wide(1)
    cells.known[STEPS + 1, far] = lambda: wide(2)
    cells.computed[STEPS + 2, far] = lambda: wide(3) + weight[side] * cells.get(STEPS + 1, near)
    return cells


def reach_of(j):
    return max([m for i, m in COMPUTED if i == j], default=0)


def sooner_kernel(start, one, given, sides, coef, edge, weight, high, two, partial, scratch):
    del given
    bx, _, nz = start.shape
    by = high.shape[0] // 4 - EDGE
    cells = second_cells(one, sides, coef, edge, weight, high, 1, two, scratch)
    for j in range(1, STEPS + 1):
        for x in range(j, bx + reach_of(j)):
            cells.get(STEPS + j, x)
    totals = products(GROUPS[1], STEPS, bx, by, nz, reader(start, one, two))
    for k, total in enumerate(totals):
        partial[k] = total


def later_kernel(start, one, given, sides, coef, edge, weight, low, early_gram, partial, two, gram, scratch):
    del given
    bx, _, nz = start.shape
    by = low.shape[0] // 4 - EDGE
    cells = second_cells(one, sides, coef, edge, weight, low, 0, two, scratch)
    for j in range(1, STEPS + 1):
        for x in range(j, bx):
            cells.known[STEPS + j, x] = lambda j=j, x=x: two[j - 1, x]
    for j in range(1, STEPS + 1):
        for x in range(-reach_of(j), j):
            cells.get(STEPS + j, x)
    before = tuple(partial[k] for k in range(len(GROUPS[1])))
    rows = summed_rows(products(GROUPS[1], 0, STEPS, by, nz, reader(start, one, two), before))
    sums = jnp.concatenate([early_gram[...]] + rows, axis=0)
    on = lax.broadcasted_iota(jnp.int32, sums.shape, 0) == lax.broadcasted_iota(jnp.int32, sums.shape, 1)
    line = jnp.sum(jnp.where(on, jnp.sum(sums, axis=1, keepdims=True), 0.0), axis=0, keepdims=True)
    gram[...] = jnp.broadcast_to(line, gram.shape)


def last_kernel(cell_count, gram, start, one, two, out, factor, result, sem):
    _, bx, by, nz = result.shape
    total = gram[0:8]
    for row in range(8, gram.shape[0], 8):
        total = total + gram[row : row + 8]
    for distance in (4, 2, 1):
        total = total + pltpu.roll(total, distance, 0)
    total = total * (1.0 / cell_count)
    cell = reader(start, one, two)
    entry, inverse, copies = {}, [], []
    for j in range(BASIS):
        for i in range(j + 1):
            k = PLACE[i, j]
            value = jnp.broadcast_to(total[:, k : k + 1], (8, 128))
            if (i, j) == (0, 0):
                mean_square = value * (1.0 / (LIFT * LIFT))
            for above in range(i):
                value = value - entry[above, i] * entry[above, j]
            if i == j:
                inverse.append(lax.rsqrt(value))
            entry[i, j] = value * inverse[i]
        for x in range(bx):
            for y in range(0, by, 8):
                for z in range(0, nz, 128):
                    window = (x, slice(y, y + 8), slice(z, z + 128))
                    value = cell(j, *window)
                    for i in range(j):
                        value = value - entry[i, j] * result[(i,) + window]
                    result[(j,) + window] = value * inverse[j]
        copies.append(pltpu.make_async_copy(result.at[j], out.at[j], sem.at[j]))
        copies[j].start()
    scale = lax.rsqrt(mean_square + EPSILON) * (1.0 / LIFT)
    sublane = lax.broadcasted_iota(jnp.int32, (8, 128), 0)
    lane = lax.broadcasted_iota(jnp.int32, (8, 128), 1)
    tops = []
    for base in range(0, BASIS, 8):
        packed = jnp.zeros((8, 128), jnp.float32)
        for (i, j), value in entry.items():
            if base <= i < base + 8:
                packed = jnp.where((sublane == i - base) & (lane == j), value, packed)
        tops.append(packed * scale)
    factor[...] = jnp.concatenate(tops, axis=0)[:BASIS, :BASIS]
    for copy in copies:
        copy.wait()


def shape(*dims):
    return jax.ShapeDtypeStruct(dims, jnp.float32)


def call(kernel, outs, *args, name, scratch=(), us=0.02, in_specs=None, out_specs=None, aliases=None):
    return pl.pallas_call(
        kernel,
        out_shape=outs,
        in_specs=in_specs or [VMEM] * len(args),
        out_specs=out_specs or [VMEM] * len(outs),
        scratch_shapes=scratch,
        input_output_aliases=aliases or {},
        compiler_params=pltpu.CompilerParams(vmem_limit_bytes=24 << 20),
        cost_estimate=pl.CostEstimate(flops=0, transcendentals=0, bytes_accessed=int(us * 3e6)),
        name=name,
    )(*args)


def per_device(forcing, reaction, velocity):
    bx, by, nz = forcing.shape
    devices = lax.axis_size("gx") * lax.axis_size("gy")
    cell_count = float(bx * by * nz * devices)
    wide = by + 2 * MARGIN
    inputs = tuple(pltpu.with_memory_space_constraint(v, pltpu.MemorySpace.HBM) for v in (forcing, reaction, velocity))
    vectors = shape(STEPS, bx, wide, nz)
    fields, to_low, to_high, rows = call(
        pack_kernel,
        [shape(5, bx, by, nz)] + [shape(sum(DEPTHS), by, nz)] * 2 + [shape(SWAPPED[5], 2 * EDGE, nz)],
        *inputs,
        name="pack",
        in_specs=[HBM] * 3,
        scratch=[pltpu.SemaphoreType.DMA((5,))],
    )
    low, high = swap_x(to_low, to_high)
    rows = swap_rows(rows[:, :EDGE], rows[:, EDGE:])
    to_low, to_high = call(
        inner_kernel,
        [shape(2, by, nz)] * 2,
        fields,
        rows,
        name="inner",
        scratch=[pltpu.VMEM((4, by + 2 * EDGE, nz), jnp.float32)],
    )
    low_later, high_later = swap_x(to_low, to_high)
    rows = swap_y(fields.reshape(5 * bx, by, nz))
    start, coef, one = call(
        prepare_kernel, [shape(bx, wide, nz), shape(4, bx, wide, nz), vectors], fields, rows, name="prepare"
    )
    corner = swap_y(jnp.concatenate([low, high]))
    one, beside, edge, weight = call(
        first_kernel,
        [vectors, shape(2, wide, nz), shape(4, 2, wide, nz), shape(2, wide, nz)],
        start,
        coef,
        low,
        high,
        corner,
        one,
        name="first",
        aliases={5: 0},
    )
    one, to_low, to_high, two, sides = call(
        rest_kernel,
        [vectors, shape(4 * by + 16, nz), shape(4 * by + 16, nz), vectors, shape(2, wide, nz)],
        start,
        coef,
        low,
        high,
        corner,
        beside,
        edge,
        weight,
        low_later,
        high_later,
        swap_y(jnp.concatenate([low_later, high_later])),
        one,
        name="rest",
        scratch=[pltpu.VMEM((2 * len(COMPUTED), wide, nz), jnp.float32)],
        aliases={11: 0},
    )
    low, high = swap_x(to_low, to_high)
    two, early_gram = call(
        lambda *refs: second_interior_kernel(by, *refs),
        [vectors, shape(STARTS[1], 128)],
        start,
        one,
        coef,
        two,
        name="second_interior",
        aliases={3: 0},
    )
    halo = [pltpu.VMEM((2 * len(COMPUTED), wide, nz), jnp.float32)]
    two, partial = call(
        sooner_kernel,
        [vectors, shape(len(GROUPS[1]), 8, 128)],
        start,
        one,
        two,
        sides,
        coef,
        edge,
        weight,
        high,
        name="sooner",
        scratch=halo,
        aliases={2: 0},
    )
    two, gram = call(
        later_kernel,
        [vectors, shape(devices, 128)],
        start,
        one,
        two,
        sides,
        coef,
        edge,
        weight,
        low,
        early_gram,
        partial,
        name="later",
        scratch=halo,
        aliases={2: 0},
    )
    gram = lax.all_to_all(gram, AXES, 0, 0, tiled=True)
    return call(
        lambda *refs: last_kernel(cell_count, *refs),
        [shape(BASIS, bx, by, nz), shape(BASIS, BASIS)],
        gram,
        start,
        one,
        two,
        name="last",
        out_specs=[pl.BlockSpec(memory_space=pl.ANY), VMEM],
        scratch=[
            pltpu.VMEM((BASIS, bx, by, nz), jnp.float32),
            pltpu.SemaphoreType.DMA((BASIS,)),
        ],
    )


def solution(mesh):
    in_specs = (P("gx", "gy", None), P("gx", "gy", None), P(None, "gx", "gy", None))
    out_specs = (P(None, "gx", "gy", None), P())
    return jax.shard_map(per_device, mesh=mesh, in_specs=in_specs, out_specs=out_specs, check_vma=False)
```

```python
import jax
import jax.numpy as jnp
from jax import lax
from jax.experimental import pallas as pl
from jax.experimental.pallas import tpu as pltpu
from jax.sharding import PartitionSpec as P

BASIS = 9
STEPS = 4
MARGIN = 8
EDGE = 4

DIFFUSION = 0.03
CENTRE_SHIFT = 1.18
HALF_WIDTH = 0.95
EPSILON = 1e-06
LIFT = 1024.0
SCALES = (2.0 / HALF_WIDTH, 1.0 / HALF_WIDTH, 1.0 / HALF_WIDTH, 1.0 / HALF_WIDTH)
SHIFTS = (2.0 * (6.0 * DIFFUSION - CENTRE_SHIFT) / HALF_WIDTH, 0.0, 0.0, 0.0)
AXES = ("gx", "gy")
VMEM = pl.BlockSpec(memory_space=pltpu.VMEM)
HBM = pl.BlockSpec(memory_space=pltpu.MemorySpace.HBM)


COMPUTED = ((1, 1), (2, 1), (2, 2), (3, 1))
GIVEN = ((0, 1), (0, 2), (1, 2))
TIP = (2, 2)
DEPTHS = (2, 1, 2, 1, 1)
OFFSETS = (0, 2, 3, 5, 6)


def pairs_of(low, high):
    return [(i, j) for j in range(low, high) for i in range(j + 1)]


GROUPS = (pairs_of(0, STEPS + 1), pairs_of(STEPS + 1, BASIS))
STARTS = (0, -(-len(GROUPS[0]) // 8) * 8)
GRAM_ROWS = STARTS[1] - (-len(GROUPS[1]) // 8) * 8
PLACE = {pair: start + k for start, group in zip(STARTS, GROUPS) for k, pair in enumerate(group)}


def ring(axis, step):
    count = lax.axis_size(axis)
    return [(i, (i + step) % count) for i in range(count)]


def swap_x(to_low, to_high):
    return lax.ppermute(to_high, "gx", ring("gx", 1)), lax.ppermute(to_low, "gx", ring("gx", -1))


def swap_y(block):
    rows = block.shape[1]
    return swap_rows(block[:, :MARGIN], block[:, rows - MARGIN :])


def swap_rows(low, high):
    if lax.axis_size("gy") == 2:
        return lax.ppermute(jnp.concatenate([low, high], axis=1), "gy", ring("gy", 1))
    above = lax.ppermute(low, "gy", ring("gy", -1))
    below = lax.ppermute(high, "gy", ring("gy", 1))
    return jnp.concatenate([above, below], axis=1)


def doubled(centre, east, west, coef):
    rows, lanes = centre.shape
    kept = east.shape[0]
    north = pltpu.roll(centre, rows - 1, 0)[:kept]
    south = pltpu.roll(centre, 1, 0)[:kept]
    centre = centre[:kept]
    upper = pltpu.roll(centre, lanes - 1, 1)
    lower = pltpu.roll(centre, 1, 1)
    around = (east + west) + (north + south) + (upper + lower)
    slopes = coef[1] * (east - west) + coef[2] * (north - south) + coef[3] * (upper - lower)
    return coef[0] * centre + slopes - (2.0 * DIFFUSION / HALF_WIDTH) * around


def scaled(k, value):
    return value * SCALES[k] + SHIFTS[k]


def products(pairs, first, last, by, nz, cell, totals=None):
    needed = sorted({i for pair in pairs for i in pair})
    tiles = by // 8

    def add(at, totals):
        x, y = first + at // tiles, pl.multiple_of(at % tiles * 8, 8)
        for z in range(0, nz, 128):
            cells = {i: cell(i, x, pl.ds(y, 8), pl.ds(z, 128)) for i in needed}
            totals = tuple(t + cells[i] * cells[j] for t, (i, j) in zip(totals, pairs))
        return totals

    if totals is None:
        totals = tuple(jnp.zeros((8, 128), jnp.float32) for _ in pairs)
    return lax.fori_loop(0, (last - first) * tiles, add, totals, unroll=True)


def later_products(layers, before, by, nz, cell):
    totals, at = [], 0
    for j in range(1, STEPS + 1):
        pairs = [pair for pair in GROUPS[1] if pair[1] == STEPS + j]
        group = tuple(before[at : at + len(pairs)])
        first, last = layers(j)
        totals += products(pairs, first, last, by, nz, cell, group) if last > first else group
        at += len(pairs)
    return totals


def summed_rows(totals):
    sublane = lax.broadcasted_iota(jnp.int32, (8, 128), 0)
    rows = []
    for base in range(0, len(totals), 8):
        packed = jnp.zeros((8, 128), jnp.float32)
        for k, total in enumerate(totals[base : base + 8]):
            for distance in (4, 2, 1):
                total = total + pltpu.roll(total, distance, 0)
            packed = jnp.where(sublane == k, total, packed)
        rows.append(packed)
    return rows


def reader(start, one, two=None):
    def cell(i, x, y, z):
        if i == 0:
            return start[x, y, z]
        if i <= STEPS:
            return one[i - 1, x, y, z]
        return two[i - 1 - STEPS, x, y, z]

    return cell


def second_interior_kernel(by, start, one, coef, given, vectors, gram, partial):
    del given
    bx, _, nz = start.shape
    places = own_places(bx, STEPS, vectors)
    cells = Cells(bx, coef, None, lambda j, x: places[j, x])
    for x in (1, 2, bx - 3, bx - 2):
        cells.known[STEPS + 1, x] = lambda x=x: vectors[0, x]
    for x in range(bx):
        cells.known[STEPS, x] = lambda x=x: one[STEPS - 1, x]
        cells.known[STEPS - 1, x] = lambda x=x: one[STEPS - 2, x]
    cells.interior(STEPS)
    for k, row in enumerate(summed_rows(products(GROUPS[0], 0, bx, by, nz, reader(start, one)))):
        gram[8 * k : 8 * k + 8] = row
    none = [jnp.zeros((8, 128), jnp.float32)] * len(GROUPS[1])
    totals = later_products(lambda j: (j, bx - j), none, by, nz, reader(start, one, vectors))
    for k, total in enumerate(totals):
        partial[k] = total


def fields_of(f, r, vel):
    return f, r, vel.at[0], vel.at[1], vel.at[2]


REACH = ((0, 3),) + ((1, 3),) * 4
SWAPPED = tuple(sum(2 * (high - low) for low, high in REACH[:k]) for k in range(6))


def edge_rows(block):
    rows = block.shape[-2]
    low, high = block[..., : 2 * EDGE, :], block[..., rows - 2 * EDGE :, :]
    row = lax.broadcasted_iota(jnp.int32, low.shape, low.ndim - 2)
    return jnp.where(row < EDGE, low, high)


def pack_kernel(f, r, vel, fields, to_low, to_high, rows, sem):
    bx = f.shape[0]
    copies = [pltpu.make_async_copy(field, fields.at[k], sem.at[k]) for k, field in enumerate(fields_of(f, r, vel))]
    for copy in copies:
        copy.start()
    for k in range(5):
        copies[k].wait()
        depth, at = DEPTHS[k], OFFSETS[k]
        to_low[at : at + depth] = fields[k, 0:depth]
        to_high[at : at + depth] = fields[k, bx - depth : bx]
        (low, high), at = REACH[k], SWAPPED[k]
        rows[at : at + high - low] = edge_rows(fields[k, low:high])
        rows[at + high - low : at + 2 * (high - low)] = edge_rows(fields[k, bx - high : bx - low])


def inner_kernel(fields, rows, to_low, to_high, scratch):
    _, bx, by, _ = fields.shape

    def layer(k, x):
        (low, high), at = REACH[k], SWAPPED[k]
        at += x - low if x < high else high - low + x - (bx - high)
        return jnp.concatenate([fields[k, x], rows[at]], axis=0)

    class Coefficients:
        shape = (4, bx)

        def __getitem__(self, at):
            return scaled(at[0], layer(at[0] + 1, at[1]))

    cells = Cells(bx, Coefficients(), None, lambda j, x: (scratch, ({1: 0, 2: 1, bx - 3: 2, bx - 2: 3}[x],)))
    for x in (0, 1, 2, 3, bx - 4, bx - 3, bx - 2, bx - 1):
        if 3 <= x < bx - 3:
            cells.known[0, x] = lambda x=x: jnp.concatenate([fields[0, x], jnp.zeros_like(rows[0])], axis=0) * LIFT
        else:
            cells.known[0, x] = lambda x=x: layer(0, x) * LIFT
    to_low[0] = cells.get(1, 1)[:by]
    to_high[0] = cells.get(1, bx - 2)[:by]
    to_low[1] = cells.tip(0, 1, True)[:by]
    to_high[1] = cells.tip(0, bx - 2, False)[:by]


class Cells:
    def __init__(self, bx, coef, edge, place):
        self.bx, self.coef, self.edge, self.place = bx, coef, edge, place
        self.known, self.computed = {}, {}

    def coefficients(self, x):
        if 0 <= x < self.bx:
            return [self.coef[k, x] for k in range(4)]
        return [self.edge[k, 0 if x < 0 else 1] for k in range(4)]

    def get(self, j, x):
        if (j, x) not in self.known:
            ref, at = self.place(j, x)
            rows = ref.shape[-2] - (2 * MARGIN if j == BASIS - 1 else 0)
            if (j, x) in self.computed:
                new = self.computed[j, x]()
            else:
                east, west = self.get(j - 1, x + 1)[:rows], self.get(j - 1, x - 1)[:rows]
                new = doubled(self.get(j - 1, x), east, west, [c[:rows] for c in self.coefficients(x)])
                new = new * 0.5 if j == 1 else new - self.get(j - 2, x)[:rows]
            at = at + (slice(0, rows),)
            ref[at] = new
            self.known[j, x] = lambda: ref[at]
        return self.known[j, x]()

    def tip(self, base, x, below):
        j = base + TIP[0]
        centre, beyond = self.get(j - 1, x), self.get(j - 1, x + 1 if below else x - 1)
        nothing = jnp.zeros_like(centre)
        pair = (beyond, nothing) if below else (nothing, beyond)
        return doubled(centre, *pair, self.coefficients(x)) - self.get(j - 2, x)

    def interior(self, base):
        for j in range(1, STEPS):
            for x in range(j, self.bx - j):
                self.get(base + j, x)

    def finish(self, base):
        for j in range(1, STEPS + 1):
            reach = max([m for i, m in COMPUTED if i == j], default=0)
            for x in range(-reach, self.bx + reach):
                self.get(base + j, x)


def halo_layer(bx, m, low_side):
    return -m if low_side else bx - 1 + m


def own_places(bx, base, ref):
    return {(base + j, x): (ref, (j - 1, x)) for j in range(1, STEPS + 1) for x in range(bx)}


def mark_interior(cells, bx, base, ref):
    for j in range(1, STEPS):
        for x in range(j, bx - j):
            cells.known[base + j, x] = lambda j=j, x=x: ref[j - 1, x]


def halo_places(bx, base, scratch, sides=None):
    places, slot = {}, 0
    for j, m in COMPUTED:
        for low_side in (True, False):
            at = (base + j, halo_layer(bx, m, low_side))
            if sides is not None and (j, m) == (STEPS - 1, 1):
                places[at] = (sides, (0 if low_side else 1,))
            else:
                places[at] = (scratch, (slot,))
                slot += 1
    return places


def prepare_kernel(fields, rows, start, coef, vectors):
    _, bx, by, _ = fields.shape
    start[:, 0:by] = fields[0] * LIFT
    start[:, by:] = rows[0:bx] * LIFT
    for k in range(4):
        coef[k, :, 0:by] = scaled(k, fields[k + 1])
        coef[k, :, by:] = scaled(k, rows[bx * (k + 1) : bx * (k + 2)])
    places = own_places(bx, 0, vectors)
    cells = Cells(bx, coef, None, lambda j, x: places[j, x])
    for x in range(bx):
        cells.known[0, x] = lambda x=x: start[x]
    cells.interior(0)


def wide_layer(slab, corner, at, base):
    return jnp.concatenate([slab[at], corner[base + at]], axis=0)


def know_start(cells, start, low, high, corner):
    bx, size = start.shape[0], low.shape[0]
    for x in range(bx):
        cells.known[0, x] = lambda x=x: start[x]
    for side, slab, base in ((0, low, 0), (1, high, size)):
        for m in (1, 2):
            at = DEPTHS[0] - m if side == 0 else m - 1
            cells.known[0, halo_layer(bx, m, side == 0)] = lambda slab=slab, base=base, at=at: (
                wide_layer(slab, corner, at, base) * LIFT
            )


def early_range(j, bx):
    return range(j - 2, bx - (j - 2))


def first_kernel(start, coef, low, high, corner, given, vectors, beside, edge, weight):
    del given
    bx, by = start.shape[0], low.shape[1]
    size = low.shape[0]
    places = own_places(bx, 0, vectors)
    places[1, -1], places[1, bx] = (beside, (0,)), (beside, (1,))
    for side, slab, base in ((0, low, 0), (1, high, size)):
        for k in range(4):
            depth, at = DEPTHS[k + 1], OFFSETS[k + 1]
            at += depth - 1 if side == 0 else 0
            edge[k, side, 0:by] = scaled(k, slab[at])
            edge[k, side, by:] = scaled(k, corner[base + at])
        at = OFFSETS[2] + (0 if side == 0 else 1)
        sign = SCALES[1] if side == 0 else -SCALES[1]
        weight[side, 0:by] = slab[at] * sign - 2.0 * DIFFUSION / HALF_WIDTH
        weight[side, by:] = corner[base + at] * sign - 2.0 * DIFFUSION / HALF_WIDTH
    cells = Cells(bx, coef, edge, lambda j, x: places[j, x])
    mark_interior(cells, bx, 0, vectors)
    know_start(cells, start, low, high, corner)
    for j in range(1, STEPS + 1):
        for x in early_range(j, bx):
            cells.get(j, x)


def rest_kernel(
    start, coef, low, high, corner, beside, edge, weight, low_later, high_later, later_corner, given, vectors, to_low, to_high, following, sides, scratch
):
    del given
    bx, by = start.shape[0], low.shape[1]
    later = low_later.shape[0]
    places = own_places(bx, 0, vectors) | own_places(bx, STEPS, following) | halo_places(bx, 0, scratch, sides)
    cells = Cells(bx, coef, edge, lambda j, x: places[j, x])
    know_start(cells, start, low, high, corner)
    for j in range(1, STEPS + 1):
        for x in early_range(j, bx):
            cells.known[j, x] = lambda j=j, x=x: vectors[j - 1, x]
    cells.known[1, -1], cells.known[1, bx] = (lambda: beside[0]), (lambda: beside[1])
    for side, slab, base in ((0, low_later, 0), (1, high_later, later)):
        near, far = halo_layer(bx, 1, side == 0), halo_layer(bx, 2, side == 0)
        cells.known[1, far] = lambda slab=slab, base=base: wide_layer(slab, later_corner, 0, base)
        cells.computed[2, far] = lambda slab=slab, base=base, side=side, near=near: (
            wide_layer(slab, later_corner, 1, base) + weight[side] * cells.get(1, near)
        )
    cells.finish(0)
    for out, below, one, two in ((to_low, True, 0, 1), (to_high, False, bx - 1, bx - 2)):
        leaving = [
            cells.get(STEPS, one),
            cells.get(STEPS, two),
            cells.get(STEPS + 1, two),
            cells.tip(STEPS, two, below),
        ]
        for at, layer in enumerate(leaving):
            out[at * by : (at + 1) * by] = layer[:by]
        tiles = [(layer[by : by + MARGIN], layer[by + MARGIN :]) for layer in leaving[:3]]
        row = lax.broadcasted_iota(jnp.int32, tiles[0][0].shape, 0)
        out[4 * by : 4 * by + 8] = jnp.where(row < EDGE, *tiles[0])
        middle = jnp.where(row < EDGE, pltpu.roll(tiles[2][0], 2, 0), pltpu.roll(tiles[2][1], 6, 0))
        outer = jnp.where(row < EDGE, *tiles[1])
        out[4 * by + 8 :] = jnp.where((row == 2) | (row == 5), middle, outer)


def second_cells(one, sides, coef, edge, weight, slab, side, two, scratch):
    bx = coef.shape[1]
    by = slab.shape[0] // 4 - EDGE
    places = own_places(bx, STEPS, two) | halo_places(bx, STEPS, scratch)
    cells = Cells(bx, coef, edge, lambda j, x: places[j, x])
    mark_interior(cells, bx, STEPS, two)
    for x in range(bx):
        cells.known[STEPS, x] = lambda x=x: one[STEPS - 1, x]
        cells.known[STEPS - 1, x] = lambda x=x: one[STEPS - 2, x]
    near, far = halo_layer(bx, 1, side == 0), halo_layer(bx, 2, side == 0)

    def wide(at):
        first, second = slab[4 * by : 4 * by + 8], slab[4 * by + 8 :]
        above, below = ((first, first), (second, second), (pltpu.roll(second, 6, 0), pltpu.roll(second, 2, 0)))[min(at, 2)]
        return jnp.concatenate([slab[at * by : (at + 1) * by], above, below], axis=0)

    cells.known[STEPS - 1, near] = lambda: sides[side]
    cells.known[STEPS, near] = lambda: wide(0)
    cells.known[STEPS, far] = lambda: wide(1)
    cells.known[STEPS + 1, far] = lambda: wide(2)
    cells.computed[STEPS + 2, far] = lambda: wide(3) + weight[side] * cells.get(STEPS + 1, near)
    return cells


def reach_of(j):
    return max([m for i, m in COMPUTED if i == j], default=0)


def sooner_kernel(start, one, given, sides, coef, edge, weight, high, before, two, partial, scratch):
    del given
    bx, _, nz = start.shape
    by = high.shape[0] // 4 - EDGE
    cells = second_cells(one, sides, coef, edge, weight, high, 1, two, scratch)
    for j in range(1, STEPS + 1):
        for x in range(j, bx + reach_of(j)):
            cells.get(STEPS + j, x)
    before = [before[k] for k in range(len(GROUPS[1]))]
    totals = later_products(lambda j: (bx - j, bx), before, by, nz, reader(start, one, two))
    for k, total in enumerate(totals):
        partial[k] = total


def later_kernel(start, one, given, sides, coef, edge, weight, low, early_gram, partial, two, gram, scratch):
    del given
    bx, _, nz = start.shape
    by = low.shape[0] // 4 - EDGE
    cells = second_cells(one, sides, coef, edge, weight, low, 0, two, scratch)
    for j in range(1, STEPS + 1):
        for x in range(j, bx):
            cells.known[STEPS + j, x] = lambda j=j, x=x: two[j - 1, x]
    for j in range(1, STEPS + 1):
        for x in range(-reach_of(j), j):
            cells.get(STEPS + j, x)
    before = [partial[k] for k in range(len(GROUPS[1]))]
    rows = summed_rows(later_products(lambda j: (0, j), before, by, nz, reader(start, one, two)))
    sums = jnp.concatenate([early_gram[...]] + rows, axis=0)
    on = lax.broadcasted_iota(jnp.int32, sums.shape, 0) == lax.broadcasted_iota(jnp.int32, sums.shape, 1)
    line = jnp.sum(jnp.where(on, jnp.sum(sums, axis=1, keepdims=True), 0.0), axis=0, keepdims=True)
    gram[...] = jnp.broadcast_to(line, gram.shape)


def last_kernel(cell_count, gram, start, one, two, out, factor, result, sem):
    _, bx, by, nz = result.shape
    total = gram[0:8]
    for row in range(8, gram.shape[0], 8):
        total = total + gram[row : row + 8]
    for distance in (4, 2, 1):
        total = total + pltpu.roll(total, distance, 0)
    total = total * (1.0 / cell_count)
    cell = reader(start, one, two)
    entry, inverse, copies = {}, [], []
    for j in range(BASIS):
        for i in range(j + 1):
            k = PLACE[i, j]
            value = jnp.broadcast_to(total[:, k : k + 1], (8, 128))
            if (i, j) == (0, 0):
                mean_square = value * (1.0 / (LIFT * LIFT))
            for above in range(i):
                value = value - entry[above, i] * entry[above, j]
            if i == j:
                inverse.append(lax.rsqrt(value))
            entry[i, j] = value * inverse[i]
        for x in range(bx):
            for y in range(0, by, 8):
                for z in range(0, nz, 128):
                    window = (x, slice(y, y + 8), slice(z, z + 128))
                    value = cell(j, *window)
                    for i in range(j):
                        value = value - entry[i, j] * result[(i,) + window]
                    result[(j,) + window] = value * inverse[j]
        copies.append(pltpu.make_async_copy(result.at[j], out.at[j], sem.at[j]))
        copies[j].start()
    scale = lax.rsqrt(mean_square + EPSILON) * (1.0 / LIFT)
    sublane = lax.broadcasted_iota(jnp.int32, (8, 128), 0)
    lane = lax.broadcasted_iota(jnp.int32, (8, 128), 1)
    tops = []
    for base in range(0, BASIS, 8):
        packed = jnp.zeros((8, 128), jnp.float32)
        for (i, j), value in entry.items():
            if base <= i < base + 8:
                packed = jnp.where((sublane == i - base) & (lane == j), value, packed)
        tops.append(packed * scale)
    factor[...] = jnp.concatenate(tops, axis=0)[:BASIS, :BASIS]
    for copy in copies:
        copy.wait()


def shape(*dims):
    return jax.ShapeDtypeStruct(dims, jnp.float32)


def call(kernel, outs, *args, name, scratch=(), us=0.02, in_specs=None, out_specs=None, aliases=None):
    return pl.pallas_call(
        kernel,
        out_shape=outs,
        in_specs=in_specs or [VMEM] * len(args),
        out_specs=out_specs or [VMEM] * len(outs),
        scratch_shapes=scratch,
        input_output_aliases=aliases or {},
        compiler_params=pltpu.CompilerParams(vmem_limit_bytes=24 << 20),
        cost_estimate=pl.CostEstimate(flops=0, transcendentals=0, bytes_accessed=int(us * 3e6)),
        name=name,
    )(*args)


def per_device(forcing, reaction, velocity):
    bx, by, nz = forcing.shape
    devices = lax.axis_size("gx") * lax.axis_size("gy")
    cell_count = float(bx * by * nz * devices)
    wide = by + 2 * MARGIN
    inputs = tuple(pltpu.with_memory_space_constraint(v, pltpu.MemorySpace.HBM) for v in (forcing, reaction, velocity))
    vectors = shape(STEPS, bx, wide, nz)
    fields, to_low, to_high, rows = call(
        pack_kernel,
        [shape(5, bx, by, nz)] + [shape(sum(DEPTHS), by, nz)] * 2 + [shape(SWAPPED[5], 2 * EDGE, nz)],
        *inputs,
        name="pack",
        in_specs=[HBM] * 3,
        scratch=[pltpu.SemaphoreType.DMA((5,))],
    )
    low, high = swap_x(to_low, to_high)
    rows = swap_rows(rows[:, :EDGE], rows[:, EDGE:])
    to_low, to_high = call(
        inner_kernel,
        [shape(2, by, nz)] * 2,
        fields,
        rows,
        name="inner",
        scratch=[pltpu.VMEM((4, by + 2 * EDGE, nz), jnp.float32)],
    )
    low_later, high_later = swap_x(to_low, to_high)
    rows = swap_y(fields.reshape(5 * bx, by, nz))
    start, coef, one = call(
        prepare_kernel, [shape(bx, wide, nz), shape(4, bx, wide, nz), vectors], fields, rows, name="prepare"
    )
    corner = swap_y(jnp.concatenate([low, high]))
    one, beside, edge, weight = call(
        first_kernel,
        [vectors, shape(2, wide, nz), shape(4, 2, wide, nz), shape(2, wide, nz)],
        start,
        coef,
        low,
        high,
        corner,
        one,
        name="first",
        aliases={5: 0},
    )
    one, to_low, to_high, two, sides = call(
        rest_kernel,
        [vectors, shape(4 * by + 16, nz), shape(4 * by + 16, nz), vectors, shape(2, wide, nz)],
        start,
        coef,
        low,
        high,
        corner,
        beside,
        edge,
        weight,
        low_later,
        high_later,
        swap_y(jnp.concatenate([low_later, high_later])),
        one,
        name="rest",
        scratch=[pltpu.VMEM((2 * len(COMPUTED), wide, nz), jnp.float32)],
        aliases={11: 0},
    )
    low, high = swap_x(to_low, to_high)
    two, early_gram, partial = call(
        lambda *refs: second_interior_kernel(by, *refs),
        [vectors, shape(STARTS[1], 128), shape(len(GROUPS[1]), 8, 128)],
        start,
        one,
        coef,
        two,
        name="second_interior",
        aliases={3: 0},
    )
    halo = [pltpu.VMEM((2 * len(COMPUTED), wide, nz), jnp.float32)]
    two, partial = call(
        sooner_kernel,
        [vectors, shape(len(GROUPS[1]), 8, 128)],
        start,
        one,
        two,
        sides,
        coef,
        edge,
        weight,
        high,
        partial,
        name="sooner",
        scratch=halo,
        aliases={2: 0},
    )
    two, gram = call(
        later_kernel,
        [vectors, shape(devices, 128)],
        start,
        one,
        two,
        sides,
        coef,
        edge,
        weight,
        low,
        early_gram,
        partial,
        name="later",
        scratch=halo,
        aliases={2: 0},
    )
    gram = lax.all_to_all(gram, AXES, 0, 0, tiled=True)
    return call(
        lambda *refs: last_kernel(cell_count, *refs),
        [shape(BASIS, bx, by, nz), shape(BASIS, BASIS)],
        gram,
        start,
        one,
        two,
        name="last",
        out_specs=[pl.BlockSpec(memory_space=pl.ANY), VMEM],
        scratch=[
            pltpu.VMEM((BASIS, bx, by, nz), jnp.float32),
            pltpu.SemaphoreType.DMA((BASIS,)),
        ],
    )


def solution(mesh):
    in_specs = (P("gx", "gy", None), P("gx", "gy", None), P(None, "gx", "gy", None))
    out_specs = (P(None, "gx", "gy", None), P())
    return jax.shard_map(per_device, mesh=mesh, in_specs=in_specs, out_specs=out_specs, check_vma=False)
```

```python
import jax
import jax.numpy as jnp
from jax import lax
from jax.experimental import pallas as pl
from jax.experimental.pallas import tpu as pltpu
from jax.sharding import PartitionSpec as P

BASIS = 9
STEPS = 4
MARGIN = 8
EDGE = 4

DIFFUSION = 0.03
CENTRE_SHIFT = 1.18
HALF_WIDTH = 0.95
EPSILON = 1e-06
LIFT = 1024.0
SCALES = (2.0 / HALF_WIDTH, 1.0 / HALF_WIDTH, 1.0 / HALF_WIDTH, 1.0 / HALF_WIDTH)
SHIFTS = (2.0 * (6.0 * DIFFUSION - CENTRE_SHIFT) / HALF_WIDTH, 0.0, 0.0, 0.0)
AXES = ("gx", "gy")
VMEM = pl.BlockSpec(memory_space=pltpu.VMEM)
HBM = pl.BlockSpec(memory_space=pltpu.MemorySpace.HBM)


COMPUTED = ((1, 1), (2, 1), (2, 2), (3, 1))
GIVEN = ((0, 1), (0, 2), (1, 2))
TIP = (2, 2)
DEPTHS = (2, 1, 2, 1, 1)
OFFSETS = (0, 2, 3, 5, 6)


def pairs_of(low, high):
    return [(i, j) for j in range(low, high) for i in range(j + 1)]


GROUPS = (pairs_of(0, STEPS + 1), pairs_of(STEPS + 1, BASIS))
STARTS = (0, -(-len(GROUPS[0]) // 8) * 8)
GRAM_ROWS = STARTS[1] - (-len(GROUPS[1]) // 8) * 8
PLACE = {pair: start + k for start, group in zip(STARTS, GROUPS) for k, pair in enumerate(group)}


def ring(axis, step):
    count = lax.axis_size(axis)
    return [(i, (i + step) % count) for i in range(count)]


def swap_x(to_low, to_high):
    return lax.ppermute(to_high, "gx", ring("gx", 1)), lax.ppermute(to_low, "gx", ring("gx", -1))


def swap_y(block):
    rows = block.shape[1]
    return swap_rows(block[:, :MARGIN], block[:, rows - MARGIN :])


def swap_rows(low, high):
    if lax.axis_size("gy") == 2:
        return lax.ppermute(jnp.concatenate([low, high], axis=1), "gy", ring("gy", 1))
    above = lax.ppermute(low, "gy", ring("gy", -1))
    below = lax.ppermute(high, "gy", ring("gy", 1))
    return jnp.concatenate([above, below], axis=1)


def doubled(centre, east, west, coef):
    rows, lanes = centre.shape
    kept = east.shape[0]
    north = pltpu.roll(centre, rows - 1, 0)[:kept]
    south = pltpu.roll(centre, 1, 0)[:kept]
    centre = centre[:kept]
    upper = pltpu.roll(centre, lanes - 1, 1)
    lower = pltpu.roll(centre, 1, 1)
    around = (east + west) + (north + south) + (upper + lower)
    slopes = coef[1] * (east - west) + coef[2] * (north - south) + coef[3] * (upper - lower)
    return coef[0] * centre + slopes - (2.0 * DIFFUSION / HALF_WIDTH) * around


def scaled(k, value):
    return value * SCALES[k] + SHIFTS[k]


def products(pairs, first, last, by, nz, cell, totals=None):
    needed = sorted({i for pair in pairs for i in pair})
    tiles = by // 8

    def add(at, totals):
        x, y = first + at // tiles, pl.multiple_of(at % tiles * 8, 8)
        for z in range(0, nz, 128):
            cells = {i: cell(i, x, pl.ds(y, 8), pl.ds(z, 128)) for i in needed}
            totals = tuple(t + cells[i] * cells[j] for t, (i, j) in zip(totals, pairs))
        return totals

    if totals is None:
        totals = tuple(jnp.zeros((8, 128), jnp.float32) for _ in pairs)
    return lax.fori_loop(0, (last - first) * tiles, add, totals, unroll=True)


def later_products(layers, before, by, nz, cell):
    totals, at = [], 0
    for j in range(1, STEPS + 1):
        pairs = [pair for pair in GROUPS[1] if pair[1] == STEPS + j]
        group = tuple(before[at : at + len(pairs)])
        first, last = layers(j)
        totals += products(pairs, first, last, by, nz, cell, group) if last > first else group
        at += len(pairs)
    return totals


def summed_rows(totals):
    sublane = lax.broadcasted_iota(jnp.int32, (8, 128), 0)
    rows = []
    for base in range(0, len(totals), 8):
        packed = jnp.zeros((8, 128), jnp.float32)
        for k, total in enumerate(totals[base : base + 8]):
            for distance in (4, 2, 1):
                total = total + pltpu.roll(total, distance, 0)
            packed = jnp.where(sublane == k, total, packed)
        rows.append(packed)
    return rows


def reader(start, one, two=None):
    def cell(i, x, y, z):
        if i == 0:
            return start[x, y, z]
        if i <= STEPS:
            return one[i - 1, x, y, z]
        return two[i - 1 - STEPS, x, y, z]

    return cell


def second_interior_kernel(by, start, one, coef, given, vectors, gram, partial):
    del given
    bx, _, nz = start.shape
    places = own_places(bx, STEPS, vectors)
    cells = Cells(bx, coef, None, lambda j, x: places[j, x])
    for x in (1, 2, bx - 3, bx - 2):
        cells.known[STEPS + 1, x] = lambda x=x: vectors[0, x]
    for x in range(bx):
        cells.known[STEPS, x] = lambda x=x: one[STEPS - 1, x]
        cells.known[STEPS - 1, x] = lambda x=x: one[STEPS - 2, x]
    cells.interior(STEPS)
    for k, row in enumerate(summed_rows(products(GROUPS[0], 0, bx, by, nz, reader(start, one)))):
        gram[8 * k : 8 * k + 8] = row
    none = [jnp.zeros((8, 128), jnp.float32)] * len(GROUPS[1])
    totals = later_products(lambda j: (j, bx - j), none, by, nz, reader(start, one, vectors))
    for k, total in enumerate(totals):
        partial[k] = total


def fields_of(f, r, vel):
    return f, r, vel.at[0], vel.at[1], vel.at[2]


REACH = ((0, 3),) + ((1, 3),) * 4
SWAPPED = tuple(sum(2 * (high - low) for low, high in REACH[:k]) for k in range(6))


def edge_rows(block):
    rows = block.shape[-2]
    low, high = block[..., : 2 * EDGE, :], block[..., rows - 2 * EDGE :, :]
    row = lax.broadcasted_iota(jnp.int32, low.shape, low.ndim - 2)
    return jnp.where(row < EDGE, low, high)


def pack_kernel(f, r, vel, fields, to_low, to_high, rows, sem):
    bx = f.shape[0]
    copies = [pltpu.make_async_copy(field, fields.at[k], sem.at[k]) for k, field in enumerate(fields_of(f, r, vel))]
    for copy in copies:
        copy.start()
    for k in range(5):
        copies[k].wait()
        depth, at = DEPTHS[k], OFFSETS[k]
        to_low[at : at + depth] = fields[k, 0:depth]
        to_high[at : at + depth] = fields[k, bx - depth : bx]
        (low, high), at = REACH[k], SWAPPED[k]
        rows[at : at + high - low] = edge_rows(fields[k, low:high])
        rows[at + high - low : at + 2 * (high - low)] = edge_rows(fields[k, bx - high : bx - low])


def inner_kernel(fields, rows, to_low, to_high, scratch):
    _, bx, by, _ = fields.shape

    def layer(k, x):
        (low, high), at = REACH[k], SWAPPED[k]
        at += x - low if x < high else high - low + x - (bx - high)
        return jnp.concatenate([fields[k, x], rows[at]], axis=0)

    class Coefficients:
        shape = (4, bx)

        def __getitem__(self, at):
            return scaled(at[0], layer(at[0] + 1, at[1]))

    cells = Cells(bx, Coefficients(), None, lambda j, x: (scratch, ({1: 0, 2: 1, bx - 3: 2, bx - 2: 3}[x],)))
    for x in (0, 1, 2, 3, bx - 4, bx - 3, bx - 2, bx - 1):
        if 3 <= x < bx - 3:
            cells.known[0, x] = lambda x=x: jnp.concatenate([fields[0, x], jnp.zeros_like(rows[0])], axis=0) * LIFT
        else:
            cells.known[0, x] = lambda x=x: layer(0, x) * LIFT
    to_low[0] = cells.get(1, 1)[:by]
    to_high[0] = cells.get(1, bx - 2)[:by]
    to_low[1] = cells.tip(0, 1, True, by)
    to_high[1] = cells.tip(0, bx - 2, False, by)


class Cells:
    def __init__(self, bx, coef, edge, place):
        self.bx, self.coef, self.edge, self.place = bx, coef, edge, place
        self.known, self.computed = {}, {}

    def coefficients(self, x):
        if 0 <= x < self.bx:
            return [self.coef[k, x] for k in range(4)]
        return [self.edge[k, 0 if x < 0 else 1] for k in range(4)]

    def get(self, j, x):
        if (j, x) not in self.known:
            ref, at = self.place(j, x)
            rows = ref.shape[-2] - (2 * MARGIN if j == BASIS - 1 else 0)
            if (j, x) in self.computed:
                new = self.computed[j, x]()
            else:
                east, west = self.get(j - 1, x + 1)[:rows], self.get(j - 1, x - 1)[:rows]
                new = doubled(self.get(j - 1, x), east, west, [c[:rows] for c in self.coefficients(x)])
                new = new * 0.5 if j == 1 else new - self.get(j - 2, x)[:rows]
            at = at + (slice(0, rows),)
            ref[at] = new
            self.known[j, x] = lambda: ref[at]
        return self.known[j, x]()

    def tip(self, base, x, below, by):
        j = base + TIP[0]
        centre, beyond = self.get(j - 1, x), self.get(j - 1, x + 1 if below else x - 1)[:by]
        nothing = jnp.zeros_like(beyond)
        pair = (beyond, nothing) if below else (nothing, beyond)
        return doubled(centre, *pair, [c[:by] for c in self.coefficients(x)]) - self.get(j - 2, x)[:by]

    def interior(self, base):
        for j in range(1, STEPS):
            for x in range(j, self.bx - j):
                self.get(base + j, x)

    def finish(self, base):
        for j in range(1, STEPS + 1):
            reach = max([m for i, m in COMPUTED if i == j], default=0)
            for x in range(-reach, self.bx + reach):
                self.get(base + j, x)


def halo_layer(bx, m, low_side):
    return -m if low_side else bx - 1 + m


def own_places(bx, base, ref):
    return {(base + j, x): (ref, (j - 1, x)) for j in range(1, STEPS + 1) for x in range(bx)}


def mark_interior(cells, bx, base, ref):
    for j in range(1, STEPS):
        for x in range(j, bx - j):
            cells.known[base + j, x] = lambda j=j, x=x: ref[j - 1, x]


def halo_places(bx, base, scratch, sides=None):
    places, slot = {}, 0
    for j, m in COMPUTED:
        for low_side in (True, False):
            at = (base + j, halo_layer(bx, m, low_side))
            if sides is not None and (j, m) == (STEPS - 1, 1):
                places[at] = (sides, (0 if low_side else 1,))
            else:
                places[at] = (scratch, (slot,))
                slot += 1
    return places


def prepare_kernel(fields, rows, start, coef, vectors):
    _, bx, by, _ = fields.shape
    start[:, 0:by] = fields[0] * LIFT
    start[:, by:] = rows[0:bx] * LIFT
    for k in range(4):
        coef[k, :, 0:by] = scaled(k, fields[k + 1])
        coef[k, :, by:] = scaled(k, rows[bx * (k + 1) : bx * (k + 2)])
    places = own_places(bx, 0, vectors)
    cells = Cells(bx, coef, None, lambda j, x: places[j, x])
    for x in range(bx):
        cells.known[0, x] = lambda x=x: start[x]
    cells.interior(0)


def wide_layer(slab, corner, at, base):
    return jnp.concatenate([slab[at], corner[base + at]], axis=0)


def know_start(cells, start, low, high, corner):
    bx, size = start.shape[0], low.shape[0]
    for x in range(bx):
        cells.known[0, x] = lambda x=x: start[x]
    for side, slab, base in ((0, low, 0), (1, high, size)):
        for m in (1, 2):
            at = DEPTHS[0] - m if side == 0 else m - 1
            cells.known[0, halo_layer(bx, m, side == 0)] = lambda slab=slab, base=base, at=at: (
                wide_layer(slab, corner, at, base) * LIFT
            )


def early_range(j, bx):
    return range(j - 2, bx - (j - 2))


def first_kernel(start, coef, low, high, corner, given, vectors, beside, edge, weight):
    del given
    bx, by = start.shape[0], low.shape[1]
    size = low.shape[0]
    places = own_places(bx, 0, vectors)
    places[1, -1], places[1, bx] = (beside, (0,)), (beside, (1,))
    for side, slab, base in ((0, low, 0), (1, high, size)):
        for k in range(4):
            depth, at = DEPTHS[k + 1], OFFSETS[k + 1]
            at += depth - 1 if side == 0 else 0
            edge[k, side, 0:by] = scaled(k, slab[at])
            edge[k, side, by:] = scaled(k, corner[base + at])
        at = OFFSETS[2] + (0 if side == 0 else 1)
        sign = SCALES[1] if side == 0 else -SCALES[1]
        weight[side, 0:by] = slab[at] * sign - 2.0 * DIFFUSION / HALF_WIDTH
        weight[side, by:] = corner[base + at] * sign - 2.0 * DIFFUSION / HALF_WIDTH
    cells = Cells(bx, coef, edge, lambda j, x: places[j, x])
    mark_interior(cells, bx, 0, vectors)
    know_start(cells, start, low, high, corner)
    for j in range(1, STEPS + 1):
        for x in early_range(j, bx):
            cells.get(j, x)


def rest_kernel(
    start, coef, low, high, corner, beside, edge, weight, low_later, high_later, later_corner, given, vectors, to_low, to_high, following, sides, scratch
):
    del given
    bx, by = start.shape[0], low.shape[1]
    later = low_later.shape[0]
    places = own_places(bx, 0, vectors) | own_places(bx, STEPS, following) | halo_places(bx, 0, scratch, sides)
    cells = Cells(bx, coef, edge, lambda j, x: places[j, x])
    know_start(cells, start, low, high, corner)
    for j in range(1, STEPS + 1):
        for x in early_range(j, bx):
            cells.known[j, x] = lambda j=j, x=x: vectors[j - 1, x]
    cells.known[1, -1], cells.known[1, bx] = (lambda: beside[0]), (lambda: beside[1])
    for side, slab, base in ((0, low_later, 0), (1, high_later, later)):
        near, far = halo_layer(bx, 1, side == 0), halo_layer(bx, 2, side == 0)
        cells.known[1, far] = lambda slab=slab, base=base: wide_layer(slab, later_corner, 0, base)
        cells.computed[2, far] = lambda slab=slab, base=base, side=side, near=near: (
            wide_layer(slab, later_corner, 1, base) + weight[side] * cells.get(1, near)
        )
    cells.finish(0)
    for out, below, one, two in ((to_low, True, 0, 1), (to_high, False, bx - 1, bx - 2)):
        leaving = [
            cells.get(STEPS, one),
            cells.get(STEPS, two),
            cells.get(STEPS + 1, two),
            cells.tip(STEPS, two, below, by),
        ]
        for at, layer in enumerate(leaving):
            out[at * by : (at + 1) * by] = layer[:by]
        tiles = [(layer[by : by + MARGIN], layer[by + MARGIN :]) for layer in leaving[:3]]
        row = lax.broadcasted_iota(jnp.int32, tiles[0][0].shape, 0)
        out[4 * by : 4 * by + 8] = jnp.where(row < EDGE, *tiles[0])
        middle = jnp.where(row < EDGE, pltpu.roll(tiles[2][0], 2, 0), pltpu.roll(tiles[2][1], 6, 0))
        outer = jnp.where(row < EDGE, *tiles[1])
        out[4 * by + 8 :] = jnp.where((row == 2) | (row == 5), middle, outer)


def second_cells(one, sides, coef, edge, weight, slab, side, two, scratch):
    bx = coef.shape[1]
    by = slab.shape[0] // 4 - EDGE
    places = own_places(bx, STEPS, two) | halo_places(bx, STEPS, scratch)
    cells = Cells(bx, coef, edge, lambda j, x: places[j, x])
    mark_interior(cells, bx, STEPS, two)
    for x in range(bx):
        cells.known[STEPS, x] = lambda x=x: one[STEPS - 1, x]
        cells.known[STEPS - 1, x] = lambda x=x: one[STEPS - 2, x]
    near, far = halo_layer(bx, 1, side == 0), halo_layer(bx, 2, side == 0)

    def wide(at):
        first, second = slab[4 * by : 4 * by + 8], slab[4 * by + 8 :]
        above, below = ((first, first), (second, second), (pltpu.roll(second, 6, 0), pltpu.roll(second, 2, 0)))[min(at, 2)]
        return jnp.concatenate([slab[at * by : (at + 1) * by], above, below], axis=0)

    cells.known[STEPS - 1, near] = lambda: sides[side]
    cells.known[STEPS, near] = lambda: wide(0)
    cells.known[STEPS, far] = lambda: wide(1)
    cells.known[STEPS + 1, far] = lambda: wide(2)
    cells.computed[STEPS + 2, far] = lambda: wide(3) + weight[side] * cells.get(STEPS + 1, near)
    return cells


def reach_of(j):
    return max([m for i, m in COMPUTED if i == j], default=0)


def sooner_kernel(start, one, given, sides, coef, edge, weight, high, before, two, partial, scratch):
    del given
    bx, _, nz = start.shape
    by = high.shape[0] // 4 - EDGE
    cells = second_cells(one, sides, coef, edge, weight, high, 1, two, scratch)
    for j in range(1, STEPS + 1):
        for x in range(j, bx + reach_of(j)):
            cells.get(STEPS + j, x)
    before = [before[k] for k in range(len(GROUPS[1]))]
    totals = later_products(lambda j: (bx - j, bx), before, by, nz, reader(start, one, two))
    for k, total in enumerate(totals):
        partial[k] = total


def later_kernel(start, one, given, sides, coef, edge, weight, low, early_gram, partial, two, gram, scratch):
    del given
    bx, _, nz = start.shape
    by = low.shape[0] // 4 - EDGE
    cells = second_cells(one, sides, coef, edge, weight, low, 0, two, scratch)
    for j in range(1, STEPS + 1):
        for x in range(j, bx):
            cells.known[STEPS + j, x] = lambda j=j, x=x: two[j - 1, x]
    for j in range(1, STEPS + 1):
        for x in range(-reach_of(j), j):
            cells.get(STEPS + j, x)
    before = [partial[k] for k in range(len(GROUPS[1]))]
    rows = summed_rows(later_products(lambda j: (0, j), before, by, nz, reader(start, one, two)))
    sums = jnp.concatenate([early_gram[...]] + rows, axis=0)
    on = lax.broadcasted_iota(jnp.int32, sums.shape, 0) == lax.broadcasted_iota(jnp.int32, sums.shape, 1)
    line = jnp.sum(jnp.where(on, jnp.sum(sums, axis=1, keepdims=True), 0.0), axis=0, keepdims=True)
    gram[...] = jnp.broadcast_to(line, gram.shape)


def last_kernel(cell_count, gram, start, one, two, out, factor, result, sem):
    _, bx, by, nz = result.shape
    total = gram[0:8]
    for row in range(8, gram.shape[0], 8):
        total = total + gram[row : row + 8]
    for distance in (4, 2, 1):
        total = total + pltpu.roll(total, distance, 0)
    total = total * (1.0 / cell_count)
    cell = reader(start, one, two)
    entry, inverse, copies = {}, [], []
    for j in range(BASIS):
        for i in range(j + 1):
            k = PLACE[i, j]
            value = jnp.broadcast_to(total[:, k : k + 1], (8, 128))
            if (i, j) == (0, 0):
                mean_square = value * (1.0 / (LIFT * LIFT))
            for above in range(i):
                value = value - entry[above, i] * entry[above, j]
            if i == j:
                inverse.append(lax.rsqrt(value))
            entry[i, j] = value * inverse[i]
        for x in range(bx):
            for y in range(0, by, 8):
                for z in range(0, nz, 128):
                    window = (x, slice(y, y + 8), slice(z, z + 128))
                    value = cell(j, *window)
                    for i in range(j):
                        value = value - entry[i, j] * result[(i,) + window]
                    result[(j,) + window] = value * inverse[j]
        copies.append(pltpu.make_async_copy(result.at[j], out.at[j], sem.at[j]))
        copies[j].start()
    scale = lax.rsqrt(mean_square + EPSILON) * (1.0 / LIFT)
    sublane = lax.broadcasted_iota(jnp.int32, (8, 128), 0)
    lane = lax.broadcasted_iota(jnp.int32, (8, 128), 1)
    tops = []
    for base in range(0, BASIS, 8):
        packed = jnp.zeros((8, 128), jnp.float32)
        for (i, j), value in entry.items():
            if base <= i < base + 8:
                packed = jnp.where((sublane == i - base) & (lane == j), value, packed)
        tops.append(packed * scale)
    factor[...] = jnp.concatenate(tops, axis=0)[:BASIS, :BASIS]
    for copy in copies:
        copy.wait()


def shape(*dims):
    return jax.ShapeDtypeStruct(dims, jnp.float32)


def call(kernel, outs, *args, name, scratch=(), us=0.02, in_specs=None, out_specs=None, aliases=None):
    return pl.pallas_call(
        kernel,
        out_shape=outs,
        in_specs=in_specs or [VMEM] * len(args),
        out_specs=out_specs or [VMEM] * len(outs),
        scratch_shapes=scratch,
        input_output_aliases=aliases or {},
        compiler_params=pltpu.CompilerParams(vmem_limit_bytes=24 << 20),
        cost_estimate=pl.CostEstimate(flops=0, transcendentals=0, bytes_accessed=int(us * 3e6)),
        name=name,
    )(*args)


def per_device(forcing, reaction, velocity):
    bx, by, nz = forcing.shape
    devices = lax.axis_size("gx") * lax.axis_size("gy")
    cell_count = float(bx * by * nz * devices)
    wide = by + 2 * MARGIN
    inputs = tuple(pltpu.with_memory_space_constraint(v, pltpu.MemorySpace.HBM) for v in (forcing, reaction, velocity))
    vectors = shape(STEPS, bx, wide, nz)
    fields, to_low, to_high, rows = call(
        pack_kernel,
        [shape(5, bx, by, nz)] + [shape(sum(DEPTHS), by, nz)] * 2 + [shape(SWAPPED[5], 2 * EDGE, nz)],
        *inputs,
        name="pack",
        in_specs=[HBM] * 3,
        scratch=[pltpu.SemaphoreType.DMA((5,))],
    )
    low, high = swap_x(to_low, to_high)
    rows = swap_rows(rows[:, :EDGE], rows[:, EDGE:])
    to_low, to_high = call(
        inner_kernel,
        [shape(2, by, nz)] * 2,
        fields,
        rows,
        name="inner",
        scratch=[pltpu.VMEM((4, by + 2 * EDGE, nz), jnp.float32)],
    )
    low_later, high_later = swap_x(to_low, to_high)
    rows = swap_y(fields.reshape(5 * bx, by, nz))
    start, coef, one = call(
        prepare_kernel, [shape(bx, wide, nz), shape(4, bx, wide, nz), vectors], fields, rows, name="prepare"
    )
    corner = swap_y(jnp.concatenate([low, high]))
    one, beside, edge, weight = call(
        first_kernel,
        [vectors, shape(2, wide, nz), shape(4, 2, wide, nz), shape(2, wide, nz)],
        start,
        coef,
        low,
        high,
        corner,
        one,
        name="first",
        aliases={5: 0},
    )
    one, to_low, to_high, two, sides = call(
        rest_kernel,
        [vectors, shape(4 * by + 16, nz), shape(4 * by + 16, nz), vectors, shape(2, wide, nz)],
        start,
        coef,
        low,
        high,
        corner,
        beside,
        edge,
        weight,
        low_later,
        high_later,
        swap_y(jnp.concatenate([low_later, high_later])),
        one,
        name="rest",
        scratch=[pltpu.VMEM((2 * len(COMPUTED), wide, nz), jnp.float32)],
        aliases={11: 0},
    )
    low, high = swap_x(to_low, to_high)
    two, early_gram, partial = call(
        lambda *refs: second_interior_kernel(by, *refs),
        [vectors, shape(STARTS[1], 128), shape(len(GROUPS[1]), 8, 128)],
        start,
        one,
        coef,
        two,
        name="second_interior",
        aliases={3: 0},
    )
    halo = [pltpu.VMEM((2 * len(COMPUTED), wide, nz), jnp.float32)]
    two, partial = call(
        sooner_kernel,
        [vectors, shape(len(GROUPS[1]), 8, 128)],
        start,
        one,
        two,
        sides,
        coef,
        edge,
        weight,
        high,
        partial,
        name="sooner",
        scratch=halo,
        aliases={2: 0},
    )
    two, gram = call(
        later_kernel,
        [vectors, shape(devices, 128)],
        start,
        one,
        two,
        sides,
        coef,
        edge,
        weight,
        low,
        early_gram,
        partial,
        name="later",
        scratch=halo,
        aliases={2: 0},
    )
    gram = lax.all_to_all(gram, AXES, 0, 0, tiled=True)
    return call(
        lambda *refs: last_kernel(cell_count, *refs),
        [shape(BASIS, bx, by, nz), shape(BASIS, BASIS)],
        gram,
        start,
        one,
        two,
        name="last",
        out_specs=[pl.BlockSpec(memory_space=pl.ANY), VMEM],
        scratch=[
            pltpu.VMEM((BASIS, bx, by, nz), jnp.float32),
            pltpu.SemaphoreType.DMA((BASIS,)),
        ],
    )


def solution(mesh):
    in_specs = (P("gx", "gy", None), P("gx", "gy", None), P(None, "gx", "gy", None))
    out_specs = (P(None, "gx", "gy", None), P())
    return jax.shard_map(per_device, mesh=mesh, in_specs=in_specs, out_specs=out_specs, check_vma=False)
```
